32 devices in a mesh: row: 4 (over z), col: 8 (over y, x, core).
Axes of the slice: x: 2, y: 2, z: 4, core: 2. Of those that a mesh axis runs over, the one named last changes fastest.
Arguments:
- slab_left: bfloat16 [16, 8, 2048, 32], P('row', 'col'), may hold values from -6 to 6
- slab_right: bfloat16 [16, 8, 2048, 32], P('row', 'col'), may hold values from -1 to 1
- slab_ranks: int32 [16, 8], P('row', 'col'), may hold values from 20 to 32
- panel_left: bfloat16 [16, 2048, 32], P('row', 'col'), may hold values from -6 to 6
- panel_right: bfloat16 [16, 2048, 32], P('row', 'col'), may hold values from -0.125 to 0.125
- panel_ranks: int32 [16], P('row'), may hold values from 20 to 32
- inverse_factor: bfloat16 [2048, 2048], P(None, 'col'), may hold values from -2 to 2, as said below
- sketch: bfloat16 [2048, 32], replicated, may hold values from -6 to 6
Outputs:
- new_left: bfloat16 [16, 8, 2048, 32], P('row', 'col')
- new_right: bfloat16 [16, 8, 2048, 32], P('row', 'col')
The draws below stay inside these ranges and needn't reach their ends.
Inputs may be any that keep to these rules, and one draw needn't show every extreme that they name: `slab_ranks`: number of live columns of a slab tile's factors; columns from that index on are padding. `panel_ranks`: number of live columns of a panel tile's factors; columns from that index on are padding. `inverse_factor`: lower triangular: entries above the diagonal are zero, diagonal entries positive.
All inputs are finite; a program needn't handle non-finite values.
Results may differ from the reference program's by a relative error of at most 0.0073.
Values may be sent and summed in bfloat16 or wider, within the bound.
No kernel may reach another device: no remote copies, remote signals or barrier semaphores. Data moves between devices by JAX's collectives and lax.ppermute only.
A program may use at most 64 MiB of HBM per device.

```python
import math
import jax
import jax.numpy as jnp
from jax import lax

B = 2048
R = 32
TR = 4
MT = 16
NT = 8
N_ROW = 4
N_COL = 8


def draw_inverse_factor(key, part):
    first_key = jax.random.fold_in(key, 11)
    second_key = jax.random.fold_in(key, 12)
    diagonal = jax.random.uniform(first_key, (B,), jnp.float32, 0.5, 1.5)
    spread = 1.0
    below_part = jnp.clip(jax.random.normal(second_key, (B, B), jnp.float32), -6.0, 6.0) * (spread / math.sqrt(B))
    lower_part = jnp.tril(below_part, -1) + jnp.diag(diagonal)
    return lower_part.astype(jnp.bfloat16)


def set_ends(result, key, low, high):
    longest = result.shape.index(max(result.shape))
    spots = []
    for shift in (0, 1):
        where = [jax.random.randint(jax.random.fold_in(key, axis), (), 0, length) for axis, length in enumerate(result.shape)]
        where[longest] = (where[longest] + shift) % result.shape[longest]
        spots.append(tuple(where))
    return result.at[spots[0]].set(low).at[spots[1]].set(high)


def levels(own_key, dims, split, least, top_value):
    factor_of, own = 1.0, jax.random.fold_in(own_key, 6)
    for position, parts in split:
        steps = jnp.exp(jax.random.uniform(jax.random.fold_in(own, position), (parts,), jnp.float32, least / len(split), top_value / len(split)))
        factor_of = factor_of * jnp.repeat(steps, dims[position] // parts).reshape([-1 if axis == position else 1 for axis in range(len(dims))])
    return factor_of


def gaussian(rng, extent, scale, bound, pieces=(), kind=jnp.bfloat16):
    result = jax.random.normal(rng, extent, jnp.float32) * scale
    if len(pieces) > 0:
        result = levels(rng, extent, pieces, -0.22, 0.18) * result
    return jnp.clip(result, min=-bound, max=bound).astype(kind)


def setup_inputs(seed: int = 0) -> dict:
    splits = jax.random.split(jax.random.key(seed), 9)
    return {
        "slab_left": gaussian(splits[0], (MT, NT, B, R), 1.0, 6.0, ((0, 4), (1, 8))),
        "slab_right": gaussian(splits[1], (MT, NT, B, R), R ** -0.5, 1.0, ((0, 4), (1, 8))),
        "slab_ranks": set_ends(jax.random.randint(splits[2], (MT, NT), (5 * R) // 8, R + 1), jax.random.fold_in(splits[2], 1), (5 * R) // 8, R).astype(jnp.int32),
        "panel_left": gaussian(splits[3], (MT, B, R), 1.0, 6.0, ((0, 4), (1, 8))),
        "panel_right": gaussian(splits[4], (MT, B, R), B ** -0.5, 0.125, ((0, 4), (1, 8))),
        "panel_ranks": set_ends(jax.random.randint(splits[5], (MT,), (5 * R) // 8, R + 1), jax.random.fold_in(splits[5], 1), (5 * R) // 8, R).astype(jnp.int32),
        "inverse_factor": draw_inverse_factor(jax.random.fold_in(splits[8], 71), 0),
        "sketch": gaussian(splits[7], (B, R), 1.0, 6.0),
    }


highest = lax.Precision.HIGHEST
shift_rate = 0.01
tiny_shift = 1e-06
factor_scale = 0.5

def product(first_matrix, second_matrix):
    return jnp.matmul(first_matrix, second_matrix, precision=highest)

def flipped(matrix):
    return jnp.swapaxes(matrix, -1, -2)

def apply_tile(outer_left, outer_right, update_left, update_core, update_right, vectors):
    direct = product(outer_left, product(flipped(outer_right), vectors))
    update = product(update_left, product(update_core, product(flipped(update_right), vectors)))
    return direct - update

def orthonormal(vectors):
    gram_matrix = product(flipped(vectors), vectors)
    shift_value = shift_rate * jnp.trace(gram_matrix, axis1=-2, axis2=-1) / gram_matrix.shape[-1] + tiny_shift
    identity = jnp.eye(gram_matrix.shape[-1], dtype=gram_matrix.dtype)
    lower_factor = jnp.linalg.cholesky(gram_matrix + shift_value[..., None, None] * identity)
    solved_rows = lax.linalg.triangular_solve(lower_factor, flipped(vectors), left_side=True, lower=True)
    return flipped(solved_rows)

def recompress(slab_factor, masked_right, row_factor, core_block, column_factor, sketch_float):
    core_flipped = flipped(core_block)

    def forward(vectors):
        return apply_tile(slab_factor, masked_right, row_factor, core_block, column_factor, vectors)

    def backward(vectors):
        return apply_tile(masked_right, slab_factor, column_factor, core_flipped, row_factor, vectors)
    basis_now = orthonormal(forward(sketch_float))
    basis_now = orthonormal(forward(backward(basis_now)))
    projected = backward(basis_now)
    factor_size = factor_scale * math.sqrt(slab_factor.shape[-2])
    return (basis_now * factor_size, projected / factor_size)

def cyclic(total_count, group_count):
    per_group = total_count // group_count
    places = jnp.arange(total_count, dtype=jnp.int32)
    return places % per_group * group_count + places // per_group

def reference(slab_left, slab_right, slab_ranks, panel_left, panel_right, panel_ranks, inverse_factor, sketch):
    row_ids = cyclic(MT, N_ROW)
    col_ids = cyclic(NT, N_COL)
    panel_keep = jnp.arange(R, dtype=jnp.int32)[None, :] < panel_ranks[:, None]
    masked_panel = jnp.where(panel_keep[:, None, :], panel_right, jnp.zeros((), jnp.bfloat16))
    solved = jnp.einsum('ab,pbr->par', inverse_factor.astype(jnp.float32), masked_panel.astype(jnp.float32), precision=highest).astype(jnp.bfloat16)
    where_col = (col_ids % N_ROW * TR + col_ids // N_ROW).astype(jnp.int32)
    column_factor = panel_left[where_col].astype(jnp.float32)
    column_solved = solved[where_col].astype(jnp.float32)
    sketch_float = sketch.astype(jnp.float32)

    def one_row(row_item):
        left_tiles, right_tiles, row_ranks, row_left, row_solved, row_id = row_item
        column_keep = jnp.arange(R, dtype=jnp.int32)[None, :] < row_ranks[:, None]
        masked_right = jnp.where(column_keep[:, None, :], right_tiles.astype(jnp.float32), 0.0)
        core_block = jnp.einsum('br,nbs->nrs', row_solved.astype(jnp.float32), column_solved, precision=highest)
        fresh_left, fresh_right = recompress(left_tiles.astype(jnp.float32), masked_right, row_left.astype(jnp.float32), core_block, column_factor, sketch_float)
        live_tile = (row_id > col_ids)[:, None, None]
        return (jnp.where(live_tile, fresh_left, 0.0).astype(jnp.bfloat16), jnp.where(live_tile, fresh_right, 0.0).astype(jnp.bfloat16))
    new_left, new_right = lax.map(one_row, (slab_left, slab_right, slab_ranks, panel_left, solved, row_ids))
    return (new_left, new_right)
```

```python
import functools
import math

import jax
import jax.numpy as jnp
from jax import lax
from jax.experimental import pallas as pl
from jax.experimental.pallas import tpu as pltpu
from jax.sharding import PartitionSpec as P

highest = lax.Precision.HIGHEST
stacked_precision = lax.Precision.HIGH
shift_rate = 0.01
tiny_shift = 1e-06
factor_scale = 0.5
LANES = 128
F32 = jnp.float32
BF16 = jnp.bfloat16
VMEM = pltpu.VMEM
SMEM = pltpu.SMEM


def spread(block, axis, owner):
    block = jnp.where(lax.axis_index(axis) == owner, block, jnp.zeros_like(block))
    return lax.psum(block, axis)


def product(first_matrix, second_matrix):
    return jnp.matmul(first_matrix, second_matrix, precision=highest)


def stacked_product(first_matrix, second_matrix):
    return jnp.matmul(first_matrix, second_matrix, precision=stacked_precision)


def flipped(matrix):
    return jnp.swapaxes(matrix, -1, -2)


def orthonormal(vectors):
    gram_matrix = product(flipped(vectors), vectors)
    shift_value = (
        shift_rate * jnp.trace(gram_matrix, axis1=-2, axis2=-1) / gram_matrix.shape[-1] + tiny_shift
    )
    identity = jnp.eye(gram_matrix.shape[-1], dtype=gram_matrix.dtype)
    lower_factor = jnp.linalg.cholesky(gram_matrix + shift_value[..., None, None] * identity)
    solved_rows = lax.linalg.triangular_solve(
        lower_factor, flipped(vectors), left_side=True, lower=True
    )
    return flipped(solved_rows)


def recompress(slab_factor, masked_right, row_factor, core_block, column_factor, sketch_float):
    target_shape = core_block.shape[:2] + slab_factor.shape[2:]
    column_wide = jnp.broadcast_to(column_factor[None], target_shape)
    row_core = product(row_factor, core_block)
    column_core = product(column_wide, flipped(core_block))
    forward_left = jnp.concatenate([slab_factor.astype(jnp.float32), -row_core], axis=-1)
    forward_right = jnp.concatenate([masked_right.astype(jnp.float32), column_wide], axis=-1)
    backward_left = jnp.concatenate([masked_right.astype(jnp.float32), -column_core], axis=-1)
    backward_right = jnp.concatenate([slab_factor.astype(jnp.float32), row_factor], axis=-1)

    def forward(vectors):
        return stacked_product(forward_left, stacked_product(flipped(forward_right), vectors))

    def backward(vectors):
        return stacked_product(backward_left, stacked_product(flipped(backward_right), vectors))

    basis_now = orthonormal(forward(sketch_float))
    basis_now = orthonormal(forward(backward(basis_now)))
    projected = backward(basis_now)
    factor_size = factor_scale * math.sqrt(slab_factor.shape[-2])
    return (basis_now * factor_size, projected / factor_size)


def plain_shards(
    slab_left, slab_right, slab_ranks, panel_left, panel_right, panel_ranks, inverse_factor, sketch
):
    rows_total = lax.axis_size("row")
    cols_total = lax.axis_size("col")
    my_row = lax.axis_index("row")
    my_col = lax.axis_index("col")
    tile_rows, piece_rows, rank_width = panel_left.shape
    column_tiles = slab_left.shape[1]
    tile_order = inverse_factor.shape[0]
    panel_keep = jnp.arange(rank_width, dtype=jnp.int32)[None, :] < panel_ranks[:, None]
    masked_panel = jnp.where(panel_keep[:, None, :], panel_right, jnp.zeros((), jnp.bfloat16))
    flat_right = jnp.swapaxes(masked_panel, 0, 1).reshape(piece_rows, tile_rows * rank_width)
    flat_left = jnp.swapaxes(panel_left, 0, 1).reshape(piece_rows, tile_rows * rank_width)
    solved_part = lax.psum_scatter(
        jnp.dot(inverse_factor, flat_right, preferred_element_type=jnp.float32),
        "col",
        scatter_dimension=0,
        tiled=True,
    ).astype(jnp.bfloat16)
    full_left, full_solved = (
        lax.all_gather(flat_left, "col", axis=0, tiled=True),
        lax.all_gather(solved_part, "col", axis=0, tiled=True),
    )
    full_left = full_left.reshape(tile_order, tile_rows, rank_width)
    full_solved = full_solved.reshape(tile_order, tile_rows, rank_width)
    first_pick = my_col // rows_total
    position = first_pick + 0
    picked_left = lax.dynamic_slice_in_dim(full_left, position, 1, 1)
    picked_solved = lax.dynamic_slice_in_dim(full_solved, position, 1, 1)
    send_left = picked_left.reshape(tile_order, column_tiles * rank_width)
    send_solved = picked_solved.reshape(tile_order, column_tiles * rank_width)
    root_row = my_col % rows_total
    column_left, column_solved = (
        spread(send_left, "row", root_row),
        spread(send_solved, "row", root_row),
    )
    row_factor = jnp.swapaxes(full_left, 0, 1)[:, None]
    row_solved = jnp.swapaxes(full_solved, 0, 1)
    column_factor = jnp.swapaxes(column_left.reshape(tile_order, column_tiles, rank_width), 0, 1)
    column_three = jnp.swapaxes(column_solved.reshape(tile_order, column_tiles, rank_width), 0, 1)
    core_block = jnp.einsum(
        "tbr,sbq->tsrq", row_solved, column_three, preferred_element_type=jnp.float32
    )
    slab_keep = jnp.arange(rank_width, dtype=jnp.int32) < slab_ranks[..., None]
    masked_right = jnp.where(slab_keep[:, :, None, :], slab_right, jnp.zeros((), jnp.bfloat16))
    fresh_left, fresh_right = recompress(
        slab_left, masked_right, row_factor, core_block, column_factor, sketch.astype(jnp.float32)
    )
    row_ids = jnp.arange(tile_rows, dtype=jnp.int32) * rows_total + my_row
    col_ids = jnp.arange(column_tiles, dtype=jnp.int32) * cols_total + my_col
    live_tile = (row_ids[:, None] > col_ids[None, :])[:, :, None, None]
    return (
        jnp.where(live_tile, fresh_left, 0.0).astype(jnp.bfloat16),
        jnp.where(live_tile, fresh_right, 0.0).astype(jnp.bfloat16),
    )


def nt(first, second):
    return lax.dot_general(first, second, (((1,), (1,)), ((), ())), preferred_element_type=F32)


def nn(first, second):
    return lax.dot_general(first, second, (((1,), (0,)), ((), ())), preferred_element_type=F32)


def split(value):
    high = value.astype(BF16)
    return high, (value - high.astype(F32)).astype(BF16)


def wide(value):
    return jnp.concatenate(split(value), axis=0)


def fold(value):
    half = value.shape[0] // 2
    return value[:half] + value[half:]


def dot_split(op, first, second_parts):
    stacked = wide(first)
    return fold(op(stacked, second_parts[0]) + op(stacked, second_parts[1]))


def solve_kernel(width, info, right_ref, inverse_ref, out_ref):
    right = right_ref[...]
    rows = lax.broadcasted_iota(jnp.int32, right.shape, 0)
    keep = jnp.zeros(right.shape, jnp.bool_)
    for tile in range(right.shape[0] // width):
        keep |= (rows >= tile * width) & (rows < tile * width + info[2 + tile])
    masked = jnp.where(keep, right, jnp.zeros((), right.dtype))
    out_ref[0] = nt(masked, inverse_ref[...])


def solve_part(info, right, inverse, odd, parts, width):
    lines, piece = right.shape
    return pl.pallas_call(
        functools.partial(solve_kernel, width),
        grid_spec=pltpu.PrefetchScalarGridSpec(
            num_scalar_prefetch=1,
            grid=(parts,),
            in_specs=[
                pl.BlockSpec((lines, piece), lambda step, info: (0, 0)),
                pl.BlockSpec((piece, piece), lambda step, info: (info[1] ^ (2 * step + odd), 0)),
            ],
            out_specs=pl.BlockSpec((1, lines, piece), lambda step, info: (step, 0, 0)),
        ),
        out_shape=jax.ShapeDtypeStruct((parts, lines, piece), F32),
        name="solve_odd" if odd else "solve_even",
        cost_estimate=pl.CostEstimate(
            flops=2 * parts * lines * piece * piece,
            bytes_accessed=2 * parts * piece * piece + 4 * parts * lines * piece,
            transcendentals=0,
        ),
    )(info, right, inverse)


def pair_add_kernel(parts, mine_ref, other_ref, keep_ref, *send_refs):
    keep_ref[...] = mine_ref[0] + other_ref[0]
    for step in range(1, parts):
        send_refs[step - 1][...] = (mine_ref[step] + other_ref[step]).astype(
            send_refs[step - 1].dtype
        )


def in_vmem(count):
    return [pl.BlockSpec(memory_space=VMEM)] * count


def small_cost(bytes_accessed, flops=0):
    return pl.CostEstimate(flops=flops, bytes_accessed=bytes_accessed, transcendentals=0)


def pair_add(mine, other, send_type):
    parts = mine.shape[0]
    shape = mine.shape[1:]
    return pl.pallas_call(
        functools.partial(pair_add_kernel, parts),
        in_specs=in_vmem(2),
        out_specs=in_vmem(parts),
        out_shape=[jax.ShapeDtypeStruct(shape, F32)]
        + [jax.ShapeDtypeStruct(shape, send_type)] * (parts - 1),
        name="pair_add",
        cost_estimate=small_cost(3 * mine.size * 4),
    )(mine, other)


def gather_add_kernel(count, head_lines, *refs):
    total = refs[0][...]
    for ref in refs[1:count]:
        total = total + ref[...].astype(F32)
    rounded = total.astype(BF16)
    refs[count][...] = rounded
    refs[count + 1][...] = rounded[:head_lines]


def gather_add(first, others, head_lines):
    count = 1 + len(others)
    return pl.pallas_call(
        functools.partial(gather_add_kernel, count, head_lines),
        in_specs=in_vmem(count),
        out_specs=in_vmem(2),
        out_shape=[
            jax.ShapeDtypeStruct(first.shape, BF16),
            jax.ShapeDtypeStruct((head_lines, first.shape[1]), BF16),
        ],
        name="gather_add",
        cost_estimate=small_cost(first.size * 10),
    )(first, *others)


def core_kernel(rows_total, cols_total, width, info, own_ref, *refs):
    others = refs[: rows_total - 1]
    even_ref, odd_ref, stage = refs[rows_total - 1 :]
    my_row, my_col = info[0], info[1]
    for shift in range(rows_total):
        source = own_ref if shift == 0 else others[shift - 1]
        from_row = lax.rem(my_row - shift + rows_total, rows_total)
        for index in range(cols_total // rows_total):
            relative = my_col ^ (index * rows_total + from_row)
            place = (relative & 1) * (cols_total // 2) + lax.shift_right_logical(relative, 1)
            stage[place] = source[index * width : (index + 1) * width, :]
    piece = own_ref.shape[1]
    half = cols_total // 2
    own = own_ref[...]
    for part, ref in ((1, odd_ref), (0, even_ref)):
        block = stage[part * half : (part + 1) * half].reshape(half * width, piece)
        ref[...] = nt(block, own).reshape(ref.shape)


def core_parts(info, own, others, rows_total, cols_total, width):
    lines, piece = own.shape
    half = cols_total // 2
    shape = jax.ShapeDtypeStruct((half, width, lines), F32)
    return pl.pallas_call(
        functools.partial(core_kernel, rows_total, cols_total, width),
        in_specs=[pl.BlockSpec(memory_space=SMEM)] + in_vmem(rows_total),
        out_specs=in_vmem(2),
        out_shape=[shape, shape],
        scratch_shapes=[VMEM((cols_total, width, piece), BF16)],
        name="core_parts",
        cost_estimate=small_cost(400000, 2 * lines * piece * cols_total * width),
    )(info, own, *others)


def message_kernel(rows_total, cols_total, width, info, own_ref, *refs):
    others = refs[: rows_total - 1]
    message_refs = refs[rows_total - 1 : -1]
    stage = refs[-1]
    my_row, my_col = info[0], info[1]
    lines = own_ref.shape[0]
    for shift in range(rows_total):
        source = own_ref if shift == 0 else others[shift - 1]
        from_row = lax.rem(my_row - shift + rows_total, rows_total)
        for index in range(cols_total // rows_total):
            stage[index * rows_total + from_row] = source[index * width : (index + 1) * width, :]
    for step, ref in enumerate(message_refs):
        target = my_col ^ (2 * step)
        ref[:width] = stage[target]
        ref[width : width + lines] = own_ref[...]
        ref[width + lines :] = stage[target ^ 1]


def messages(info, own, others, rows_total, cols_total, width):
    lines, piece = own.shape
    half = cols_total // 2
    return pl.pallas_call(
        functools.partial(message_kernel, rows_total, cols_total, width),
        in_specs=[pl.BlockSpec(memory_space=SMEM)] + in_vmem(rows_total),
        out_specs=in_vmem(half),
        out_shape=[jax.ShapeDtypeStruct((lines + 2 * width, piece), BF16)] * half,
        scratch_shapes=[VMEM((cols_total, width, piece), BF16)],
        name="messages",
        cost_estimate=small_cost(half * (lines + 2 * width) * piece * 4),
    )(info, own, *others)


def piece_views(even_refs, odd_ref, width, lines):
    for step, ref in enumerate(even_refs):
        yield 2 * step, ref.at[width : width + lines], ref.at[:width]
    for step in range(len(even_refs)):
        yield 2 * step + 1, odd_ref.at[step, :lines], odd_ref.at[step, lines:]


def gram_kernel(half, width, info, left_ref, right_ref, sketch_ref, *refs):
    even_refs = refs[:half]
    odd_ref, row_gram_ref, column_gram_ref = refs[half:]
    lines = left_ref.shape[0]
    piece = odd_ref.shape[2]
    my_col = info[1]
    row_gram = jnp.zeros(row_gram_ref.shape, F32)
    column_gram = jnp.zeros(column_gram_ref.shape, F32)
    for relative, panel, column in piece_views(even_refs, odd_ref, width, lines):
        spot = pl.ds(pl.multiple_of((my_col ^ relative) * piece, LANES), piece)
        rows = jnp.concatenate([left_ref[:, spot], panel[...]], axis=0)
        row_gram = row_gram + nt(rows, rows)
        columns = jnp.concatenate([right_ref[:, spot], column[...]], axis=0)
        tall = jnp.concatenate([columns, sketch_ref[:, spot]], axis=0)
        column_gram = column_gram + nt(tall, columns)
    row_gram_ref[...] = row_gram
    column_gram_ref[...] = column_gram


def grams(info, left, right, sketch, even, odd, width):
    lines, order = left.shape
    half = len(even)
    return pl.pallas_call(
        functools.partial(gram_kernel, half, width),
        in_specs=[pl.BlockSpec(memory_space=SMEM)] + in_vmem(4 + half),
        out_specs=in_vmem(2),
        out_shape=[
            jax.ShapeDtypeStruct((2 * lines, 2 * lines), F32),
            jax.ShapeDtypeStruct((lines + 2 * width, lines + width), F32),
        ],
        name="grams",
        cost_estimate=small_cost(2000000, 2 * order * lines * lines * 8),
    )(info, left, right, sketch, *even, odd)


def factor_and_apply(gram, shift, bands):
    width = gram.shape[0]
    blocks = width // 8
    lanes = lax.broadcasted_iota(jnp.int32, (8, LANES), 1)
    group = lanes - lax.rem(lanes, width)
    sub = lax.broadcasted_iota(jnp.int32, (8, LANES), 0)
    gram_rows = [gram[8 * b : 8 * b + 8] for b in range(blocks)]
    bands = [[band[8 * b : 8 * b + 8] for b in range(blocks)] for band in bands]
    rows = []
    for k in range(width):
        first = k // 8
        rows.append(
            {
                b: jnp.take_along_axis(gram_rows[b], group + k, axis=1)
                for b in range(first, blocks)
            }
        )
    for k in range(width):
        first, inner = divmod(k, 8)
        row = rows[k]
        pivot = row[first][inner : inner + 1] + shift[:1]
        scale = lax.rsqrt(pivot)
        scaled = {b: row[b] * scale for b in row}
        for i in range(k + 1, width):
            lead = scaled[i // 8][i % 8 : i % 8 + 1]
            for b in rows[i]:
                rows[i][b] = rows[i][b] - lead * scaled[b]
        below = dict(scaled)
        below[first] = jnp.where(sub > inner, scaled[first], 0.0)
        for band in bands:
            done = band[first][inner : inner + 1] * scale
            for b in range(first, blocks):
                band[b] = band[b] - below[b] * done
            band[first] = jnp.where(sub == inner, done, band[first])
    return [jnp.concatenate(band, axis=0) for band in bands]


def finish_kernel(half, width, rows_total, info, *refs):
    core_refs = refs[:half]
    row_gram_ref, column_gram_ref, left_ref, right_ref = refs[half : half + 4]
    even_refs = refs[half + 4 : 2 * half + 4]
    odd_ref, out_left_ref, out_right_ref = refs[2 * half + 4 :]
    my_row, my_col = info[0], info[1]
    lines, order = left_ref.shape
    tiles = lines // width
    piece = odd_ref.shape[2]
    lane = lax.broadcasted_iota(jnp.int32, (lines, lines), 1)
    line = lax.broadcasted_iota(jnp.int32, (lines, lines), 0)
    same = (lane // width) == (line // width)

    def diagonal(value):
        return jnp.where(same, value, 0.0)

    def stacked(value):
        return diagonal(jnp.concatenate([value] * tiles, axis=0))

    def blocks(value):
        return jnp.concatenate([stacked(value[:, :lines]), stacked(value[:, lines:])], axis=1)

    lane_row = lax.broadcasted_iota(jnp.int32, (1, lines), 1)
    line_col = lax.broadcasted_iota(jnp.int32, (lines, 1), 0)
    keep_lane = jnp.zeros((1, lines), jnp.bool_)
    keep_line = jnp.zeros((lines, 1), jnp.bool_)
    live_line = jnp.zeros((1, lines), jnp.bool_)
    for tile in range(tiles):
        low, high = tile * width, tile * width + info[2 + tile]
        keep_lane |= (lane_row >= low) & (lane_row < high)
        keep_line |= (line_col >= low) & (line_col < high)
        live = (tile * rows_total + my_row) > my_col
        live_line |= (lane_row >= low) & (lane_row < low + jnp.where(live, width, 0))

    row_gram = row_gram_ref[...]
    row_parts = split(
        jnp.concatenate(
            [
                jnp.concatenate(
                    [diagonal(row_gram[:lines, :lines]), diagonal(row_gram[:lines, lines:])], axis=1
                ),
                jnp.concatenate(
                    [diagonal(row_gram[lines:, :lines]), diagonal(row_gram[lines:, lines:])], axis=1
                ),
            ],
            axis=0,
        )
    )
    column_gram = column_gram_ref[...]
    right_right = jnp.where(same & keep_line & keep_lane, column_gram[:lines, :lines], 0.0)
    right_column = jnp.where(keep_line, column_gram[:lines, lines:], 0.0)
    column_column = column_gram[lines : lines + width, lines:]
    sketch_right = jnp.where(keep_lane, column_gram[lines + width :, :lines], 0.0)
    sketch_column = column_gram[lines + width :, lines:]

    core = core_refs[0][...]
    for ref in core_refs[1:]:
        core = core + ref[...]
    core_split = split(core)
    core_blocks = stacked(core)
    core_block_split = split(core_blocks)

    first = jnp.concatenate([sketch_right, -dot_split(nn, sketch_column, core_split)], axis=1)
    ones = jnp.where(same, 1.0, 0.0).astype(BF16)

    def traced(one, two):
        both = jnp.sum(one * two, axis=0, keepdims=True)
        both = both[:, :lines] + both[:, lines:]
        high, low = split(jnp.broadcast_to(both, (8, lines)))
        return (nn(high, ones) + nn(low, ones)) * (shift_rate / width) + tiny_shift

    image = dot_split(nn, first, row_parts)
    shift = traced(first, image)
    gram = dot_split(nt, first, split(blocks(image)))
    top, bottom = factor_and_apply(gram, shift, [image[:, :lines], image[:, lines:]])
    basis = jnp.concatenate([top, bottom], axis=1)

    cross = -diagonal(dot_split(nn, right_column, core_split))
    inner = dot_split(nn, column_column, core_split)
    core_lines = core.T
    corner = diagonal(dot_split(nn, core_lines, split(inner)))
    middle_parts = split(
        jnp.concatenate(
            [
                jnp.concatenate([right_right, cross], axis=1),
                jnp.concatenate([cross.T, corner], axis=1),
            ],
            axis=0,
        )
    )
    second = dot_split(nn, basis, middle_parts)
    image = dot_split(nn, second, row_parts)
    shift = traced(second, image)
    gram = dot_split(nt, second, split(blocks(image)))
    back = -dot_split(nt, image[:, lines:], core_block_split)
    left_top, left_bottom, right_top, right_bottom = factor_and_apply(
        gram, shift, [second[:, :lines], second[:, lines:], image[:, :lines], back]
    )
    factor_size = factor_scale * math.sqrt(order)
    live_scale = jnp.where(live_line, factor_size, 0.0)
    live_back = jnp.where(live_line, 1.0 / factor_size, 0.0)
    left_small = wide(
        jnp.concatenate([stacked(left_top * live_scale), stacked(left_bottom * live_scale)], axis=1)
    )
    right_small = wide(
        jnp.concatenate(
            [
                stacked(jnp.where(keep_lane, right_top * live_back, 0.0)),
                stacked(right_bottom * live_back),
            ],
            axis=1,
        )
    )
    for relative, panel, column in piece_views(even_refs, odd_ref, width, lines):
        spot = pl.ds(pl.multiple_of((my_col ^ relative) * piece, LANES), piece)
        rows = jnp.concatenate([left_ref[:, spot], panel[...]], axis=0)
        out_left_ref[:, spot] = fold(nn(left_small, rows)).astype(BF16)
        columns = jnp.concatenate([right_ref[:, spot]] + [column[...]] * tiles, axis=0)
        out_right_ref[:, spot] = fold(nn(right_small, columns)).astype(BF16)


def finish(info, cores, row_gram, column_gram, left, right, even, odd, rows_total, width):
    half = len(even)
    shape = jax.ShapeDtypeStruct(left.shape, BF16)
    return pl.pallas_call(
        functools.partial(finish_kernel, half, width, rows_total),
        in_specs=[pl.BlockSpec(memory_space=SMEM)] + in_vmem(2 * half + 5),
        out_specs=in_vmem(2),
        out_shape=[shape, shape],
        name="finish",
        cost_estimate=small_cost(5000000, 10**9),
    )(info, *cores, row_gram, column_gram, left, right, *even, odd)


def flat_lines(block):
    return jnp.swapaxes(block, -1, -2).reshape(-1, block.shape[-2])


def fast_shards(
    slab_left, slab_right, slab_ranks, panel_left, panel_right, panel_ranks, inverse_factor, sketch
):
    rows_total = lax.axis_size("row")
    cols_total = lax.axis_size("col")
    width = panel_left.shape[-1]
    half = cols_total // 2
    place = jnp.stack([lax.axis_index("row"), lax.axis_index("col")]).astype(jnp.int32)
    panel_info = jnp.concatenate([place, panel_ranks])
    slab_info = jnp.concatenate([place, slab_ranks.reshape(-1)])
    left, right = flat_lines(slab_left), flat_lines(slab_right)
    panel, solve_right = flat_lines(panel_left), flat_lines(panel_right)
    sketch_lines = flat_lines(sketch)
    head = width * (cols_total // rows_total)

    def swap(block, step):
        return lax.ppermute(block, "col", [(i, i ^ step) for i in range(cols_total)])

    def turn(block, shift):
        pairs = [(i, (i + shift) % rows_total) for i in range(rows_total)]
        return lax.ppermute(block, "row", pairs)

    odd = solve_part(panel_info, solve_right, inverse_factor, 1, half, width)
    other = swap(odd, 1)
    even = solve_part(panel_info, solve_right, inverse_factor, 0, half, width)
    kept, *sends = pair_add(even, other, BF16)
    received = [swap(block, 2 * (step + 1)) for step, block in enumerate(sends)]
    panel, *_ = lax.optimization_barrier((panel, *sends))
    panel_others = [turn(panel[:head], shift) for shift in range(1, rows_total)]
    solved, solved_head = gather_add(kept, received, head)
    solved_others = [turn(solved_head, shift) for shift in range(1, rows_total)]
    own_message, *sends = messages(slab_info, panel, panel_others, rows_total, cols_total, width)
    even_pieces = [own_message] + [
        swap(block, 2 * (step + 1)) for step, block in enumerate(sends)
    ]
    core_even, core_odd = core_parts(
        slab_info, solved, solved_others, rows_total, cols_total, width
    )
    core_other = swap(core_odd, 1)
    core_kept, *sends = pair_add(core_even, core_other, F32)
    odd_pieces = swap(jnp.stack([block[width:] for block in even_pieces]), 1)
    cores = [core_kept] + [swap(block, 2 * (step + 1)) for step, block in enumerate(sends)]
    row_gram, column_gram = grams(
        slab_info, left, right, sketch_lines, even_pieces, odd_pieces, width
    )
    fresh_left, fresh_right = finish(
        slab_info,
        cores,
        row_gram,
        column_gram,
        left,
        right,
        even_pieces,
        odd_pieces,
        rows_total,
        width,
    )

    def placed(block):
        tiles = slab_left.shape[:2] + (width, slab_left.shape[2])
        return jnp.swapaxes(block.reshape(tiles), -1, -2)

    return placed(fresh_left), placed(fresh_right)


def shards(*args):
    slab_left, panel_left = args[0], args[3]
    rows_total, cols_total = lax.axis_size("row"), lax.axis_size("col")
    tile_rows, piece_rows, width = panel_left.shape
    fits = (
        slab_left.shape[1] == 1
        and tile_rows * width == LANES
        and width % 8 == 0
        and piece_rows % LANES == 0
        and cols_total & (cols_total - 1) == 0
        and cols_total >= 4
        and cols_total % rows_total == 0
        and rows_total > 1
        and cols_total <= tile_rows * rows_total
    )
    return fast_shards(*args) if fits else plain_shards(*args)


def solution(mesh):
    placed = (
        P("row", "col", None, None),
        P("row", "col", None, None),
        P("row", "col"),
        P("row", "col", None),
        P("row", "col", None),
        P("row"),
        P(None, "col"),
        P(),
    )
    return jax.shard_map(
        shards,
        mesh=mesh,
        in_specs=placed,
        out_specs=(P("row", "col", None, None), P("row", "col", None, None)),
        check_vma=False,
    )
```

```python
import functools
import math

import jax
import jax.numpy as jnp
from jax import lax
from jax.experimental import pallas as pl
from jax.experimental.pallas import tpu as pltpu
from jax.sharding import PartitionSpec as P


highest = lax.Precision.HIGHEST
stacked_precision = lax.Precision.HIGH
shift_rate = 0.01
tiny_shift = 1e-06
factor_scale = 0.5
LANES = 128
F32 = jnp.float32
BF16 = jnp.bfloat16
VMEM = pltpu.VMEM
SMEM = pltpu.SMEM


def spread(block, axis, owner):
    block = jnp.where(lax.axis_index(axis) == owner, block, jnp.zeros_like(block))
    return lax.psum(block, axis)


def product(first_matrix, second_matrix):
    return jnp.matmul(first_matrix, second_matrix, precision=highest)


def stacked_product(first_matrix, second_matrix):
    return jnp.matmul(first_matrix, second_matrix, precision=stacked_precision)


def flipped(matrix):
    return jnp.swapaxes(matrix, -1, -2)


def orthonormal(vectors):
    gram_matrix = product(flipped(vectors), vectors)
    shift_value = (
        shift_rate * jnp.trace(gram_matrix, axis1=-2, axis2=-1) / gram_matrix.shape[-1] + tiny_shift
    )
    identity = jnp.eye(gram_matrix.shape[-1], dtype=gram_matrix.dtype)
    lower_factor = jnp.linalg.cholesky(gram_matrix + shift_value[..., None, None] * identity)
    solved_rows = lax.linalg.triangular_solve(
        lower_factor, flipped(vectors), left_side=True, lower=True
    )
    return flipped(solved_rows)


def recompress(slab_factor, masked_right, row_factor, core_block, column_factor, sketch_float):
    target_shape = core_block.shape[:2] + slab_factor.shape[2:]
    column_wide = jnp.broadcast_to(column_factor[None], target_shape)
    row_core = product(row_factor, core_block)
    column_core = product(column_wide, flipped(core_block))
    forward_left = jnp.concatenate([slab_factor.astype(jnp.float32), -row_core], axis=-1)
    forward_right = jnp.concatenate([masked_right.astype(jnp.float32), column_wide], axis=-1)
    backward_left = jnp.concatenate([masked_right.astype(jnp.float32), -column_core], axis=-1)
    backward_right = jnp.concatenate([slab_factor.astype(jnp.float32), row_factor], axis=-1)

    def forward(vectors):
        return stacked_product(forward_left, stacked_product(flipped(forward_right), vectors))

    def backward(vectors):
        return stacked_product(backward_left, stacked_product(flipped(backward_right), vectors))

    basis_now = orthonormal(forward(sketch_float))
    basis_now = orthonormal(forward(backward(basis_now)))
    projected = backward(basis_now)
    factor_size = factor_scale * math.sqrt(slab_factor.shape[-2])
    return (basis_now * factor_size, projected / factor_size)


def plain_shards(
    slab_left, slab_right, slab_ranks, panel_left, panel_right, panel_ranks, inverse_factor, sketch
):
    rows_total = lax.axis_size("row")
    cols_total = lax.axis_size("col")
    my_row = lax.axis_index("row")
    my_col = lax.axis_index("col")
    tile_rows, piece_rows, rank_width = panel_left.shape
    column_tiles = slab_left.shape[1]
    tile_order = inverse_factor.shape[0]
    panel_keep = jnp.arange(rank_width, dtype=jnp.int32)[None, :] < panel_ranks[:, None]
    masked_panel = jnp.where(panel_keep[:, None, :], panel_right, jnp.zeros((), jnp.bfloat16))
    flat_right = jnp.swapaxes(masked_panel, 0, 1).reshape(piece_rows, tile_rows * rank_width)
    flat_left = jnp.swapaxes(panel_left, 0, 1).reshape(piece_rows, tile_rows * rank_width)
    solved_part = lax.psum_scatter(
        jnp.dot(inverse_factor, flat_right, preferred_element_type=jnp.float32),
        "col",
        scatter_dimension=0,
        tiled=True,
    ).astype(jnp.bfloat16)
    full_left, full_solved = (
        lax.all_gather(flat_left, "col", axis=0, tiled=True),
        lax.all_gather(solved_part, "col", axis=0, tiled=True),
    )
    full_left = full_left.reshape(tile_order, tile_rows, rank_width)
    full_solved = full_solved.reshape(tile_order, tile_rows, rank_width)
    first_pick = my_col // rows_total
    position = first_pick + 0
    picked_left = lax.dynamic_slice_in_dim(full_left, position, 1, 1)
    picked_solved = lax.dynamic_slice_in_dim(full_solved, position, 1, 1)
    send_left = picked_left.reshape(tile_order, column_tiles * rank_width)
    send_solved = picked_solved.reshape(tile_order, column_tiles * rank_width)
    root_row = my_col % rows_total
    column_left, column_solved = (
        spread(send_left, "row", root_row),
        spread(send_solved, "row", root_row),
    )
    row_factor = jnp.swapaxes(full_left, 0, 1)[:, None]
    row_solved = jnp.swapaxes(full_solved, 0, 1)
    column_factor = jnp.swapaxes(column_left.reshape(tile_order, column_tiles, rank_width), 0, 1)
    column_three = jnp.swapaxes(column_solved.reshape(tile_order, column_tiles, rank_width), 0, 1)
    core_block = jnp.einsum(
        "tbr,sbq->tsrq", row_solved, column_three, preferred_element_type=jnp.float32
    )
    slab_keep = jnp.arange(rank_width, dtype=jnp.int32) < slab_ranks[..., None]
    masked_right = jnp.where(slab_keep[:, :, None, :], slab_right, jnp.zeros((), jnp.bfloat16))
    fresh_left, fresh_right = recompress(
        slab_left, masked_right, row_factor, core_block, column_factor, sketch.astype(jnp.float32)
    )
    row_ids = jnp.arange(tile_rows, dtype=jnp.int32) * rows_total + my_row
    col_ids = jnp.arange(column_tiles, dtype=jnp.int32) * cols_total + my_col
    live_tile = (row_ids[:, None] > col_ids[None, :])[:, :, None, None]
    return (
        jnp.where(live_tile, fresh_left, 0.0).astype(jnp.bfloat16),
        jnp.where(live_tile, fresh_right, 0.0).astype(jnp.bfloat16),
    )


def nt(first, second):
    return lax.dot_general(first, second, (((1,), (1,)), ((), ())), preferred_element_type=F32)


def nn(first, second):
    return lax.dot_general(first, second, (((1,), (0,)), ((), ())), preferred_element_type=F32)


def split(value):
    high = value.astype(BF16)
    return high, (value - high.astype(F32)).astype(BF16)


def wide(value):
    return jnp.concatenate(split(value), axis=0)


def fold(value):
    half = value.shape[0] // 2
    return value[:half] + value[half:]


def dot_split(op, first, second_parts):
    stacked = wide(first)
    return fold(op(stacked, second_parts[0]) + op(stacked, second_parts[1]))


def grant(mebibytes):
    return pltpu.CompilerParams(vmem_limit_bytes=mebibytes << 20)


def solve_kernel(width, info, right_ref, inverse_ref, out_ref):
    right = right_ref[...]
    rows = lax.broadcasted_iota(jnp.int32, right.shape, 0)
    keep = jnp.zeros(right.shape, jnp.bool_)
    for tile in range(right.shape[0] // width):
        keep |= (rows >= tile * width) & (rows < tile * width + info[2 + tile])
    masked = jnp.where(keep, right, jnp.zeros((), right.dtype))
    out_ref[0] = nt(masked, inverse_ref[...])


def solve_part(info, right, inverse, odd, parts, width):
    lines, piece = right.shape
    return pl.pallas_call(
        functools.partial(solve_kernel, width),
        grid_spec=pltpu.PrefetchScalarGridSpec(
            num_scalar_prefetch=1,
            grid=(parts,),
            in_specs=[
                pl.BlockSpec((lines, piece), lambda step, info: (0, 0)),
                pl.BlockSpec((piece, piece), lambda step, info: (info[1] ^ (2 * step + odd), 0)),
            ],
            out_specs=pl.BlockSpec((1, lines, piece), lambda step, info: (step, 0, 0)),
        ),
        out_shape=jax.ShapeDtypeStruct((parts, lines, piece), F32),
        name="solve_odd" if odd else "solve_even",
        compiler_params=grant(4),
        cost_estimate=pl.CostEstimate(
            flops=2 * parts * lines * piece * piece,
            bytes_accessed=2 * parts * piece * piece + 4 * parts * lines * piece,
            transcendentals=0,
        ),
    )(info, right, inverse)


def pair_add_kernel(parts, mine_ref, other_ref, keep_ref, *send_refs):
    keep_ref[...] = mine_ref[0] + other_ref[0]
    for step in range(1, parts):
        send_refs[step - 1][...] = (mine_ref[step] + other_ref[step]).astype(
            send_refs[step - 1].dtype
        )


def in_vmem(count):
    return [pl.BlockSpec(memory_space=VMEM)] * count


def small_cost(bytes_accessed, flops=0):
    return pl.CostEstimate(flops=flops, bytes_accessed=bytes_accessed, transcendentals=0)


def pair_add(mine, other, send_type):
    parts = mine.shape[0]
    shape = mine.shape[1:]
    return pl.pallas_call(
        functools.partial(pair_add_kernel, parts),
        in_specs=in_vmem(2),
        out_specs=in_vmem(parts),
        out_shape=[jax.ShapeDtypeStruct(shape, F32)]
        + [jax.ShapeDtypeStruct(shape, send_type)] * (parts - 1),
        name="pair_add",
        compiler_params=grant(4),
        cost_estimate=small_cost(3 * mine.size * 4),
    )(mine, other)


def gather_add_kernel(count, head_lines, *refs):
    total = refs[0][...]
    for ref in refs[1:count]:
        total = total + ref[...].astype(F32)
    rounded = total.astype(BF16)
    refs[count][...] = rounded
    refs[count + 1][...] = rounded[:head_lines]


def gather_add(first, others, head_lines):
    count = 1 + len(others)
    return pl.pallas_call(
        functools.partial(gather_add_kernel, count, head_lines),
        in_specs=in_vmem(count),
        out_specs=in_vmem(2),
        out_shape=[
            jax.ShapeDtypeStruct(first.shape, BF16),
            jax.ShapeDtypeStruct((head_lines, first.shape[1]), BF16),
        ],
        name="gather_add",
        compiler_params=grant(4),
        cost_estimate=small_cost(first.size * 10),
    )(first, *others)


def core_kernel(rows_total, cols_total, width, info, own_ref, *refs):
    others = refs[: rows_total - 1]
    even_ref, odd_ref, stage = refs[rows_total - 1 :]
    my_row, my_col = info[0], info[1]
    for shift in range(rows_total):
        source = own_ref if shift == 0 else others[shift - 1]
        from_row = lax.rem(my_row - shift + rows_total, rows_total)
        for index in range(cols_total // rows_total):
            relative = my_col ^ (index * rows_total + from_row)
            place = (relative & 1) * (cols_total // 2) + lax.shift_right_logical(relative, 1)
            stage[place] = source[index * width : (index + 1) * width, :]
    piece = own_ref.shape[1]
    half = cols_total // 2
    own = own_ref[...]
    for part, ref in ((1, odd_ref), (0, even_ref)):
        block = stage[part * half : (part + 1) * half].reshape(half * width, piece)
        ref[...] = nt(block, own).reshape(ref.shape)


def core_parts(info, own, others, rows_total, cols_total, width):
    lines, piece = own.shape
    half = cols_total // 2
    shape = jax.ShapeDtypeStruct((half, width, lines), F32)
    return pl.pallas_call(
        functools.partial(core_kernel, rows_total, cols_total, width),
        in_specs=[pl.BlockSpec(memory_space=SMEM)] + in_vmem(rows_total),
        out_specs=in_vmem(2),
        out_shape=[shape, shape],
        scratch_shapes=[VMEM((cols_total, width, piece), BF16)],
        name="core_parts",
        compiler_params=grant(4),
        cost_estimate=small_cost(400000, 2 * lines * piece * cols_total * width),
    )(info, own, *others)


def message_kernel(rows_total, cols_total, width, info, own_ref, *refs):
    others = refs[: rows_total - 1]
    message_refs = refs[rows_total - 1 : -1]
    stage = refs[-1]
    my_row, my_col = info[0], info[1]
    lines = own_ref.shape[0]
    for shift in range(rows_total):
        source = own_ref if shift == 0 else others[shift - 1]
        from_row = lax.rem(my_row - shift + rows_total, rows_total)
        for index in range(cols_total // rows_total):
            stage[index * rows_total + from_row] = source[index * width : (index + 1) * width, :]
    for step, ref in enumerate(message_refs):
        target = my_col ^ (2 * step)
        ref[:width] = stage[target]
        ref[width : width + lines] = own_ref[...]
        ref[width + lines :] = stage[target ^ 1]


def messages(info, own, others, rows_total, cols_total, width):
    lines, piece = own.shape
    half = cols_total // 2
    return pl.pallas_call(
        functools.partial(message_kernel, rows_total, cols_total, width),
        in_specs=[pl.BlockSpec(memory_space=SMEM)] + in_vmem(rows_total),
        out_specs=in_vmem(half),
        out_shape=[jax.ShapeDtypeStruct((lines + 2 * width, piece), BF16)] * half,
        scratch_shapes=[VMEM((cols_total, width, piece), BF16)],
        name="messages",
        compiler_params=grant(4),
        cost_estimate=small_cost(half * (lines + 2 * width) * piece * 4),
    )(info, own, *others)


def bundle_kernel(count, width, *refs):
    out_ref = refs[count]
    for step in range(count):
        out_ref[step] = refs[step][width:]


def bundle(pieces, width):
    lines, piece = pieces[0].shape
    count = len(pieces)
    return pl.pallas_call(
        functools.partial(bundle_kernel, count, width),
        in_specs=in_vmem(count),
        out_specs=pl.BlockSpec(memory_space=VMEM),
        out_shape=jax.ShapeDtypeStruct((count, lines - width, piece), BF16),
        name="bundle",
        compiler_params=grant(4),
        cost_estimate=small_cost(count * (lines - width) * piece * 4),
    )(*pieces)


def piece_views(even_refs, odd_ref, width, lines):
    for step, ref in enumerate(even_refs):
        yield 2 * step, ref.at[width : width + lines], ref.at[:width]
    for step in range(len(even_refs)):
        yield 2 * step + 1, odd_ref.at[step, :lines], odd_ref.at[step, lines:]


def gram_kernel(half, width, info, left_ref, right_ref, sketch_ref, *refs):
    even_refs = refs[:half]
    odd_ref, row_gram_ref, column_gram_ref = refs[half:]
    lines = left_ref.shape[0]
    piece = odd_ref.shape[2]
    my_col = info[1]
    row_gram = jnp.zeros(row_gram_ref.shape, F32)
    column_gram = jnp.zeros(column_gram_ref.shape, F32)
    for relative, panel, column in piece_views(even_refs, odd_ref, width, lines):
        spot = pl.ds(pl.multiple_of((my_col ^ relative) * piece, LANES), piece)
        rows = jnp.concatenate([left_ref[:, spot], panel[...]], axis=0)
        row_gram = row_gram + nt(rows, rows)
        columns = jnp.concatenate([right_ref[:, spot], column[...]], axis=0)
        tall = jnp.concatenate([columns, sketch_ref[:, spot]], axis=0)
        column_gram = column_gram + nt(tall, columns)
    row_gram_ref[...] = row_gram
    column_gram_ref[...] = column_gram


def grams(info, left, right, sketch, even, odd, width):
    lines, order = left.shape
    half = len(even)
    return pl.pallas_call(
        functools.partial(gram_kernel, half, width),
        in_specs=[pl.BlockSpec(memory_space=SMEM)] + in_vmem(4 + half),
        out_specs=in_vmem(2),
        out_shape=[
            jax.ShapeDtypeStruct((2 * lines, 2 * lines), F32),
            jax.ShapeDtypeStruct((lines + 2 * width, lines + width), F32),
        ],
        name="grams",
        compiler_params=grant(16),
        cost_estimate=small_cost(2000000, 2 * order * lines * lines * 8),
    )(info, left, right, sketch, *even, odd)


def factor_and_apply(gram, shift, bands):
    width = gram.shape[0]
    blocks = width // 8
    lanes = lax.broadcasted_iota(jnp.int32, (8, LANES), 1)
    group = lanes - lax.rem(lanes, width)
    sub = lax.broadcasted_iota(jnp.int32, (8, LANES), 0)
    gram_rows = [gram[8 * b : 8 * b + 8] for b in range(blocks)]
    bands = [[band[8 * b : 8 * b + 8] for b in range(blocks)] for band in bands]
    rows = []
    for k in range(width):
        first = k // 8
        rows.append(
            {
                b: jnp.take_along_axis(gram_rows[b], group + k, axis=1)
                for b in range(first, blocks)
            }
        )
    for k in range(width):
        first, inner = divmod(k, 8)
        row = rows[k]
        pivot = row[first][inner : inner + 1] + shift[:1]
        scale = lax.rsqrt(pivot)
        scaled = {b: row[b] * scale for b in row}
        for i in range(k + 1, width):
            lead = scaled[i // 8][i % 8 : i % 8 + 1]
            for b in rows[i]:
                rows[i][b] = rows[i][b] - lead * scaled[b]
        below = dict(scaled)
        below[first] = jnp.where(sub > inner, scaled[first], 0.0)
        for band in bands:
            done = band[first][inner : inner + 1] * scale
            for b in range(first, blocks):
                band[b] = band[b] - below[b] * done
            band[first] = jnp.where(sub == inner, done, band[first])
    return [jnp.concatenate(band, axis=0) for band in bands]


def finish_kernel(half, width, rows_total, info, *refs):
    core_refs = refs[:half]
    row_gram_ref, column_gram_ref, left_ref, right_ref = refs[half : half + 4]
    even_refs = refs[half + 4 : 2 * half + 4]
    odd_ref, out_left_ref, out_right_ref = refs[2 * half + 4 :]
    my_row, my_col = info[0], info[1]
    lines, order = left_ref.shape
    tiles = lines // width
    piece = odd_ref.shape[2]
    lane = lax.broadcasted_iota(jnp.int32, (lines, lines), 1)
    line = lax.broadcasted_iota(jnp.int32, (lines, lines), 0)
    same = (lane // width) == (line // width)

    def diagonal(value):
        return jnp.where(same, value, 0.0)

    def stacked(value):
        return diagonal(jnp.concatenate([value] * tiles, axis=0))

    def blocks(value):
        return jnp.concatenate([stacked(value[:, :lines]), stacked(value[:, lines:])], axis=1)

    lane_row = lax.broadcasted_iota(jnp.int32, (1, lines), 1)
    line_col = lax.broadcasted_iota(jnp.int32, (lines, 1), 0)
    keep_lane = jnp.zeros((1, lines), jnp.bool_)
    keep_line = jnp.zeros((lines, 1), jnp.bool_)
    live_line = jnp.zeros((1, lines), jnp.bool_)
    for tile in range(tiles):
        low, high = tile * width, tile * width + info[2 + tile]
        keep_lane |= (lane_row >= low) & (lane_row < high)
        keep_line |= (line_col >= low) & (line_col < high)
        live = (tile * rows_total + my_row) > my_col
        live_line |= (lane_row >= low) & (lane_row < low + jnp.where(live, width, 0))

    row_gram = row_gram_ref[...]
    row_parts = split(
        jnp.concatenate(
            [
                jnp.concatenate(
                    [diagonal(row_gram[:lines, :lines]), diagonal(row_gram[:lines, lines:])], axis=1
                ),
                jnp.concatenate(
                    [diagonal(row_gram[lines:, :lines]), diagonal(row_gram[lines:, lines:])], axis=1
                ),
            ],
            axis=0,
        )
    )
    column_gram = column_gram_ref[...]
    right_right = jnp.where(same & keep_line & keep_lane, column_gram[:lines, :lines], 0.0)
    right_column = jnp.where(keep_line, column_gram[:lines, lines:], 0.0)
    column_column = column_gram[lines : lines + width, lines:]
    sketch_right = jnp.where(keep_lane, column_gram[lines + width :, :lines], 0.0)
    sketch_column = column_gram[lines + width :, lines:]

    core = core_refs[0][...]
    for ref in core_refs[1:]:
        core = core + ref[...]
    core_split = split(core)
    core_blocks = stacked(core)
    core_block_split = split(core_blocks)

    first = jnp.concatenate([sketch_right, -dot_split(nn, sketch_column, core_split)], axis=1)
    ones = jnp.where(same, 1.0, 0.0).astype(BF16)

    def traced(one, two):
        both = jnp.sum(one * two, axis=0, keepdims=True)
        both = both[:, :lines] + both[:, lines:]
        high, low = split(jnp.broadcast_to(both, (8, lines)))
        return (nn(high, ones) + nn(low, ones)) * (shift_rate / width) + tiny_shift

    image = dot_split(nn, first, row_parts)
    shift = traced(first, image)
    gram = dot_split(nt, first, split(blocks(image)))
    top, bottom = factor_and_apply(gram, shift, [image[:, :lines], image[:, lines:]])
    basis = jnp.concatenate([top, bottom], axis=1)

    cross = -diagonal(dot_split(nn, right_column, core_split))
    inner = dot_split(nn, column_column, core_split)
    core_lines = core.T
    corner = diagonal(dot_split(nn, core_lines, split(inner)))
    middle_parts = split(
        jnp.concatenate(
            [
                jnp.concatenate([right_right, cross], axis=1),
                jnp.concatenate([cross.T, corner], axis=1),
            ],
            axis=0,
        )
    )
    second = dot_split(nn, basis, middle_parts)
    image = dot_split(nn, second, row_parts)
    shift = traced(second, image)
    gram = dot_split(nt, second, split(blocks(image)))
    back = -dot_split(nt, image[:, lines:], core_block_split)
    left_top, left_bottom, right_top, right_bottom = factor_and_apply(
        gram, shift, [second[:, :lines], second[:, lines:], image[:, :lines], back]
    )
    factor_size = factor_scale * math.sqrt(order)
    live_scale = jnp.where(live_line, factor_size, 0.0)
    live_back = jnp.where(live_line, 1.0 / factor_size, 0.0)
    left_small = wide(
        jnp.concatenate([stacked(left_top * live_scale), stacked(left_bottom * live_scale)], axis=1)
    )
    right_small = wide(
        jnp.concatenate(
            [
                stacked(jnp.where(keep_lane, right_top * live_back, 0.0)),
                stacked(right_bottom * live_back),
            ],
            axis=1,
        )
    )
    for relative, panel, column in piece_views(even_refs, odd_ref, width, lines):
        spot = pl.ds(pl.multiple_of((my_col ^ relative) * piece, LANES), piece)
        rows = jnp.concatenate([left_ref[:, spot], panel[...]], axis=0)
        out_left_ref[:, spot] = fold(nn(left_small, rows)).astype(BF16)
        columns = jnp.concatenate([right_ref[:, spot]] + [column[...]] * tiles, axis=0)
        out_right_ref[:, spot] = fold(nn(right_small, columns)).astype(BF16)


def finish(info, cores, row_gram, column_gram, left, right, even, odd, rows_total, width):
    half = len(even)
    shape = jax.ShapeDtypeStruct(left.shape, BF16)
    return pl.pallas_call(
        functools.partial(finish_kernel, half, width, rows_total),
        in_specs=[pl.BlockSpec(memory_space=SMEM)] + in_vmem(2 * half + 5),
        out_specs=in_vmem(2),
        out_shape=[shape, shape],
        name="finish",
        compiler_params=grant(16),
        cost_estimate=small_cost(5000000, 10**9),
    )(info, *cores, row_gram, column_gram, left, right, *even, odd)


def flat_lines(block):
    return jnp.swapaxes(block, -1, -2).reshape(-1, block.shape[-2])


def fast_shards(
    slab_left, slab_right, slab_ranks, panel_left, panel_right, panel_ranks, inverse_factor, sketch
):
    rows_total = lax.axis_size("row")
    cols_total = lax.axis_size("col")
    width = panel_left.shape[-1]
    half = cols_total // 2
    place = jnp.stack([lax.axis_index("row"), lax.axis_index("col")]).astype(jnp.int32)
    panel_info = jnp.concatenate([place, panel_ranks])
    slab_info = jnp.concatenate([place, slab_ranks.reshape(-1)])
    left, right = flat_lines(slab_left), flat_lines(slab_right)
    panel, solve_right = flat_lines(panel_left), flat_lines(panel_right)
    sketch_lines = flat_lines(sketch)
    head = width * (cols_total // rows_total)

    def swap(block, step):
        return lax.ppermute(block, "col", [(i, i ^ step) for i in range(cols_total)])

    def turn(block, shift):
        pairs = [(i, (i + shift) % rows_total) for i in range(rows_total)]
        return lax.ppermute(block, "row", pairs)

    def across(blocks):
        return [swap(block, 2 * (step + 1)) for step, block in enumerate(blocks)]

    def along(block):
        return [turn(block, shift) for shift in range(1, rows_total)]

    odd = solve_part(panel_info, solve_right, inverse_factor, 1, half, width)
    other = swap(odd, 1)
    even = solve_part(panel_info, solve_right, inverse_factor, 0, half, width)
    kept, *sends = pair_add(even, other, BF16)
    received = across(sends)
    panel_others = along(panel[:head])
    solved, solved_head = gather_add(kept, received, head)
    solved_others = along(solved_head)
    own_message, *sends = messages(slab_info, panel, panel_others, rows_total, cols_total, width)
    even_pieces = [own_message] + across(sends)
    core_even, core_odd = core_parts(
        slab_info, solved, solved_others, rows_total, cols_total, width
    )
    core_other = swap(core_odd, 1)
    odd_pieces = swap(bundle(even_pieces, width), 1)
    core_kept, *sends = pair_add(core_even, core_other, F32)
    cores = [core_kept] + across(sends)
    row_gram, column_gram = grams(
        slab_info, left, right, sketch_lines, even_pieces, odd_pieces, width
    )
    fresh_left, fresh_right = finish(
        slab_info,
        cores,
        row_gram,
        column_gram,
        left,
        right,
        even_pieces,
        odd_pieces,
        rows_total,
        width,
    )

    def placed(block):
        tiles = slab_left.shape[:2] + (width, slab_left.shape[2])
        return jnp.swapaxes(block.reshape(tiles), -1, -2)

    return placed(fresh_left), placed(fresh_right)


def fast_fits(rows_total, cols_total, tile_rows, piece_rows, width, column_tiles):
    return (
        column_tiles == 1
        and tile_rows * width == LANES
        and width % 8 == 0
        and piece_rows % LANES == 0
        and cols_total & (cols_total - 1) == 0
        and cols_total >= 4
        and cols_total % rows_total == 0
        and rows_total > 1
        and cols_total <= tile_rows * rows_total
    )


def shards(*args):
    tile_rows, piece_rows, width = args[3].shape
    rows_total, cols_total = lax.axis_size("row"), lax.axis_size("col")
    fits = fast_fits(rows_total, cols_total, tile_rows, piece_rows, width, args[0].shape[1])
    return fast_shards(*args) if fits else plain_shards(*args)


def solution(mesh):
    placed = (
        P("row", "col", None, None),
        P("row", "col", None, None),
        P("row", "col"),
        P("row", "col", None),
        P("row", "col", None),
        P("row"),
        P(None, "col"),
        P(),
    )
    return jax.shard_map(
        shards,
        mesh=mesh,
        in_specs=placed,
        out_specs=(P("row", "col", None, None), P("row", "col", None, None)),
        check_vma=False,
    )
```

```python
import functools
import math

import jax
import jax.numpy as jnp
from jax import lax
from jax.experimental import pallas as pl
from jax.experimental.pallas import tpu as pltpu
from jax.sharding import PartitionSpec as P


highest = lax.Precision.HIGHEST
stacked_precision = lax.Precision.HIGH
shift_rate = 0.01
tiny_shift = 1e-06
factor_scale = 0.5
LANES = 128
F32 = jnp.float32
BF16 = jnp.bfloat16
VMEM = pltpu.VMEM


def spread(block, axis, owner):
    block = jnp.where(lax.axis_index(axis) == owner, block, jnp.zeros_like(block))
    return lax.psum(block, axis)


def product(first_matrix, second_matrix):
    return jnp.matmul(first_matrix, second_matrix, precision=highest)


def stacked_product(first_matrix, second_matrix):
    return jnp.matmul(first_matrix, second_matrix, precision=stacked_precision)


def flipped(matrix):
    return jnp.swapaxes(matrix, -1, -2)


def orthonormal(vectors):
    gram_matrix = product(flipped(vectors), vectors)
    shift_value = (
        shift_rate * jnp.trace(gram_matrix, axis1=-2, axis2=-1) / gram_matrix.shape[-1] + tiny_shift
    )
    identity = jnp.eye(gram_matrix.shape[-1], dtype=gram_matrix.dtype)
    lower_factor = jnp.linalg.cholesky(gram_matrix + shift_value[..., None, None] * identity)
    solved_rows = lax.linalg.triangular_solve(
        lower_factor, flipped(vectors), left_side=True, lower=True
    )
    return flipped(solved_rows)


def recompress(slab_factor, masked_right, row_factor, core_block, column_factor, sketch_float):
    target_shape = core_block.shape[:2] + slab_factor.shape[2:]
    column_wide = jnp.broadcast_to(column_factor[None], target_shape)
    row_core = product(row_factor, core_block)
    column_core = product(column_wide, flipped(core_block))
    forward_left = jnp.concatenate([slab_factor.astype(jnp.float32), -row_core], axis=-1)
    forward_right = jnp.concatenate([masked_right.astype(jnp.float32), column_wide], axis=-1)
    backward_left = jnp.concatenate([masked_right.astype(jnp.float32), -column_core], axis=-1)
    backward_right = jnp.concatenate([slab_factor.astype(jnp.float32), row_factor], axis=-1)

    def forward(vectors):
        return stacked_product(forward_left, stacked_product(flipped(forward_right), vectors))

    def backward(vectors):
        return stacked_product(backward_left, stacked_product(flipped(backward_right), vectors))

    basis_now = orthonormal(forward(sketch_float))
    basis_now = orthonormal(forward(backward(basis_now)))
    projected = backward(basis_now)
    factor_size = factor_scale * math.sqrt(slab_factor.shape[-2])
    return (basis_now * factor_size, projected / factor_size)


def plain_shards(
    slab_left, slab_right, slab_ranks, panel_left, panel_right, panel_ranks, inverse_factor, sketch
):
    rows_total = lax.axis_size("row")
    cols_total = lax.axis_size("col")
    my_row = lax.axis_index("row")
    my_col = lax.axis_index("col")
    tile_rows, piece_rows, rank_width = panel_left.shape
    column_tiles = slab_left.shape[1]
    tile_order = inverse_factor.shape[0]
    panel_keep = jnp.arange(rank_width, dtype=jnp.int32)[None, :] < panel_ranks[:, None]
    masked_panel = jnp.where(panel_keep[:, None, :], panel_right, jnp.zeros((), jnp.bfloat16))
    flat_right = jnp.swapaxes(masked_panel, 0, 1).reshape(piece_rows, tile_rows * rank_width)
    flat_left = jnp.swapaxes(panel_left, 0, 1).reshape(piece_rows, tile_rows * rank_width)
    solved_part = lax.psum_scatter(
        jnp.dot(inverse_factor, flat_right, preferred_element_type=jnp.float32),
        "col",
        scatter_dimension=0,
        tiled=True,
    ).astype(jnp.bfloat16)
    full_left, full_solved = (
        lax.all_gather(flat_left, "col", axis=0, tiled=True),
        lax.all_gather(solved_part, "col", axis=0, tiled=True),
    )
    full_left = full_left.reshape(tile_order, tile_rows, rank_width)
    full_solved = full_solved.reshape(tile_order, tile_rows, rank_width)
    first_pick = my_col // rows_total
    position = first_pick + 0
    picked_left = lax.dynamic_slice_in_dim(full_left, position, 1, 1)
    picked_solved = lax.dynamic_slice_in_dim(full_solved, position, 1, 1)
    send_left = picked_left.reshape(tile_order, column_tiles * rank_width)
    send_solved = picked_solved.reshape(tile_order, column_tiles * rank_width)
    root_row = my_col % rows_total
    column_left, column_solved = (
        spread(send_left, "row", root_row),
        spread(send_solved, "row", root_row),
    )
    row_factor = jnp.swapaxes(full_left, 0, 1)[:, None]
    row_solved = jnp.swapaxes(full_solved, 0, 1)
    column_factor = jnp.swapaxes(column_left.reshape(tile_order, column_tiles, rank_width), 0, 1)
    column_three = jnp.swapaxes(column_solved.reshape(tile_order, column_tiles, rank_width), 0, 1)
    core_block = jnp.einsum(
        "tbr,sbq->tsrq", row_solved, column_three, preferred_element_type=jnp.float32
    )
    slab_keep = jnp.arange(rank_width, dtype=jnp.int32) < slab_ranks[..., None]
    masked_right = jnp.where(slab_keep[:, :, None, :], slab_right, jnp.zeros((), jnp.bfloat16))
    fresh_left, fresh_right = recompress(
        slab_left, masked_right, row_factor, core_block, column_factor, sketch.astype(jnp.float32)
    )
    row_ids = jnp.arange(tile_rows, dtype=jnp.int32) * rows_total + my_row
    col_ids = jnp.arange(column_tiles, dtype=jnp.int32) * cols_total + my_col
    live_tile = (row_ids[:, None] > col_ids[None, :])[:, :, None, None]
    return (
        jnp.where(live_tile, fresh_left, 0.0).astype(jnp.bfloat16),
        jnp.where(live_tile, fresh_right, 0.0).astype(jnp.bfloat16),
    )


def nt(first, second):
    return lax.dot_general(first, second, (((1,), (1,)), ((), ())), preferred_element_type=F32)


def nn(first, second):
    return lax.dot_general(first, second, (((1,), (0,)), ((), ())), preferred_element_type=F32)


def split(value):
    high = value.astype(BF16)
    return high, (value - high.astype(F32)).astype(BF16)


def wide(value):
    return jnp.concatenate(split(value), axis=0)


def fold(value):
    half = value.shape[0] // 2
    return value[:half] + value[half:]


def dot_split(op, first, second_parts):
    stacked = wide(first)
    return fold(op(stacked, second_parts[0]) + op(stacked, second_parts[1]))


def grant(mebibytes):
    return pltpu.CompilerParams(vmem_limit_bytes=mebibytes << 20)


def line_mask(tile_lines, ranks):
    width = tile_lines // ranks.shape[0]
    keep = (jnp.arange(width, dtype=jnp.int32)[None, :] < ranks[:, None]).astype(F32).reshape(-1)
    return (
        jnp.broadcast_to(keep[:, None], (tile_lines, LANES)),
        jnp.broadcast_to(keep[None, :], (8, tile_lines)),
    )


def in_vmem(count):
    return [pl.BlockSpec(memory_space=VMEM)] * count


def small_cost(bytes_accessed, flops=0):
    return pl.CostEstimate(flops=flops, bytes_accessed=bytes_accessed, transcendentals=0)


def solve_kernel(odd, right_hbm, inverse_hbm, out_ref, right_ref, inverse_ref, sems):
    parts = out_ref.shape[0]
    piece = right_ref.shape[1]
    my_col = lax.axis_index("col")
    first = pltpu.make_async_copy(right_hbm, right_ref, sems.at[parts])
    first.start()
    copies = []
    for step in range(parts):
        block = my_col ^ (2 * step + odd)
        copy = pltpu.make_async_copy(
            inverse_hbm.at[pl.ds(pl.multiple_of(block * piece, piece), piece)],
            inverse_ref.at[step],
            sems.at[step],
        )
        copy.start()
        copies.append(copy)
    first.wait()
    right = right_ref[...]
    for step, copy in enumerate(copies):
        copy.wait()
        out_ref[step] = nt(right, inverse_ref[step])


def solve_part(right, inverse, odd, parts):
    lines, piece = right.shape
    return pl.pallas_call(
        functools.partial(solve_kernel, odd),
        in_specs=[pl.BlockSpec(memory_space=pltpu.HBM)] * 2,
        out_specs=pl.BlockSpec(memory_space=VMEM),
        out_shape=jax.ShapeDtypeStruct((parts, lines, piece), F32),
        scratch_shapes=[
            VMEM((lines, piece), BF16),
            VMEM((parts, piece, piece), BF16),
            pltpu.SemaphoreType.DMA((parts + 1,)),
        ],
        name="solve_odd" if odd else "solve_even",
        compiler_params=grant(4),
        cost_estimate=small_cost(
            2 * parts * piece * piece + 4 * parts * lines * piece,
            2 * parts * lines * piece * piece,
        ),
    )(right, inverse)


def pair_add_kernel(mine_ref, other_ref, keep_ref, *send_refs):
    keep_ref[...] = mine_ref[0] + other_ref[0]
    for step, ref in enumerate(send_refs):
        ref[...] = (mine_ref[step + 1] + other_ref[step + 1]).astype(BF16)


def pair_add(mine, other):
    parts, lines, piece = mine.shape
    return pl.pallas_call(
        pair_add_kernel,
        in_specs=in_vmem(2),
        out_specs=in_vmem(parts),
        out_shape=[jax.ShapeDtypeStruct((lines, piece), F32)]
        + [jax.ShapeDtypeStruct((lines, piece), BF16)] * (parts - 1),
        name="pair_add",
        compiler_params=grant(4),
        cost_estimate=small_cost(3 * mine.size * 4),
    )(mine, other)


def gather_add_kernel(head, first_ref, panel_ref, mask_ref, *refs):
    *others, solved_ref, head_ref = refs
    total = first_ref[...]
    for ref in others:
        total = total + ref[...].astype(F32)
    keep = jnp.concatenate([mask_ref[...]] * (total.shape[1] // LANES), axis=1)
    rounded = jnp.where(keep > 0.0, total, 0.0).astype(BF16)
    solved_ref[...] = rounded
    head_ref[:head] = rounded[:head]
    head_ref[head:] = panel_ref[:head]


def gather_add(first, panel, mask, others, head):
    return pl.pallas_call(
        functools.partial(gather_add_kernel, head),
        in_specs=in_vmem(3 + len(others)),
        out_specs=in_vmem(2),
        out_shape=[
            jax.ShapeDtypeStruct(first.shape, BF16),
            jax.ShapeDtypeStruct((2 * head, first.shape[1]), BF16),
        ],
        name="gather_add",
        compiler_params=grant(4),
        cost_estimate=small_cost(first.size * 10),
    )(first, panel, mask, *others)


def bundle_kernel(*refs):
    *pieces, out_ref = refs
    for step, ref in enumerate(pieces):
        out_ref[step] = ref[...]


def bundle(pieces):
    count = len(pieces)
    return pl.pallas_call(
        bundle_kernel,
        in_specs=in_vmem(count),
        out_specs=pl.BlockSpec(memory_space=VMEM),
        out_shape=jax.ShapeDtypeStruct((count,) + pieces[0].shape, BF16),
        name="bundle",
        compiler_params=grant(4),
        cost_estimate=small_cost(count * pieces[0].size * 4),
    )(*pieces)


def both_halves(value):
    return jnp.concatenate(split(value), axis=1)


def from_halves(value):
    half = value.shape[1] // 2
    return value[:, :half].astype(F32) + value[:, half:].astype(F32)


def core_kernel(rows_total, cols_total, width, own_ref, panel_ref, *refs):
    others = refs[: rows_total - 1]
    even_ref, even_panel_ref, odd_ref, solved_stage, panel_stage = refs[rows_total - 1 :]
    my_row, my_col = lax.axis_index("row"), lax.axis_index("col")
    half = cols_total // 2
    per_row = cols_total // rows_total
    head = per_row * width
    for shift in range(rows_total):
        from_row = my_row ^ shift
        for index in range(per_row):
            relative = my_col ^ (index * rows_total + from_row)
            place = (relative & 1) * half + lax.shift_right_logical(relative, 1)
            lines = slice(index * width, (index + 1) * width)
            if shift == 0:
                solved_stage[place] = own_ref[lines, :]
                panel_stage[place] = panel_ref[lines, :]
            else:
                source = others[shift - 1]
                solved_stage[place] = source[lines, :]
                panel_stage[place] = source[head + index * width : head + (index + 1) * width, :]
    piece = own_ref.shape[1]
    own = own_ref[...]
    odd_core = nt(solved_stage[half:].reshape(half * width, piece), own)
    for step in range(half):
        odd_ref[step, :width] = both_halves(odd_core[step * width : (step + 1) * width])
        odd_ref[step, width:] = panel_stage[half + step]
    even_ref[...] = nt(solved_stage[:half].reshape(half * width, piece), own).reshape(
        even_ref.shape
    )
    even_panel_ref[...] = panel_stage[:half]


def core_parts(own, panel, others, rows_total, cols_total, width):
    lines, piece = own.shape
    half = cols_total // 2
    return pl.pallas_call(
        functools.partial(core_kernel, rows_total, cols_total, width),
        in_specs=in_vmem(1 + rows_total),
        out_specs=in_vmem(3),
        out_shape=[
            jax.ShapeDtypeStruct((half, width, lines), F32),
            jax.ShapeDtypeStruct((half, width, piece), BF16),
            jax.ShapeDtypeStruct((half, 2 * width, piece), BF16),
        ],
        scratch_shapes=[VMEM((cols_total, width, piece), BF16)] * 2,
        name="core_parts",
        compiler_params=grant(4),
        cost_estimate=small_cost(400000, 2 * lines * piece * cols_total * width),
    )(own, panel, *others)


def core_add_kernel(mine_ref, panel_ref, other_ref, keep_ref, keep_panel_ref, *send_refs):
    width = mine_ref.shape[1]
    for step in range(mine_ref.shape[0]):
        total = mine_ref[step] + from_halves(other_ref[step, :width])
        if step == 0:
            keep_ref[...] = total
            keep_panel_ref[:width] = panel_ref[0]
            keep_panel_ref[width:] = other_ref[0, width:]
        else:
            ref = send_refs[step - 1]
            ref[:width] = both_halves(total)
            ref[width : 2 * width] = panel_ref[step]
            ref[2 * width :] = other_ref[step, width:]


def core_add(mine, panel, other):
    half, width, lines = mine.shape
    piece = panel.shape[2]
    return pl.pallas_call(
        core_add_kernel,
        in_specs=in_vmem(3),
        out_specs=in_vmem(1 + half),
        out_shape=[
            jax.ShapeDtypeStruct((width, lines), F32),
            jax.ShapeDtypeStruct((2 * width, piece), BF16),
        ]
        + [jax.ShapeDtypeStruct((3 * width, piece), BF16)] * (half - 1),
        name="core_add",
        compiler_params=grant(4),
        cost_estimate=small_cost(1000000),
    )(mine, panel, other)


def piece_spot(relative, piece):
    block = lax.axis_index("col") ^ relative
    return pl.ds(pl.multiple_of(block * piece, LANES), piece)


def gram_kernel(left_ref, right_ref, sketch_ref, even_ref, odd_ref, row_ref, column_ref):
    half, _, piece = even_ref.shape
    row_gram = jnp.zeros(row_ref.shape, F32)
    column_gram = jnp.zeros(column_ref.shape, F32)
    for relative in range(2 * half):
        spot = piece_spot(relative, piece)
        source = odd_ref if relative & 1 else even_ref
        rows = jnp.concatenate([left_ref[:, spot], source[relative // 2]], axis=0)
        row_gram = row_gram + nt(rows, rows)
        right = right_ref[:, spot]
        tall = jnp.concatenate([right, sketch_ref[:, spot]], axis=0)
        column_gram = column_gram + nt(tall, right)
    row_ref[...] = row_gram
    column_ref[...] = column_gram


def grams(left, right, sketch, even, odd):
    lines, order = left.shape
    return pl.pallas_call(
        gram_kernel,
        in_specs=in_vmem(5),
        out_specs=in_vmem(2),
        out_shape=[
            jax.ShapeDtypeStruct((2 * lines, 2 * lines), F32),
            jax.ShapeDtypeStruct((lines + sketch.shape[0], lines), F32),
        ],
        name="grams",
        compiler_params=grant(16),
        cost_estimate=small_cost(2000000, 2 * order * lines * lines * 8),
    )(left, right, sketch, even, odd)


def factor_and_apply(gram, shift, bands):
    width = gram.shape[0]
    blocks = width // 8
    lanes = lax.broadcasted_iota(jnp.int32, (8, LANES), 1)
    group = lanes - lax.rem(lanes, width)
    sub = lax.broadcasted_iota(jnp.int32, (8, LANES), 0)
    gram_rows = [gram[8 * b : 8 * b + 8] for b in range(blocks)]
    bands = [[band[8 * b : 8 * b + 8] for b in range(blocks)] for band in bands]
    rows = []
    for k in range(width):
        first = k // 8
        rows.append(
            {
                b: jnp.take_along_axis(gram_rows[b], group + k, axis=1)
                for b in range(first, blocks)
            }
        )
    for k in range(width):
        first, inner = divmod(k, 8)
        row = rows[k]
        pivot = row[first][inner : inner + 1] + shift[:1]
        scale = lax.rsqrt(pivot)
        scaled = {b: row[b] * scale for b in row}
        for i in range(k + 1, width):
            lead = scaled[i // 8][i % 8 : i % 8 + 1]
            for b in rows[i]:
                rows[i][b] = rows[i][b] - lead * scaled[b]
        below = dict(scaled)
        below[first] = jnp.where(sub > inner, scaled[first], 0.0)
        for band in bands:
            done = band[first][inner : inner + 1] * scale
            for b in range(first, blocks):
                band[b] = band[b] - below[b] * done
            band[first] = jnp.where(sub == inner, done, band[first])
    return [jnp.concatenate(band, axis=0) for band in bands]


def finish_kernel(half, width, rows_total, *refs):
    core_ref, column_ref = refs[:2]
    core_refs = refs[2 : half + 1]
    (
        row_gram_ref,
        column_gram_ref,
        left_ref,
        right_ref,
        sketch_ref,
        even_ref,
        odd_ref,
        keep_line_ref,
        keep_lane_ref,
        out_left_ref,
        out_right_ref,
    ) = refs[half + 1 :]
    my_row, my_col = lax.axis_index("row"), lax.axis_index("col")
    lines, order = left_ref.shape
    tiles = lines // width
    piece = odd_ref.shape[2]
    lane = lax.broadcasted_iota(jnp.int32, (lines, lines), 1)
    line = lax.broadcasted_iota(jnp.int32, (lines, lines), 0)
    same = (lane // width) == (line // width)

    def diagonal(value):
        return jnp.where(same, value, 0.0)

    def stacked(value):
        return diagonal(jnp.concatenate([value] * tiles, axis=0))

    def blocks(value):
        return jnp.concatenate([stacked(value[:, :lines]), stacked(value[:, lines:])], axis=1)

    def column_piece(relative):
        step, side = divmod(relative, 2)
        if step == 0:
            return column_ref[side * width : (side + 1) * width]
        return core_refs[step - 1][(1 + side) * width : (2 + side) * width]

    keep_line = keep_line_ref[...] > 0.0
    keep_lane = keep_lane_ref[:1] > 0.0
    lane_row = lax.broadcasted_iota(jnp.int32, (1, lines), 1)
    live_line = jnp.zeros((1, lines), jnp.bool_)
    for tile in range(tiles):
        low = tile * width
        live = (tile * rows_total + my_row) > my_col
        live_line |= (lane_row >= low) & (lane_row < low + jnp.where(live, width, 0))

    right_column = jnp.zeros((lines, width), F32)
    column_column = jnp.zeros((width, width), F32)
    sketch_column = jnp.zeros((width, width), F32)
    for relative in range(2 * half):
        spot = piece_spot(relative, piece)
        column = column_piece(relative)
        tall = nt(jnp.concatenate([right_ref[:, spot], column, sketch_ref[:, spot]], axis=0), column)
        right_column = right_column + tall[:lines]
        column_column = column_column + tall[lines : lines + width]
        sketch_column = sketch_column + tall[lines + width :]
    right_column = jnp.where(keep_line[:, :width], right_column, 0.0)

    row_gram = row_gram_ref[...]
    row_parts = split(
        jnp.concatenate(
            [
                jnp.concatenate(
                    [diagonal(row_gram[:lines, :lines]), diagonal(row_gram[:lines, lines:])], axis=1
                ),
                jnp.concatenate(
                    [diagonal(row_gram[lines:, :lines]), diagonal(row_gram[lines:, lines:])], axis=1
                ),
            ],
            axis=0,
        )
    )
    column_gram = column_gram_ref[...]
    right_right = jnp.where(same & keep_line & keep_lane, column_gram[:lines], 0.0)
    sketch_right = jnp.where(keep_lane, column_gram[lines:], 0.0)

    core = core_ref[...]
    for ref in core_refs:
        core = core + from_halves(ref[:width])
    core_split = split(core)
    core_blocks = stacked(core)
    core_block_split = split(core_blocks)

    first = jnp.concatenate([sketch_right, -dot_split(nn, sketch_column, core_split)], axis=1)
    ones = jnp.where(same, 1.0, 0.0).astype(BF16)

    def traced(one, two):
        both = jnp.sum(one * two, axis=0, keepdims=True)
        both = both[:, :lines] + both[:, lines:]
        high, low = split(jnp.broadcast_to(both, (8, lines)))
        return (nn(high, ones) + nn(low, ones)) * (shift_rate / width) + tiny_shift

    image = dot_split(nn, first, row_parts)
    shift = traced(first, image)
    gram = dot_split(nt, first, split(blocks(image)))
    top, bottom = factor_and_apply(gram, shift, [image[:, :lines], image[:, lines:]])
    basis = jnp.concatenate([top, bottom], axis=1)

    cross = -diagonal(dot_split(nn, right_column, core_split))
    inner = dot_split(nn, column_column, core_split)
    core_lines = core.T
    corner = diagonal(dot_split(nn, core_lines, split(inner)))
    middle_parts = split(
        jnp.concatenate(
            [
                jnp.concatenate([right_right, cross], axis=1),
                jnp.concatenate([cross.T, corner], axis=1),
            ],
            axis=0,
        )
    )
    second = dot_split(nn, basis, middle_parts)
    image = dot_split(nn, second, row_parts)
    shift = traced(second, image)
    gram = dot_split(nt, second, split(blocks(image)))
    back = -dot_split(nt, image[:, lines:], core_block_split)
    left_top, left_bottom, right_top, right_bottom = factor_and_apply(
        gram, shift, [second[:, :lines], second[:, lines:], image[:, :lines], back]
    )
    factor_size = factor_scale * math.sqrt(order)
    live_scale = jnp.where(live_line, factor_size, 0.0)
    live_back = jnp.where(live_line, 1.0 / factor_size, 0.0)
    left_small = wide(
        jnp.concatenate([stacked(left_top * live_scale), stacked(left_bottom * live_scale)], axis=1)
    )
    right_small = wide(
        jnp.concatenate(
            [
                stacked(jnp.where(keep_lane, right_top * live_back, 0.0)),
                stacked(right_bottom * live_back),
            ],
            axis=1,
        )
    )
    for relative in range(2 * half):
        spot = piece_spot(relative, piece)
        source = odd_ref if relative & 1 else even_ref
        rows = jnp.concatenate([left_ref[:, spot], source[relative // 2]], axis=0)
        out_left_ref[:, spot] = fold(nn(left_small, rows)).astype(BF16)
        columns = jnp.concatenate([right_ref[:, spot]] + [column_piece(relative)] * tiles, axis=0)
        out_right_ref[:, spot] = fold(nn(right_small, columns)).astype(BF16)


def finish(core, column, cores, others, rows_total, width):
    half = len(cores) + 1
    left = others[2]
    shape = jax.ShapeDtypeStruct(left.shape, BF16)
    operands = (core, column, *cores, *others)
    return pl.pallas_call(
        functools.partial(finish_kernel, half, width, rows_total),
        in_specs=in_vmem(len(operands)),
        out_specs=in_vmem(2),
        out_shape=[shape, shape],
        name="finish",
        compiler_params=grant(16),
        cost_estimate=small_cost(5000000, 10**9),
    )(*operands)


def flat_lines(block):
    return jnp.swapaxes(block, -1, -2).reshape(-1, block.shape[-2])


def fast_shards(
    slab_left, slab_right, slab_ranks, panel_left, panel_right, panel_ranks, inverse_factor, sketch
):
    rows_total = lax.axis_size("row")
    cols_total = lax.axis_size("col")
    width = panel_left.shape[-1]
    half = cols_total // 2
    left, right = flat_lines(slab_left), flat_lines(slab_right)
    panel, solve_right = flat_lines(panel_left), flat_lines(panel_right)
    sketch_lines = flat_lines(sketch)
    head = width * (cols_total // rows_total)

    def swap(block, step):
        return lax.ppermute(block, "col", [(i, i ^ step) for i in range(cols_total)])

    def turn(block, shift):
        pairs = [(i, i ^ shift) for i in range(rows_total)]
        return lax.ppermute(block, "row", pairs)

    def across(blocks):
        return [swap(block, 2 * (step + 1)) for step, block in enumerate(blocks)]

    def along(block):
        return [turn(block, shift) for shift in range(1, rows_total)]

    panel_keep, _ = line_mask(panel.shape[0], panel_ranks)
    slab_line, slab_lane = line_mask(panel.shape[0], slab_ranks.reshape(-1))
    solve_right = pltpu.with_memory_space_constraint(solve_right, pltpu.HBM)
    inverse_factor = pltpu.with_memory_space_constraint(inverse_factor, pltpu.HBM)
    odd = solve_part(solve_right, inverse_factor, 1, half)
    other = swap(odd, 1)
    even = solve_part(solve_right, inverse_factor, 0, half)
    kept, *sends = pair_add(even, other)
    received = across(sends)
    solved, solved_head = gather_add(kept, panel, panel_keep, received, head)
    solved_others = along(solved_head)
    even_panel = bundle([panel] + across([panel] * (half - 1)))
    odd_panel = swap(even_panel, 1)
    row_gram, column_gram = grams(left, right, sketch_lines, even_panel, odd_panel)
    core_even, even_column, odd_message = core_parts(
        solved, panel, solved_others, rows_total, cols_total, width
    )
    other = swap(odd_message, 1)
    core, column, *sends = core_add(core_even, even_column, other)
    cores = across(sends)
    fresh_left, fresh_right = finish(
        core,
        column,
        cores,
        (
            row_gram,
            column_gram,
            left,
            right,
            sketch_lines,
            even_panel,
            odd_panel,
            slab_line,
            slab_lane,
        ),
        rows_total,
        width,
    )

    def placed(block):
        tiles = slab_left.shape[:2] + (width, slab_left.shape[2])
        return jnp.swapaxes(block.reshape(tiles), -1, -2)

    return placed(fresh_left), placed(fresh_right)


def fast_fits(rows_total, cols_total, tile_rows, piece_rows, width, column_tiles):
    return (
        column_tiles == 1
        and tile_rows * width == LANES
        and width % 8 == 0
        and piece_rows % LANES == 0
        and cols_total & (cols_total - 1) == 0
        and cols_total >= 4
        and rows_total & (rows_total - 1) == 0
        and cols_total % rows_total == 0
        and rows_total > 1
        and cols_total <= tile_rows * rows_total
    )


def shards(*args):
    tile_rows, piece_rows, width = args[3].shape
    rows_total, cols_total = lax.axis_size("row"), lax.axis_size("col")
    fits = fast_fits(rows_total, cols_total, tile_rows, piece_rows, width, args[0].shape[1])
    return fast_shards(*args) if fits else plain_shards(*args)


def solution(mesh):
    placed = (
        P("row", "col", None, None),
        P("row", "col", None, None),
        P("row", "col"),
        P("row", "col", None),
        P("row", "col", None),
        P("row"),
        P(None, "col"),
        P(),
    )
    return jax.shard_map(
        shards,
        mesh=mesh,
        in_specs=placed,
        out_specs=(P("row", "col", None, None), P("row", "col", None, None)),
        check_vma=False,
    )
```

```python
import functools
import math

import jax
import jax.numpy as jnp
from jax import lax
from jax.experimental import pallas as pl
from jax.experimental.pallas import tpu as pltpu
from jax.sharding import PartitionSpec as P


highest = lax.Precision.HIGHEST
stacked_precision = lax.Precision.HIGH
shift_rate = 0.01
tiny_shift = 1e-06
factor_scale = 0.5
LANES = 128
F32 = jnp.float32
BF16 = jnp.bfloat16
VMEM = pltpu.VMEM


def spread(block, axis, owner):
    block = jnp.where(lax.axis_index(axis) == owner, block, jnp.zeros_like(block))
    return lax.psum(block, axis)


def product(first_matrix, second_matrix):
    return jnp.matmul(first_matrix, second_matrix, precision=highest)


def stacked_product(first_matrix, second_matrix):
    return jnp.matmul(first_matrix, second_matrix, precision=stacked_precision)


def flipped(matrix):
    return jnp.swapaxes(matrix, -1, -2)


def orthonormal(vectors):
    gram_matrix = product(flipped(vectors), vectors)
    shift_value = (
        shift_rate * jnp.trace(gram_matrix, axis1=-2, axis2=-1) / gram_matrix.shape[-1] + tiny_shift
    )
    identity = jnp.eye(gram_matrix.shape[-1], dtype=gram_matrix.dtype)
    lower_factor = jnp.linalg.cholesky(gram_matrix + shift_value[..., None, None] * identity)
    solved_rows = lax.linalg.triangular_solve(
        lower_factor, flipped(vectors), left_side=True, lower=True
    )
    return flipped(solved_rows)


def recompress(slab_factor, masked_right, row_factor, core_block, column_factor, sketch_float):
    target_shape = core_block.shape[:2] + slab_factor.shape[2:]
    column_wide = jnp.broadcast_to(column_factor[None], target_shape)
    row_core = product(row_factor, core_block)
    column_core = product(column_wide, flipped(core_block))
    forward_left = jnp.concatenate([slab_factor.astype(jnp.float32), -row_core], axis=-1)
    forward_right = jnp.concatenate([masked_right.astype(jnp.float32), column_wide], axis=-1)
    backward_left = jnp.concatenate([masked_right.astype(jnp.float32), -column_core], axis=-1)
    backward_right = jnp.concatenate([slab_factor.astype(jnp.float32), row_factor], axis=-1)

    def forward(vectors):
        return stacked_product(forward_left, stacked_product(flipped(forward_right), vectors))

    def backward(vectors):
        return stacked_product(backward_left, stacked_product(flipped(backward_right), vectors))

    basis_now = orthonormal(forward(sketch_float))
    basis_now = orthonormal(forward(backward(basis_now)))
    projected = backward(basis_now)
    factor_size = factor_scale * math.sqrt(slab_factor.shape[-2])
    return (basis_now * factor_size, projected / factor_size)


def plain_shards(
    slab_left, slab_right, slab_ranks, panel_left, panel_right, panel_ranks, inverse_factor, sketch
):
    rows_total = lax.axis_size("row")
    cols_total = lax.axis_size("col")
    my_row = lax.axis_index("row")
    my_col = lax.axis_index("col")
    tile_rows, piece_rows, rank_width = panel_left.shape
    column_tiles = slab_left.shape[1]
    tile_order = inverse_factor.shape[0]
    panel_keep = jnp.arange(rank_width, dtype=jnp.int32)[None, :] < panel_ranks[:, None]
    masked_panel = jnp.where(panel_keep[:, None, :], panel_right, jnp.zeros((), jnp.bfloat16))
    flat_right = jnp.swapaxes(masked_panel, 0, 1).reshape(piece_rows, tile_rows * rank_width)
    flat_left = jnp.swapaxes(panel_left, 0, 1).reshape(piece_rows, tile_rows * rank_width)
    solved_part = lax.psum_scatter(
        jnp.dot(inverse_factor, flat_right, preferred_element_type=jnp.float32),
        "col",
        scatter_dimension=0,
        tiled=True,
    ).astype(jnp.bfloat16)
    full_left, full_solved = (
        lax.all_gather(flat_left, "col", axis=0, tiled=True),
        lax.all_gather(solved_part, "col", axis=0, tiled=True),
    )
    full_left = full_left.reshape(tile_order, tile_rows, rank_width)
    full_solved = full_solved.reshape(tile_order, tile_rows, rank_width)
    first_pick = my_col // rows_total
    position = first_pick + 0
    picked_left = lax.dynamic_slice_in_dim(full_left, position, 1, 1)
    picked_solved = lax.dynamic_slice_in_dim(full_solved, position, 1, 1)
    send_left = picked_left.reshape(tile_order, column_tiles * rank_width)
    send_solved = picked_solved.reshape(tile_order, column_tiles * rank_width)
    root_row = my_col % rows_total
    column_left, column_solved = (
        spread(send_left, "row", root_row),
        spread(send_solved, "row", root_row),
    )
    row_factor = jnp.swapaxes(full_left, 0, 1)[:, None]
    row_solved = jnp.swapaxes(full_solved, 0, 1)
    column_factor = jnp.swapaxes(column_left.reshape(tile_order, column_tiles, rank_width), 0, 1)
    column_three = jnp.swapaxes(column_solved.reshape(tile_order, column_tiles, rank_width), 0, 1)
    core_block = jnp.einsum(
        "tbr,sbq->tsrq", row_solved, column_three, preferred_element_type=jnp.float32
    )
    slab_keep = jnp.arange(rank_width, dtype=jnp.int32) < slab_ranks[..., None]
    masked_right = jnp.where(slab_keep[:, :, None, :], slab_right, jnp.zeros((), jnp.bfloat16))
    fresh_left, fresh_right = recompress(
        slab_left, masked_right, row_factor, core_block, column_factor, sketch.astype(jnp.float32)
    )
    row_ids = jnp.arange(tile_rows, dtype=jnp.int32) * rows_total + my_row
    col_ids = jnp.arange(column_tiles, dtype=jnp.int32) * cols_total + my_col
    live_tile = (row_ids[:, None] > col_ids[None, :])[:, :, None, None]
    return (
        jnp.where(live_tile, fresh_left, 0.0).astype(jnp.bfloat16),
        jnp.where(live_tile, fresh_right, 0.0).astype(jnp.bfloat16),
    )


def nt(first, second):
    return lax.dot_general(first, second, (((1,), (1,)), ((), ())), preferred_element_type=F32)


def nn(first, second):
    return lax.dot_general(first, second, (((1,), (0,)), ((), ())), preferred_element_type=F32)


def split(value):
    high = value.astype(BF16)
    return high, (value - high.astype(F32)).astype(BF16)


def wide(value):
    return jnp.concatenate(split(value), axis=0)


def fold(value):
    half = value.shape[0] // 2
    return value[:half] + value[half:]


def dot_split(op, first, second_parts):
    stacked = wide(first)
    return fold(op(stacked, second_parts[0]) + op(stacked, second_parts[1]))


def grant(mebibytes):
    return pltpu.CompilerParams(vmem_limit_bytes=mebibytes << 20)


def line_mask(tile_lines, ranks):
    width = tile_lines // ranks.shape[0]
    keep = (jnp.arange(width, dtype=jnp.int32)[None, :] < ranks[:, None]).astype(F32).reshape(-1)
    return (
        jnp.broadcast_to(keep[:, None], (tile_lines, LANES)),
        jnp.broadcast_to(keep[None, :], (8, tile_lines)),
    )


def in_vmem(count):
    return [pl.BlockSpec(memory_space=VMEM)] * count


def small_cost(bytes_accessed, flops=0):
    return pl.CostEstimate(flops=flops, bytes_accessed=bytes_accessed, transcendentals=0)


def solve_kernel(odd, right_hbm, inverse_hbm, out_ref, right_ref, inverse_ref, sems):
    parts = out_ref.shape[0]
    piece = right_ref.shape[1]
    my_col = lax.axis_index("col")
    first = pltpu.make_async_copy(right_hbm, right_ref, sems.at[parts])
    first.start()
    copies = []
    for step in range(parts):
        block = my_col ^ (2 * step + odd)
        copy = pltpu.make_async_copy(
            inverse_hbm.at[pl.ds(pl.multiple_of(block * piece, piece), piece)],
            inverse_ref.at[step],
            sems.at[step],
        )
        copy.start()
        copies.append(copy)
    first.wait()
    right = right_ref[...]
    for step, copy in enumerate(copies):
        copy.wait()
        out_ref[step] = nt(right, inverse_ref[step])


def solve_part(right, inverse, odd, parts):
    lines, piece = right.shape
    return pl.pallas_call(
        functools.partial(solve_kernel, odd),
        in_specs=[pl.BlockSpec(memory_space=pltpu.HBM)] * 2,
        out_specs=pl.BlockSpec(memory_space=VMEM),
        out_shape=jax.ShapeDtypeStruct((parts, lines, piece), F32),
        scratch_shapes=[
            VMEM((lines, piece), BF16),
            VMEM((parts, piece, piece), BF16),
            pltpu.SemaphoreType.DMA((parts + 1,)),
        ],
        name="solve_odd" if odd else "solve_even",
        compiler_params=grant(4),
        cost_estimate=small_cost(
            2 * parts * piece * piece + 4 * parts * lines * piece,
            2 * parts * lines * piece * piece,
        ),
    )(right, inverse)


def pair_add_kernel(mine_ref, other_ref, keep_ref, *send_refs):
    keep_ref[...] = mine_ref[0] + other_ref[0]
    for step, ref in enumerate(send_refs):
        ref[...] = (mine_ref[step + 1] + other_ref[step + 1]).astype(BF16)


def pair_add(mine, other):
    parts, lines, piece = mine.shape
    return pl.pallas_call(
        pair_add_kernel,
        in_specs=in_vmem(2),
        out_specs=in_vmem(parts),
        out_shape=[jax.ShapeDtypeStruct((lines, piece), F32)]
        + [jax.ShapeDtypeStruct((lines, piece), BF16)] * (parts - 1),
        name="pair_add",
        compiler_params=grant(4),
        cost_estimate=small_cost(3 * mine.size * 4),
    )(mine, other)


def gather_add_kernel(head, first_ref, panel_ref, mask_ref, *refs):
    *others, solved_ref, head_ref = refs
    total = first_ref[...]
    for ref in others:
        total = total + ref[...].astype(F32)
    keep = jnp.concatenate([mask_ref[...]] * (total.shape[1] // LANES), axis=1)
    rounded = jnp.where(keep > 0.0, total, 0.0).astype(BF16)
    solved_ref[...] = rounded
    head_ref[:head] = rounded[:head]
    head_ref[head:] = panel_ref[:head]


def gather_add(first, panel, mask, others, head):
    return pl.pallas_call(
        functools.partial(gather_add_kernel, head),
        in_specs=in_vmem(3 + len(others)),
        out_specs=in_vmem(2),
        out_shape=[
            jax.ShapeDtypeStruct(first.shape, BF16),
            jax.ShapeDtypeStruct((2 * head, first.shape[1]), BF16),
        ],
        name="gather_add",
        compiler_params=grant(4),
        cost_estimate=small_cost(first.size * 10),
    )(first, panel, mask, *others)


def bundle_kernel(*refs):
    *pieces, out_ref = refs
    for step, ref in enumerate(pieces):
        out_ref[step] = ref[...]


def bundle(pieces):
    count = len(pieces)
    return pl.pallas_call(
        bundle_kernel,
        in_specs=in_vmem(count),
        out_specs=pl.BlockSpec(memory_space=VMEM),
        out_shape=jax.ShapeDtypeStruct((count,) + pieces[0].shape, BF16),
        name="bundle",
        compiler_params=grant(4),
        cost_estimate=small_cost(count * pieces[0].size * 4),
    )(*pieces)


def both_halves(value):
    return jnp.concatenate(split(value), axis=1)


def from_halves(value):
    half = value.shape[1] // 2
    return value[:, :half].astype(F32) + value[:, half:].astype(F32)


def core_kernel(rows_total, cols_total, width, own_ref, panel_ref, *refs):
    others = refs[: rows_total - 1]
    even_ref, even_panel_ref, odd_ref, solved_stage, panel_stage = refs[rows_total - 1 :]
    my_row, my_col = lax.axis_index("row"), lax.axis_index("col")
    half = cols_total // 2
    per_row = cols_total // rows_total
    head = per_row * width
    for shift in range(rows_total):
        from_row = my_row ^ shift
        for index in range(per_row):
            relative = my_col ^ (index * rows_total + from_row)
            place = (relative & 1) * half + lax.shift_right_logical(relative, 1)
            lines = slice(index * width, (index + 1) * width)
            if shift == 0:
                solved_stage[place] = own_ref[lines, :]
                panel_stage[place] = panel_ref[lines, :]
            else:
                source = others[shift - 1]
                solved_stage[place] = source[lines, :]
                panel_stage[place] = source[head + index * width : head + (index + 1) * width, :]
    piece = own_ref.shape[1]
    own = own_ref[...]
    odd_core = nt(solved_stage[half:].reshape(half * width, piece), own)
    for step in range(half):
        odd_ref[step, :width] = both_halves(odd_core[step * width : (step + 1) * width])
        odd_ref[step, width:] = panel_stage[half + step]
    even_ref[...] = nt(solved_stage[:half].reshape(half * width, piece), own).reshape(
        even_ref.shape
    )
    even_panel_ref[...] = panel_stage[:half]


def core_parts(own, panel, others, rows_total, cols_total, width):
    lines, piece = own.shape
    half = cols_total // 2
    return pl.pallas_call(
        functools.partial(core_kernel, rows_total, cols_total, width),
        in_specs=in_vmem(1 + rows_total),
        out_specs=in_vmem(3),
        out_shape=[
            jax.ShapeDtypeStruct((half, width, lines), F32),
            jax.ShapeDtypeStruct((half, width, piece), BF16),
            jax.ShapeDtypeStruct((half, 2 * width, piece), BF16),
        ],
        scratch_shapes=[VMEM((cols_total, width, piece), BF16)] * 2,
        name="core_parts",
        compiler_params=grant(4),
        cost_estimate=small_cost(400000, 2 * lines * piece * cols_total * width),
    )(own, panel, *others)


def core_add_kernel(mine_ref, panel_ref, other_ref, keep_ref, keep_panel_ref, *send_refs):
    width = mine_ref.shape[1]
    for step in range(mine_ref.shape[0]):
        total = mine_ref[step] + from_halves(other_ref[step, :width])
        if step == 0:
            keep_ref[...] = total
            keep_panel_ref[:width] = panel_ref[0]
            keep_panel_ref[width:] = other_ref[0, width:]
        else:
            ref = send_refs[step - 1]
            ref[:width] = both_halves(total)
            ref[width : 2 * width] = panel_ref[step]
            ref[2 * width :] = other_ref[step, width:]


def core_add(mine, panel, other):
    half, width, lines = mine.shape
    piece = panel.shape[2]
    return pl.pallas_call(
        core_add_kernel,
        in_specs=in_vmem(3),
        out_specs=in_vmem(1 + half),
        out_shape=[
            jax.ShapeDtypeStruct((width, lines), F32),
            jax.ShapeDtypeStruct((2 * width, piece), BF16),
        ]
        + [jax.ShapeDtypeStruct((3 * width, piece), BF16)] * (half - 1),
        name="core_add",
        compiler_params=grant(4),
        cost_estimate=small_cost(1000000),
    )(mine, panel, other)


def piece_spot(relative, piece):
    block = lax.axis_index("col") ^ relative
    return pl.ds(pl.multiple_of(block * piece, LANES), piece)


def pieces_wide(ref, count, piece):
    return jnp.concatenate([ref[:, piece_spot(k, piece)] for k in range(count)], axis=1)


def same_tile(lines, width):
    lane = lax.broadcasted_iota(jnp.int32, (lines, lines), 1)
    line = lax.broadcasted_iota(jnp.int32, (lines, lines), 0)
    return (lane // width) == (line // width)


def gram_kernel(width, *refs):
    left_ref, right_ref, sketch_ref, even_ref, odd_ref, keep_line_ref, keep_lane_ref = refs[:7]
    row_high_ref, row_low_ref, right_gram_ref, sketch_right_ref = refs[7:]
    half, lines, piece = even_ref.shape
    count = 2 * half
    same = same_tile(lines, width)
    panel = jnp.concatenate(
        [(odd_ref if k & 1 else even_ref)[k // 2] for k in range(count)], axis=1
    )
    left = pieces_wide(left_ref, count, piece)
    for i, one in enumerate((left, panel)):
        for j, two in enumerate((left, panel)):
            high, low = split(jnp.where(same, nt(one, two), 0.0))
            row_high_ref[i * lines : (i + 1) * lines, j * lines : (j + 1) * lines] = high
            row_low_ref[i * lines : (i + 1) * lines, j * lines : (j + 1) * lines] = low
    right = right_ref[...]
    keep_line = keep_line_ref[...] > 0.0
    keep_lane = keep_lane_ref[:1] > 0.0
    right_gram_ref[...] = jnp.where(same & keep_line & keep_lane, nt(right, right), 0.0)
    sketch_right_ref[...] = jnp.where(keep_lane, nt(sketch_ref[...], right), 0.0)


def grams(left, right, sketch, even, odd, keep_line, keep_lane, width):
    lines, order = left.shape
    square = jax.ShapeDtypeStruct((2 * lines, 2 * lines), BF16)
    return pl.pallas_call(
        functools.partial(gram_kernel, width),
        in_specs=in_vmem(7),
        out_specs=in_vmem(4),
        out_shape=[
            square,
            square,
            jax.ShapeDtypeStruct((lines, lines), F32),
            jax.ShapeDtypeStruct((sketch.shape[0], lines), F32),
        ],
        name="grams",
        compiler_params=grant(16),
        cost_estimate=small_cost(2000000, 2 * order * lines * lines * 8),
    )(left, right, sketch, even, odd, keep_line, keep_lane)


def factor_and_apply(gram, shift, bands):
    width = gram.shape[0]
    count = width // 8
    chunk = count // 2
    lanes = lax.broadcasted_iota(jnp.int32, (8, LANES), 1)
    inner_lane = lax.rem(lanes, width)
    group = lanes - inner_lane
    sub = lax.broadcasted_iota(jnp.int32, (8, LANES), 0)
    inverse_shift = 1.0 / shift
    matrix = [
        gram[8 * b : 8 * b + 8] * inverse_shift + jnp.where(inner_lane == sub + 8 * b, 1.0, 0.0)
        for b in range(count)
    ]
    bands = [matrix] + [[band[8 * b : 8 * b + 8] for b in range(count)] for band in bands]

    def pick(vector, row):
        return vector[row : row + 1]

    for start in range(0, count, chunk):
        first_column = 8 * start
        columns = [
            {
                b: jnp.take_along_axis(matrix[b], group + first_column + k, axis=1)
                for b in range(start + k // 8, count)
            }
            for k in range(8 * chunk)
        ]
        last_half = start + chunk == count
        for k in range(0, 8 * chunk, 2):
            b, row = start + k // 8, k % 8
            one, two = columns[k], columns[k + 1]
            corner = pick(one[b], row)
            side = pick(one[b], row + 1)
            other = pick(two[b], row + 1)
            scale_one = lax.rsqrt(corner)
            scale_two = (corner * scale_one) * lax.rsqrt(corner * other - side * side)
            side = side * scale_one
            one = {c: one[c] * scale_one for c in one}
            two = {c: (two[c] - side * one[c]) * scale_two for c in two}
            for i in range(k + 2, 8 * chunk):
                c, place = start + i // 8, i % 8
                lead_one, lead_two = pick(one[c], place), pick(two[c], place)
                for d in columns[i]:
                    columns[i][d] = columns[i][d] - lead_one * one[d] - lead_two * two[d]
            below_one = dict(one)
            below_two = dict(two)
            below_one[b] = jnp.where(sub > row, one[b], 0.0)
            below_two[b] = jnp.where(sub > row + 1, two[b], 0.0)
            for number, band in enumerate(bands):
                if number == 0 and last_half:
                    continue
                done_one = pick(band[b], row) * scale_one
                done_two = (pick(band[b], row + 1) - side * done_one) * scale_two
                for c in range(b, count):
                    band[c] = band[c] - below_one[c] * done_one - below_two[c] * done_two
                if number > 0:
                    band[b] = jnp.where(
                        sub == row, done_one, jnp.where(sub == row + 1, done_two, band[b])
                    )
    scale = lax.rsqrt(shift)
    return [jnp.concatenate([part * scale for part in band], axis=0) for band in bands[1:]]


def finish_kernel(half, width, rows_total, *refs):
    core_ref, column_ref = refs[:2]
    core_refs = refs[2 : half + 1]
    (
        row_high_ref,
        row_low_ref,
        right_gram_ref,
        sketch_right_ref,
        left_ref,
        right_ref,
        sketch_ref,
        even_ref,
        odd_ref,
        keep_lane_ref,
        out_left_hbm,
        out_right_hbm,
        out_left_ref,
        out_right_ref,
        sems,
    ) = refs[half + 1 :]
    my_row, my_col = lax.axis_index("row"), lax.axis_index("col")
    lines, order = left_ref.shape
    tiles = lines // width
    piece = odd_ref.shape[2]
    count = 2 * half
    same = same_tile(lines, width)

    def diagonal(value):
        return jnp.where(same, value, 0.0)

    def stacked(value):
        return diagonal(jnp.concatenate([value] * tiles, axis=0))

    def blocks(value):
        return jnp.concatenate([stacked(value[:, :lines]), stacked(value[:, lines:])], axis=1)

    def column_piece(relative):
        step, side = divmod(relative, 2)
        if step == 0:
            return column_ref[side * width : (side + 1) * width]
        return core_refs[step - 1][(1 + side) * width : (2 + side) * width]

    keep_lane = keep_lane_ref[:1] > 0.0
    lane_row = lax.broadcasted_iota(jnp.int32, (1, lines), 1)
    live_line = jnp.zeros((1, lines), jnp.bool_)
    for tile in range(tiles):
        low = tile * width
        live = (tile * rows_total + my_row) > my_col
        live_line |= (lane_row >= low) & (lane_row < low + jnp.where(live, width, 0))

    columns = jnp.concatenate([column_piece(k) for k in range(count)], axis=1)
    sketch_column = nt(pieces_wide(sketch_ref, count, piece), columns)
    row_parts = (row_high_ref[...], row_low_ref[...])

    core = core_ref[...]
    for ref in core_refs:
        core = core + from_halves(ref[:width])
    core_split = split(core)
    core_blocks = stacked(core)
    core_block_split = split(core_blocks)

    first = jnp.concatenate([sketch_right_ref[...], -dot_split(nn, sketch_column, core_split)], axis=1)
    ones = jnp.where(same, 1.0, 0.0).astype(BF16)

    def traced(one, two):
        both = jnp.sum(one * two, axis=0, keepdims=True)
        both = both[:, :lines] + both[:, lines:]
        high, low = split(jnp.broadcast_to(both, (8, lines)))
        return (nn(high, ones) + nn(low, ones)) * (shift_rate / width) + tiny_shift

    image = dot_split(nn, first, row_parts)
    shift = traced(first, image)
    gram = dot_split(nt, first, split(blocks(image)))
    tall = jnp.concatenate([pieces_wide(right_ref, count, piece), columns], axis=0)
    column_wide = nt(columns, tall)
    column_right = jnp.where(keep_lane, column_wide[:, :lines], 0.0)
    core_lines = core.T
    cross = -diagonal(dot_split(nn, core_lines, split(column_right)))
    inner = dot_split(nn, column_wide[:, lines:], core_split)
    corner = diagonal(dot_split(nn, core_lines, split(inner)))
    middle = jnp.concatenate(
        [
            jnp.concatenate([right_gram_ref[...], cross.T], axis=1),
            jnp.concatenate([cross, corner], axis=1),
        ],
        axis=0,
    )
    middle_parts = split(middle)
    beyond_parts = split(dot_split(nn, middle, row_parts))
    top, bottom = factor_and_apply(gram, shift, [image[:, :lines], image[:, lines:]])
    basis = jnp.concatenate([top, bottom], axis=1)

    second = dot_split(nn, basis, middle_parts)
    image = dot_split(nn, basis, beyond_parts)
    shift = traced(second, image)
    gram = dot_split(nt, second, split(blocks(image)))
    back = -dot_split(nt, image[:, lines:], core_block_split)
    left_top, left_bottom, right_top, right_bottom = factor_and_apply(
        gram, shift, [second[:, :lines], second[:, lines:], image[:, :lines], back]
    )
    factor_size = factor_scale * math.sqrt(order)
    live_scale = jnp.where(live_line, factor_size, 0.0)
    live_back = jnp.where(live_line, 1.0 / factor_size, 0.0)
    left_small = jnp.concatenate(
        [stacked(left_top * live_scale), stacked(left_bottom * live_scale)], axis=1
    ).astype(BF16)
    right_small = jnp.concatenate(
        [
            stacked(jnp.where(keep_lane, right_top * live_back, 0.0)),
            stacked(right_bottom * live_back),
        ],
        axis=1,
    ).astype(BF16)
    copies = []
    for relative in range(count):
        spot = piece_spot(relative, piece)
        rows = jnp.concatenate(
            [left_ref[:, spot], (odd_ref if relative & 1 else even_ref)[relative // 2]], axis=0
        )
        out_left_ref[relative] = nn(left_small, rows).astype(BF16)
        tall = jnp.concatenate([right_ref[:, spot]] + [column_piece(relative)] * tiles, axis=0)
        out_right_ref[relative] = nn(right_small, tall).astype(BF16)
        for side, (ref, hbm) in enumerate(
            ((out_left_ref, out_left_hbm), (out_right_ref, out_right_hbm))
        ):
            copy = pltpu.make_async_copy(ref.at[relative], hbm.at[:, spot], sems.at[relative, side])
            copy.start()
            copies.append(copy)
    for copy in copies:
        copy.wait()


def finish(core, column, cores, others, rows_total, width):
    half = len(cores) + 1
    left, panel = others[4], others[7]
    lines, piece = panel.shape[1:]
    shape = jax.ShapeDtypeStruct(left.shape, BF16)
    operands = (core, column, *cores, *others)
    return pl.pallas_call(
        functools.partial(finish_kernel, half, width, rows_total),
        in_specs=in_vmem(len(operands)),
        out_specs=[pl.BlockSpec(memory_space=pltpu.HBM)] * 2,
        out_shape=[shape, shape],
        scratch_shapes=[
            VMEM((2 * half, lines, piece), BF16),
            VMEM((2 * half, lines, piece), BF16),
            pltpu.SemaphoreType.DMA((2 * half, 2)),
        ],
        name="finish",
        compiler_params=grant(16),
        cost_estimate=small_cost(5000000, 10**9),
    )(*operands)


def flat_lines(block):
    return jnp.swapaxes(block, -1, -2).reshape(-1, block.shape[-2])


def fast_shards(
    slab_left, slab_right, slab_ranks, panel_left, panel_right, panel_ranks, inverse_factor, sketch
):
    rows_total = lax.axis_size("row")
    cols_total = lax.axis_size("col")
    width = panel_left.shape[-1]
    half = cols_total // 2
    left, right = flat_lines(slab_left), flat_lines(slab_right)
    panel, solve_right = flat_lines(panel_left), flat_lines(panel_right)
    sketch_lines = flat_lines(sketch)
    head = width * (cols_total // rows_total)

    def swap(block, step):
        return lax.ppermute(block, "col", [(i, i ^ step) for i in range(cols_total)])

    def turn(block, shift):
        pairs = [(i, i ^ shift) for i in range(rows_total)]
        return lax.ppermute(block, "row", pairs)

    def across(blocks):
        return [swap(block, 2 * (step + 1)) for step, block in enumerate(blocks)]

    def along(block):
        return [turn(block, shift) for shift in range(1, rows_total)]

    panel_keep, _ = line_mask(panel.shape[0], panel_ranks)
    slab_line, slab_lane = line_mask(panel.shape[0], slab_ranks.reshape(-1))
    solve_right = pltpu.with_memory_space_constraint(solve_right, pltpu.HBM)
    inverse_factor = pltpu.with_memory_space_constraint(inverse_factor, pltpu.HBM)
    odd = solve_part(solve_right, inverse_factor, 1, half)
    other = swap(odd, 1)
    even = solve_part(solve_right, inverse_factor, 0, half)
    kept, *sends = pair_add(even, other)
    received = across(sends)
    solved, solved_head = gather_add(kept, panel, panel_keep, received, head)
    solved_others = along(solved_head)
    even_panel = bundle([panel] + across([panel] * (half - 1)))
    odd_panel = swap(even_panel, 1)
    gram_parts = grams(
        left, right, sketch_lines, even_panel, odd_panel, slab_line, slab_lane, width
    )
    core_even, even_column, odd_message = core_parts(
        solved, panel, solved_others, rows_total, cols_total, width
    )
    other = swap(odd_message, 1)
    core, column, *sends = core_add(core_even, even_column, other)
    cores = across(sends)
    fresh_left, fresh_right = finish(
        core,
        column,
        cores,
        (*gram_parts, left, right, sketch_lines, even_panel, odd_panel, slab_lane),
        rows_total,
        width,
    )

    def placed(block):
        tiles = slab_left.shape[:2] + (width, slab_left.shape[2])
        return jnp.swapaxes(block.reshape(tiles), -1, -2)

    return placed(fresh_left), placed(fresh_right)


def fast_fits(rows_total, cols_total, tile_rows, piece_rows, width, column_tiles):
    return (
        column_tiles == 1
        and tile_rows * width == LANES
        and width % 8 == 0
        and piece_rows % LANES == 0
        and cols_total & (cols_total - 1) == 0
        and cols_total >= 4
        and rows_total & (rows_total - 1) == 0
        and cols_total % rows_total == 0
        and rows_total > 1
        and cols_total <= tile_rows * rows_total
    )


def shards(*args):
    tile_rows, piece_rows, width = args[3].shape
    rows_total, cols_total = lax.axis_size("row"), lax.axis_size("col")
    fits = fast_fits(rows_total, cols_total, tile_rows, piece_rows, width, args[0].shape[1])
    return fast_shards(*args) if fits else plain_shards(*args)


def solution(mesh):
    placed = (
        P("row", "col", None, None),
        P("row", "col", None, None),
        P("row", "col"),
        P("row", "col", None),
        P("row", "col", None),
        P("row"),
        P(None, "col"),
        P(),
    )
    return jax.shard_map(
        shards,
        mesh=mesh,
        in_specs=placed,
        out_specs=(P("row", "col", None, None), P("row", "col", None, None)),
        check_vma=False,
    )
```

```python
import functools
import math

import jax
import jax.numpy as jnp
from jax import lax
from jax.experimental import pallas as pl
from jax.experimental.pallas import tpu as pltpu
from jax.sharding import PartitionSpec as P


highest = lax.Precision.HIGHEST
stacked_precision = lax.Precision.HIGH
shift_rate = 0.01
tiny_shift = 1e-06
factor_scale = 0.5
LANES = 128
F32 = jnp.float32
BF16 = jnp.bfloat16
VMEM = pltpu.VMEM
PAIR_TYPE = BF16
CROSSED = 1


def spread(block, axis, owner):
    block = jnp.where(lax.axis_index(axis) == owner, block, jnp.zeros_like(block))
    return lax.psum(block, axis)


def product(first_matrix, second_matrix):
    return jnp.matmul(first_matrix, second_matrix, precision=highest)


def stacked_product(first_matrix, second_matrix):
    return jnp.matmul(first_matrix, second_matrix, precision=stacked_precision)


def flipped(matrix):
    return jnp.swapaxes(matrix, -1, -2)


def orthonormal(vectors):
    gram_matrix = product(flipped(vectors), vectors)
    shift_value = (
        shift_rate * jnp.trace(gram_matrix, axis1=-2, axis2=-1) / gram_matrix.shape[-1] + tiny_shift
    )
    identity = jnp.eye(gram_matrix.shape[-1], dtype=gram_matrix.dtype)
    lower_factor = jnp.linalg.cholesky(gram_matrix + shift_value[..., None, None] * identity)
    solved_rows = lax.linalg.triangular_solve(
        lower_factor, flipped(vectors), left_side=True, lower=True
    )
    return flipped(solved_rows)


def recompress(slab_factor, masked_right, row_factor, core_block, column_factor, sketch_float):
    target_shape = core_block.shape[:2] + slab_factor.shape[2:]
    column_wide = jnp.broadcast_to(column_factor[None], target_shape)
    row_core = product(row_factor, core_block)
    column_core = product(column_wide, flipped(core_block))
    forward_left = jnp.concatenate([slab_factor.astype(jnp.float32), -row_core], axis=-1)
    forward_right = jnp.concatenate([masked_right.astype(jnp.float32), column_wide], axis=-1)
    backward_left = jnp.concatenate([masked_right.astype(jnp.float32), -column_core], axis=-1)
    backward_right = jnp.concatenate([slab_factor.astype(jnp.float32), row_factor], axis=-1)

    def forward(vectors):
        return stacked_product(forward_left, stacked_product(flipped(forward_right), vectors))

    def backward(vectors):
        return stacked_product(backward_left, stacked_product(flipped(backward_right), vectors))

    basis_now = orthonormal(forward(sketch_float))
    basis_now = orthonormal(forward(backward(basis_now)))
    projected = backward(basis_now)
    factor_size = factor_scale * math.sqrt(slab_factor.shape[-2])
    return (basis_now * factor_size, projected / factor_size)


def plain_shards(
    slab_left, slab_right, slab_ranks, panel_left, panel_right, panel_ranks, inverse_factor, sketch
):
    rows_total = lax.axis_size("row")
    cols_total = lax.axis_size("col")
    my_row = lax.axis_index("row")
    my_col = lax.axis_index("col")
    tile_rows, piece_rows, rank_width = panel_left.shape
    column_tiles = slab_left.shape[1]
    tile_order = inverse_factor.shape[0]
    panel_keep = jnp.arange(rank_width, dtype=jnp.int32)[None, :] < panel_ranks[:, None]
    masked_panel = jnp.where(panel_keep[:, None, :], panel_right, jnp.zeros((), jnp.bfloat16))
    flat_right = jnp.swapaxes(masked_panel, 0, 1).reshape(piece_rows, tile_rows * rank_width)
    flat_left = jnp.swapaxes(panel_left, 0, 1).reshape(piece_rows, tile_rows * rank_width)
    solved_part = lax.psum_scatter(
        jnp.dot(inverse_factor, flat_right, preferred_element_type=jnp.float32),
        "col",
        scatter_dimension=0,
        tiled=True,
    ).astype(jnp.bfloat16)
    full_left, full_solved = (
        lax.all_gather(flat_left, "col", axis=0, tiled=True),
        lax.all_gather(solved_part, "col", axis=0, tiled=True),
    )
    full_left = full_left.reshape(tile_order, tile_rows, rank_width)
    full_solved = full_solved.reshape(tile_order, tile_rows, rank_width)
    first_pick = my_col // rows_total
    position = first_pick + 0
    picked_left = lax.dynamic_slice_in_dim(full_left, position, 1, 1)
    picked_solved = lax.dynamic_slice_in_dim(full_solved, position, 1, 1)
    send_left = picked_left.reshape(tile_order, column_tiles * rank_width)
    send_solved = picked_solved.reshape(tile_order, column_tiles * rank_width)
    root_row = my_col % rows_total
    column_left, column_solved = (
        spread(send_left, "row", root_row),
        spread(send_solved, "row", root_row),
    )
    row_factor = jnp.swapaxes(full_left, 0, 1)[:, None]
    row_solved = jnp.swapaxes(full_solved, 0, 1)
    column_factor = jnp.swapaxes(column_left.reshape(tile_order, column_tiles, rank_width), 0, 1)
    column_three = jnp.swapaxes(column_solved.reshape(tile_order, column_tiles, rank_width), 0, 1)
    core_block = jnp.einsum(
        "tbr,sbq->tsrq", row_solved, column_three, preferred_element_type=jnp.float32
    )
    slab_keep = jnp.arange(rank_width, dtype=jnp.int32) < slab_ranks[..., None]
    masked_right = jnp.where(slab_keep[:, :, None, :], slab_right, jnp.zeros((), jnp.bfloat16))
    fresh_left, fresh_right = recompress(
        slab_left, masked_right, row_factor, core_block, column_factor, sketch.astype(jnp.float32)
    )
    row_ids = jnp.arange(tile_rows, dtype=jnp.int32) * rows_total + my_row
    col_ids = jnp.arange(column_tiles, dtype=jnp.int32) * cols_total + my_col
    live_tile = (row_ids[:, None] > col_ids[None, :])[:, :, None, None]
    return (
        jnp.where(live_tile, fresh_left, 0.0).astype(jnp.bfloat16),
        jnp.where(live_tile, fresh_right, 0.0).astype(jnp.bfloat16),
    )


def partner(step):
    return 2 * step + CROSSED * min(step, 1)


def nt(first, second):
    return lax.dot_general(first, second, (((1,), (1,)), ((), ())), preferred_element_type=F32)


def nn(first, second):
    return lax.dot_general(first, second, (((1,), (0,)), ((), ())), preferred_element_type=F32)


def split(value):
    high = value.astype(BF16)
    return high, (value - high.astype(F32)).astype(BF16)


def wide(value):
    return jnp.concatenate(split(value), axis=0)


def fold(value):
    half = value.shape[0] // 2
    return value[:half] + value[half:]


def dot_split(op, first, second_parts):
    stacked = wide(first)
    return fold(op(stacked, second_parts[0]) + op(stacked, second_parts[1]))


def grant(mebibytes):
    return pltpu.CompilerParams(vmem_limit_bytes=mebibytes << 20)


def line_mask(tile_lines, ranks):
    width = tile_lines // ranks.shape[0]
    keep = (jnp.arange(width, dtype=jnp.int32)[None, :] < ranks[:, None]).astype(F32).reshape(-1)
    return (
        jnp.broadcast_to(keep[:, None], (tile_lines, LANES)),
        jnp.broadcast_to(keep[None, :], (8, tile_lines)),
    )


def in_vmem(count):
    return [pl.BlockSpec(memory_space=VMEM)] * count


def small_cost(bytes_accessed, flops=0):
    return pl.CostEstimate(flops=flops, bytes_accessed=bytes_accessed, transcendentals=0)


def solve_step(block, my_col, right_ref, inverse, out_ref, step, copy=None):
    @pl.when(block >= my_col)
    def _():
        if copy is not None:
            copy.wait()
        out_ref[step] = nt(right_ref[...], inverse[step]).astype(out_ref.dtype)

    @pl.when(block < my_col)
    def _():
        out_ref[step] = jnp.zeros(out_ref.shape[1:], out_ref.dtype)


def solve_odd_kernel(
    right_hbm, inverse_hbm, out_ref, right_ref, even_ref, inverse_ref, odd_sems, even_sems
):
    parts = out_ref.shape[0]
    piece = right_ref.shape[1]
    my_col = lax.axis_index("col")
    right_copy = pltpu.make_async_copy(right_hbm, right_ref, odd_sems.at[parts])
    right_copy.start()
    copies = []
    for odd, target, sems in ((1, inverse_ref, odd_sems), (0, even_ref, even_sems)):
        for step in range(parts):
            block = my_col ^ (partner(step) ^ odd)
            rows = pl.ds(pl.multiple_of(block * piece, piece), piece)
            copy = pltpu.make_async_copy(inverse_hbm.at[rows], target.at[step], sems.at[step])
            pl.when(block >= my_col)(copy.start)
            copies.append((block, copy))
    right_copy.wait()
    for step in range(parts):
        block, copy = copies[step]
        solve_step(block, my_col, right_ref, inverse_ref, out_ref, step, copy)
    for block, copy in copies[parts:]:
        pl.when(block >= my_col)(copy.wait)


def solve_odd(right, inverse, parts):
    lines, piece = right.shape
    return pl.pallas_call(
        solve_odd_kernel,
        in_specs=[pl.BlockSpec(memory_space=pltpu.HBM)] * 2,
        out_specs=in_vmem(3),
        out_shape=[
            jax.ShapeDtypeStruct((parts, lines, piece), PAIR_TYPE),
            jax.ShapeDtypeStruct((lines, piece), BF16),
            jax.ShapeDtypeStruct((parts, piece, piece), BF16),
        ],
        scratch_shapes=[
            VMEM((parts, piece, piece), BF16),
            pltpu.SemaphoreType.DMA((parts + 1,)),
            pltpu.SemaphoreType.DMA((parts,)),
        ],
        name="solve_odd",
        compiler_params=grant(4),
        cost_estimate=small_cost(
            4 * parts * piece * piece + 4 * parts * lines * piece,
            2 * parts * lines * piece * piece,
        ),
    )(right, inverse)


def solve_even_kernel(right_ref, even_ref, out_ref):
    my_col = lax.axis_index("col")
    for step in range(out_ref.shape[0]):
        solve_step(my_col ^ partner(step), my_col, right_ref, even_ref, out_ref, step)


def solve_even(right, even):
    lines, piece = right.shape
    parts = even.shape[0]
    return pl.pallas_call(
        solve_even_kernel,
        in_specs=in_vmem(2),
        out_specs=pl.BlockSpec(memory_space=VMEM),
        out_shape=jax.ShapeDtypeStruct((parts, lines, piece), F32),
        name="solve_even",
        compiler_params=grant(4),
        cost_estimate=small_cost(
            2 * parts * piece * piece + 4 * parts * lines * piece,
            2 * parts * lines * piece * piece,
        ),
    )(right, even)


def pair_add_kernel(mine_ref, other_ref, keep_ref, *send_refs):
    keep_ref[...] = mine_ref[0] + other_ref[0].astype(F32)
    for step, ref in enumerate(send_refs):
        ref[...] = (mine_ref[step + 1] + other_ref[step + 1].astype(F32)).astype(ref.dtype)


def pair_add(mine, other, send_type):
    parts, lines, piece = mine.shape
    return pl.pallas_call(
        pair_add_kernel,
        in_specs=in_vmem(2),
        out_specs=in_vmem(parts),
        out_shape=[jax.ShapeDtypeStruct((lines, piece), F32)]
        + [jax.ShapeDtypeStruct((lines, piece), send_type)] * (parts - 1),
        name="pair_add",
        compiler_params=grant(4),
        cost_estimate=small_cost(3 * mine.size * 4),
    )(mine, other)


def gather_add_kernel(head, first_ref, mask_ref, *refs):
    *others, solved_ref, head_ref = refs
    total = first_ref[...]
    for ref in others:
        total = total + ref[...].astype(F32)
    keep = jnp.concatenate([mask_ref[...]] * (total.shape[1] // LANES), axis=1)
    rounded = jnp.where(keep > 0.0, total, 0.0).astype(BF16)
    solved_ref[...] = rounded
    head_ref[...] = rounded[:head]


def gather_add(first, mask, others, head):
    return pl.pallas_call(
        functools.partial(gather_add_kernel, head),
        in_specs=in_vmem(2 + len(others)),
        out_specs=in_vmem(2),
        out_shape=[
            jax.ShapeDtypeStruct(first.shape, BF16),
            jax.ShapeDtypeStruct((head, first.shape[1]), BF16),
        ],
        name="gather_add",
        compiler_params=grant(4),
        cost_estimate=small_cost(first.size * 10),
    )(first, mask, *others)


def column_tiles(rows_total, cols_total, width, own_ref, others):
    my_row = lax.axis_index("row")
    for shift in range(rows_total):
        source = own_ref if shift == 0 else others[shift - 1]
        for index in range(cols_total // rows_total):
            lines = source[index * width : (index + 1) * width, :]
            yield index * rows_total + (my_row ^ shift), lines


def message_kernel(rows_total, cols_total, width, own_ref, *refs):
    others = refs[: rows_total - 1]
    *message_refs, stage = refs[rows_total - 1 :]
    my_col = lax.axis_index("col")
    lines = own_ref.shape[0]
    for tile, value in column_tiles(rows_total, cols_total, width, own_ref, others):
        stage[tile] = value
    for step, ref in enumerate(message_refs):
        target = my_col ^ partner(step)
        ref[:width] = stage[target]
        ref[width : width + lines] = own_ref[...]
        ref[width + lines :] = stage[target ^ 1]


def messages(own, others, rows_total, cols_total, width):
    lines, piece = own.shape
    half = cols_total // 2
    return pl.pallas_call(
        functools.partial(message_kernel, rows_total, cols_total, width),
        in_specs=in_vmem(rows_total),
        out_specs=in_vmem(half),
        out_shape=[jax.ShapeDtypeStruct((lines + 2 * width, piece), BF16)] * half,
        scratch_shapes=[VMEM((cols_total, width, piece), BF16)],
        name="messages",
        compiler_params=grant(4),
        cost_estimate=small_cost(half * (lines + 2 * width) * piece * 4),
    )(own, *others)


def bundle_kernel(width, *refs):
    *pieces, here_ref, there_ref = refs
    for step, ref in enumerate(pieces):
        here_ref[step] = ref[: here_ref.shape[1]]
        there_ref[step] = ref[width:]


def bundle(pieces, width):
    count = len(pieces)
    lines, piece = pieces[0].shape
    shape = jax.ShapeDtypeStruct((count, lines - width, piece), BF16)
    return pl.pallas_call(
        functools.partial(bundle_kernel, width),
        in_specs=in_vmem(count),
        out_specs=in_vmem(2),
        out_shape=[shape, shape],
        name="bundle",
        compiler_params=grant(4),
        cost_estimate=small_cost(count * pieces[0].size * 6),
    )(*pieces)


def core_kernel(rows_total, cols_total, width, own_ref, *refs):
    others = refs[: rows_total - 1]
    even_ref, odd_ref, stage = refs[rows_total - 1 :]
    my_col = lax.axis_index("col")
    half = cols_total // 2
    for tile, value in column_tiles(rows_total, cols_total, width, own_ref, others):
        relative = my_col ^ tile
        step = lax.shift_right_logical(relative, 1)
        given = (relative & 1) ^ (jnp.minimum(step, 1) * CROSSED)
        stage[given * half + step] = value
    piece = own_ref.shape[1]
    own = own_ref[...]
    odd_ref[...] = nt(stage[half:].reshape(half * width, piece), own).reshape(odd_ref.shape)
    even_ref[...] = nt(stage[:half].reshape(half * width, piece), own).reshape(even_ref.shape)


def core_parts(own, others, rows_total, cols_total, width):
    lines, piece = own.shape
    half = cols_total // 2
    shape = jax.ShapeDtypeStruct((half, width, lines), F32)
    return pl.pallas_call(
        functools.partial(core_kernel, rows_total, cols_total, width),
        in_specs=in_vmem(rows_total),
        out_specs=in_vmem(2),
        out_shape=[shape, shape],
        scratch_shapes=[VMEM((cols_total, width, piece), BF16)],
        name="core_parts",
        compiler_params=grant(4),
        cost_estimate=small_cost(400000, 2 * lines * piece * cols_total * width),
    )(own, *others)


def piece_spot(relative, piece):
    block = lax.axis_index("col") ^ relative
    return pl.ds(pl.multiple_of(block * piece, LANES), piece)


def pieces_wide(ref, count, piece):
    return jnp.concatenate([ref[:, piece_spot(k, piece)] for k in range(count)], axis=1)


def same_tile(lines, width):
    lane = lax.broadcasted_iota(jnp.int32, (lines, lines), 1)
    line = lax.broadcasted_iota(jnp.int32, (lines, lines), 0)
    return (lane // width) == (line // width)


def panel_piece(even_ref, odd_ref, relative, width):
    step = relative // 2
    if relative != partner(step):
        lines = odd_ref.shape[1] - width
        return odd_ref[step, :lines], odd_ref[step, lines:]
    return even_ref[step, width:], even_ref[step, :width]


def panel_wide(even_ref, odd_ref, width):
    parts = [panel_piece(even_ref, odd_ref, k, width) for k in range(2 * even_ref.shape[0])]
    return [jnp.concatenate(side, axis=1) for side in zip(*parts)]


def gram_kernel(width, *refs):
    left_ref, right_ref, sketch_ref, even_ref, odd_ref, keep_line_ref, keep_lane_ref = refs[:7]
    (
        row_high_ref,
        row_low_ref,
        right_gram_ref,
        sketch_right_ref,
        column_right_ref,
        column_column_ref,
        sketch_column_ref,
    ) = refs[7:]
    lines = left_ref.shape[0]
    piece = even_ref.shape[2]
    count = 2 * even_ref.shape[0]
    same = same_tile(lines, width)
    panel, column = panel_wide(even_ref, odd_ref, width)
    left = pieces_wide(left_ref, count, piece)
    for i, one in enumerate((left, panel)):
        for j, two in enumerate((left, panel)):
            high, low = split(jnp.where(same, nt(one, two), 0.0))
            row_high_ref[i * lines : (i + 1) * lines, j * lines : (j + 1) * lines] = high
            row_low_ref[i * lines : (i + 1) * lines, j * lines : (j + 1) * lines] = low
    right = pieces_wide(right_ref, count, piece)
    sketch = pieces_wide(sketch_ref, count, piece)
    keep_line = keep_line_ref[...] > 0.0
    keep_lane = keep_lane_ref[:1] > 0.0
    right_gram_ref[...] = jnp.where(same & keep_line & keep_lane, nt(right, right), 0.0)
    sketch_right_ref[...] = jnp.where(keep_lane, nt(sketch, right), 0.0)
    column_right_ref[...] = jnp.where(keep_lane, nt(column, right), 0.0)
    column_column_ref[...] = nt(column, column)
    sketch_column_ref[...] = nt(sketch, column)


def grams(left, right, sketch, even, odd, keep_line, keep_lane, width):
    lines, order = left.shape
    square = jax.ShapeDtypeStruct((2 * lines, 2 * lines), BF16)
    flat = jax.ShapeDtypeStruct((width, lines), F32)
    small = jax.ShapeDtypeStruct((width, width), F32)
    return pl.pallas_call(
        functools.partial(gram_kernel, width),
        in_specs=in_vmem(7),
        out_specs=in_vmem(7),
        out_shape=[
            square,
            square,
            jax.ShapeDtypeStruct((lines, lines), F32),
            flat,
            flat,
            small,
            small,
        ],
        name="grams",
        compiler_params=grant(16),
        cost_estimate=small_cost(2000000, 2 * order * lines * lines * 8),
    )(left, right, sketch, even, odd, keep_line, keep_lane)


def factor_and_apply(gram, shift, bands):
    width = gram.shape[0]
    count = width // 8
    chunk = count // 2
    lanes = lax.broadcasted_iota(jnp.int32, (8, LANES), 1)
    inner_lane = lax.rem(lanes, width)
    group = lanes - inner_lane
    sub = lax.broadcasted_iota(jnp.int32, (8, LANES), 0)
    inverse_shift = 1.0 / shift
    matrix = [
        gram[8 * b : 8 * b + 8] * inverse_shift + jnp.where(inner_lane == sub + 8 * b, 1.0, 0.0)
        for b in range(count)
    ]
    bands = [matrix] + [[band[8 * b : 8 * b + 8] for b in range(count)] for band in bands]

    def pick(vector, row):
        return vector[row : row + 1]

    for start in range(0, count, chunk):
        first_column = 8 * start
        columns = [
            {
                b: jnp.take_along_axis(matrix[b], group + first_column + k, axis=1)
                for b in range(start + k // 8, count)
            }
            for k in range(8 * chunk)
        ]
        last_half = start + chunk == count
        for k in range(0, 8 * chunk, 2):
            b, row = start + k // 8, k % 8
            one, two = columns[k], columns[k + 1]
            corner = pick(one[b], row)
            side = pick(one[b], row + 1)
            other = pick(two[b], row + 1)
            scale_one = lax.rsqrt(corner)
            scale_two = (corner * scale_one) * lax.rsqrt(corner * other - side * side)
            side = side * scale_one
            one = {c: one[c] * scale_one for c in one}
            two = {c: (two[c] - side * one[c]) * scale_two for c in two}
            for i in range(k + 2, 8 * chunk):
                c, place = start + i // 8, i % 8
                lead_one, lead_two = pick(one[c], place), pick(two[c], place)
                for d in columns[i]:
                    columns[i][d] = columns[i][d] - lead_one * one[d] - lead_two * two[d]
            below_one = dict(one)
            below_two = dict(two)
            below_one[b] = jnp.where(sub > row, one[b], 0.0)
            below_two[b] = jnp.where(sub > row + 1, two[b], 0.0)
            for number, band in enumerate(bands):
                if number == 0 and last_half:
                    continue
                done_one = pick(band[b], row) * scale_one
                done_two = (pick(band[b], row + 1) - side * done_one) * scale_two
                for c in range(b, count):
                    band[c] = band[c] - below_one[c] * done_one - below_two[c] * done_two
                if number > 0:
                    band[b] = jnp.where(
                        sub == row, done_one, jnp.where(sub == row + 1, done_two, band[b])
                    )
    scale = lax.rsqrt(shift)
    return [jnp.concatenate([part * scale for part in band], axis=0) for band in bands[1:]]


def finish_kernel(half, width, rows_total, *refs):
    core_refs = refs[:half]
    (
        row_high_ref,
        row_low_ref,
        right_gram_ref,
        sketch_right_ref,
        column_right_ref,
        column_column_ref,
        sketch_column_ref,
        left_ref,
        right_ref,
        even_ref,
        odd_ref,
        keep_lane_ref,
        out_left_hbm,
        out_right_hbm,
        out_left_ref,
        out_right_ref,
        sems,
    ) = refs[half:]
    my_row, my_col = lax.axis_index("row"), lax.axis_index("col")
    lines, order = left_ref.shape
    tiles = lines // width
    piece = odd_ref.shape[2]
    count = 2 * half
    same = same_tile(lines, width)

    def diagonal(value):
        return jnp.where(same, value, 0.0)

    def stacked(value):
        return diagonal(jnp.concatenate([value] * tiles, axis=0))

    def blocks(value):
        return jnp.concatenate([stacked(value[:, :lines]), stacked(value[:, lines:])], axis=1)

    keep_lane = keep_lane_ref[:1] > 0.0
    lane_row = lax.broadcasted_iota(jnp.int32, (1, lines), 1)
    live_line = jnp.zeros((1, lines), jnp.bool_)
    for tile in range(tiles):
        low = tile * width
        live = (tile * rows_total + my_row) > my_col
        live_line |= (lane_row >= low) & (lane_row < low + jnp.where(live, width, 0))

    row_parts = (row_high_ref[...], row_low_ref[...])
    core = core_refs[0][...]
    for ref in core_refs[1:]:
        core = core + ref[...]
    core_split = split(core)
    core_blocks = stacked(core)
    core_block_split = split(core_blocks)

    first = jnp.concatenate([sketch_right_ref[...], -dot_split(nn, sketch_column_ref[...], core_split)], axis=1)
    ones = jnp.where(same, 1.0, 0.0).astype(BF16)

    def traced(one, two):
        both = jnp.sum(one * two, axis=0, keepdims=True)
        both = both[:, :lines] + both[:, lines:]
        high, low = split(jnp.broadcast_to(both, (8, lines)))
        return (nn(high, ones) + nn(low, ones)) * (shift_rate / width) + tiny_shift

    image = dot_split(nn, first, row_parts)
    shift = traced(first, image)
    gram = dot_split(nt, first, split(blocks(image)))
    core_lines = core.T
    cross = -diagonal(dot_split(nn, core_lines, split(column_right_ref[...])))
    inner = dot_split(nn, column_column_ref[...], core_split)
    corner = diagonal(dot_split(nn, core_lines, split(inner)))
    middle = jnp.concatenate(
        [
            jnp.concatenate([right_gram_ref[...], cross.T], axis=1),
            jnp.concatenate([cross, corner], axis=1),
        ],
        axis=0,
    )
    middle_parts = split(middle)
    beyond_parts = split(dot_split(nn, middle, row_parts))
    top, bottom = factor_and_apply(gram, shift, [image[:, :lines], image[:, lines:]])
    basis = jnp.concatenate([top, bottom], axis=1)

    second = dot_split(nn, basis, middle_parts)
    image = dot_split(nn, basis, beyond_parts)
    shift = traced(second, image)
    gram = dot_split(nt, second, split(blocks(image)))
    back = -dot_split(nt, image[:, lines:], core_block_split)
    left_top, left_bottom, right_top, right_bottom = factor_and_apply(
        gram, shift, [second[:, :lines], second[:, lines:], image[:, :lines], back]
    )
    factor_size = factor_scale * math.sqrt(order)
    live_scale = jnp.where(live_line, factor_size, 0.0)
    live_back = jnp.where(live_line, 1.0 / factor_size, 0.0)
    left_small = jnp.concatenate(
        [stacked(left_top * live_scale), stacked(left_bottom * live_scale)], axis=1
    ).astype(BF16)
    right_small = jnp.concatenate(
        [
            stacked(jnp.where(keep_lane, right_top * live_back, 0.0)),
            stacked(right_bottom * live_back),
        ],
        axis=1,
    ).astype(BF16)
    copies = []
    for relative in range(count):
        spot = piece_spot(relative, piece)
        panel, column = panel_piece(even_ref, odd_ref, relative, width)
        rows = jnp.concatenate([left_ref[:, spot], panel], axis=0)
        out_left_ref[relative] = nn(left_small, rows).astype(BF16)
        tall = jnp.concatenate([right_ref[:, spot]] + [column] * tiles, axis=0)
        out_right_ref[relative] = nn(right_small, tall).astype(BF16)
        for side, (ref, hbm) in enumerate(
            ((out_left_ref, out_left_hbm), (out_right_ref, out_right_hbm))
        ):
            copy = pltpu.make_async_copy(ref.at[relative], hbm.at[:, spot], sems.at[relative, side])
            copy.start()
            copies.append(copy)
    for copy in copies:
        copy.wait()


def finish(cores, others, rows_total, width):
    half = len(cores)
    left = others[7]
    lines, piece = left.shape[0], left.shape[1] // (2 * half)
    shape = jax.ShapeDtypeStruct(left.shape, BF16)
    operands = (*cores, *others)
    return pl.pallas_call(
        functools.partial(finish_kernel, half, width, rows_total),
        in_specs=in_vmem(len(operands)),
        out_specs=[pl.BlockSpec(memory_space=pltpu.HBM)] * 2,
        out_shape=[shape, shape],
        scratch_shapes=[
            VMEM((2 * half, lines, piece), BF16),
            VMEM((2 * half, lines, piece), BF16),
            pltpu.SemaphoreType.DMA((2 * half, 2)),
        ],
        name="finish",
        compiler_params=grant(16),
        cost_estimate=small_cost(5000000, 10**9),
    )(*operands)


def flat_lines(block):
    return jnp.swapaxes(block, -1, -2).reshape(-1, block.shape[-2])


def fast_shards(
    slab_left, slab_right, slab_ranks, panel_left, panel_right, panel_ranks, inverse_factor, sketch
):
    rows_total = lax.axis_size("row")
    cols_total = lax.axis_size("col")
    width = panel_left.shape[-1]
    half = cols_total // 2
    left, right = flat_lines(slab_left), flat_lines(slab_right)
    panel, solve_right = flat_lines(panel_left), flat_lines(panel_right)
    sketch_lines = flat_lines(sketch)
    head = width * (cols_total // rows_total)

    def swap(block, step):
        return lax.ppermute(block, "col", [(i, i ^ step) for i in range(cols_total)])

    def turn(block, shift):
        pairs = [(i, i ^ shift) for i in range(rows_total)]
        return lax.ppermute(block, "row", pairs)

    def across(blocks):
        return [swap(block, partner(step + 1)) for step, block in enumerate(blocks)]

    def along(block):
        return [turn(block, shift) for shift in range(1, rows_total)]

    panel_keep, _ = line_mask(panel.shape[0], panel_ranks)
    slab_line, slab_lane = line_mask(panel.shape[0], slab_ranks.reshape(-1))
    solve_right = pltpu.with_memory_space_constraint(solve_right, pltpu.HBM)
    inverse_factor = pltpu.with_memory_space_constraint(inverse_factor, pltpu.HBM)
    odd, right_panel, even_blocks = solve_odd(solve_right, inverse_factor, half)
    other = swap(odd, 1)
    even = solve_even(right_panel, even_blocks)
    kept, *sends = pair_add(even, other, BF16)
    received = across(sends)
    panel_others = along(panel[:head])
    solved, solved_head = gather_add(kept, panel_keep, received, head)
    solved_others = along(solved_head)
    own_message, *sends = messages(panel, panel_others, rows_total, cols_total, width)
    even_panel, odd_panel = bundle([own_message] + across(sends), width)
    odd_panel = swap(odd_panel, 1)
    gram_parts = grams(
        left, right, sketch_lines, even_panel, odd_panel, slab_line, slab_lane, width
    )
    core_even, core_odd = core_parts(solved, solved_others, rows_total, cols_total, width)
    kept, *sends = pair_add(core_even, swap(core_odd, 1), F32)
    fresh_left, fresh_right = finish(
        [kept] + across(sends),
        (*gram_parts, left, right, even_panel, odd_panel, slab_lane),
        rows_total,
        width,
    )

    def placed(block):
        tiles = slab_left.shape[:2] + (width, slab_left.shape[2])
        return jnp.swapaxes(block.reshape(tiles), -1, -2)

    return placed(fresh_left), placed(fresh_right)


def fast_fits(rows_total, cols_total, tile_rows, piece_rows, width, column_tiles):
    return (
        column_tiles == 1
        and tile_rows * width == LANES
        and width % 8 == 0
        and piece_rows % LANES == 0
        and cols_total & (cols_total - 1) == 0
        and cols_total >= 4
        and rows_total & (rows_total - 1) == 0
        and cols_total % rows_total == 0
        and rows_total > 1
        and cols_total <= tile_rows * rows_total
    )


def shards(*args):
    tile_rows, piece_rows, width = args[3].shape
    rows_total, cols_total = lax.axis_size("row"), lax.axis_size("col")
    fits = fast_fits(rows_total, cols_total, tile_rows, piece_rows, width, args[0].shape[1])
    return fast_shards(*args) if fits else plain_shards(*args)


def solution(mesh):
    placed = (
        P("row", "col", None, None),
        P("row", "col", None, None),
        P("row", "col"),
        P("row", "col", None),
        P("row", "col", None),
        P("row"),
        P(None, "col"),
        P(),
    )
    return jax.shard_map(
        shards,
        mesh=mesh,
        in_specs=placed,
        out_specs=(P("row", "col", None, None), P("row", "col", None, None)),
        check_vma=False,
    )
```

```python
import functools
import math

import jax
import jax.numpy as jnp
from jax import lax
from jax.experimental import pallas as pl
from jax.experimental.pallas import tpu as pltpu
from jax.sharding import PartitionSpec as P


highest = lax.Precision.HIGHEST
stacked_precision = lax.Precision.HIGH
shift_rate = 0.01
tiny_shift = 1e-06
factor_scale = 0.5
LANES = 128
F32 = jnp.float32
BF16 = jnp.bfloat16
VMEM = pltpu.VMEM
PAIR_TYPE = BF16
CROSSED = 1


def spread(block, axis, owner):
    block = jnp.where(lax.axis_index(axis) == owner, block, jnp.zeros_like(block))
    return lax.psum(block, axis)


def product(first_matrix, second_matrix):
    return jnp.matmul(first_matrix, second_matrix, precision=highest)


def stacked_product(first_matrix, second_matrix):
    return jnp.matmul(first_matrix, second_matrix, precision=stacked_precision)


def flipped(matrix):
    return jnp.swapaxes(matrix, -1, -2)


def orthonormal(vectors):
    gram_matrix = product(flipped(vectors), vectors)
    shift_value = (
        shift_rate * jnp.trace(gram_matrix, axis1=-2, axis2=-1) / gram_matrix.shape[-1] + tiny_shift
    )
    identity = jnp.eye(gram_matrix.shape[-1], dtype=gram_matrix.dtype)
    lower_factor = jnp.linalg.cholesky(gram_matrix + shift_value[..., None, None] * identity)
    solved_rows = lax.linalg.triangular_solve(
        lower_factor, flipped(vectors), left_side=True, lower=True
    )
    return flipped(solved_rows)


def recompress(slab_factor, masked_right, row_factor, core_block, column_factor, sketch_float):
    target_shape = core_block.shape[:2] + slab_factor.shape[2:]
    column_wide = jnp.broadcast_to(column_factor[None], target_shape)
    row_core = product(row_factor, core_block)
    column_core = product(column_wide, flipped(core_block))
    forward_left = jnp.concatenate([slab_factor.astype(jnp.float32), -row_core], axis=-1)
    forward_right = jnp.concatenate([masked_right.astype(jnp.float32), column_wide], axis=-1)
    backward_left = jnp.concatenate([masked_right.astype(jnp.float32), -column_core], axis=-1)
    backward_right = jnp.concatenate([slab_factor.astype(jnp.float32), row_factor], axis=-1)

    def forward(vectors):
        return stacked_product(forward_left, stacked_product(flipped(forward_right), vectors))

    def backward(vectors):
        return stacked_product(backward_left, stacked_product(flipped(backward_right), vectors))

    basis_now = orthonormal(forward(sketch_float))
    basis_now = orthonormal(forward(backward(basis_now)))
    projected = backward(basis_now)
    factor_size = factor_scale * math.sqrt(slab_factor.shape[-2])
    return (basis_now * factor_size, projected / factor_size)


def plain_shards(
    slab_left, slab_right, slab_ranks, panel_left, panel_right, panel_ranks, inverse_factor, sketch
):
    rows_total = lax.axis_size("row")
    cols_total = lax.axis_size("col")
    my_row = lax.axis_index("row")
    my_col = lax.axis_index("col")
    tile_rows, piece_rows, rank_width = panel_left.shape
    column_tiles = slab_left.shape[1]
    tile_order = inverse_factor.shape[0]
    panel_keep = jnp.arange(rank_width, dtype=jnp.int32)[None, :] < panel_ranks[:, None]
    masked_panel = jnp.where(panel_keep[:, None, :], panel_right, jnp.zeros((), jnp.bfloat16))
    flat_right = jnp.swapaxes(masked_panel, 0, 1).reshape(piece_rows, tile_rows * rank_width)
    flat_left = jnp.swapaxes(panel_left, 0, 1).reshape(piece_rows, tile_rows * rank_width)
    solved_part = lax.psum_scatter(
        jnp.dot(inverse_factor, flat_right, preferred_element_type=jnp.float32),
        "col",
        scatter_dimension=0,
        tiled=True,
    ).astype(jnp.bfloat16)
    full_left, full_solved = (
        lax.all_gather(flat_left, "col", axis=0, tiled=True),
        lax.all_gather(solved_part, "col", axis=0, tiled=True),
    )
    full_left = full_left.reshape(tile_order, tile_rows, rank_width)
    full_solved = full_solved.reshape(tile_order, tile_rows, rank_width)
    first_pick = my_col // rows_total
    position = first_pick + 0
    picked_left = lax.dynamic_slice_in_dim(full_left, position, 1, 1)
    picked_solved = lax.dynamic_slice_in_dim(full_solved, position, 1, 1)
    send_left = picked_left.reshape(tile_order, column_tiles * rank_width)
    send_solved = picked_solved.reshape(tile_order, column_tiles * rank_width)
    root_row = my_col % rows_total
    column_left, column_solved = (
        spread(send_left, "row", root_row),
        spread(send_solved, "row", root_row),
    )
    row_factor = jnp.swapaxes(full_left, 0, 1)[:, None]
    row_solved = jnp.swapaxes(full_solved, 0, 1)
    column_factor = jnp.swapaxes(column_left.reshape(tile_order, column_tiles, rank_width), 0, 1)
    column_three = jnp.swapaxes(column_solved.reshape(tile_order, column_tiles, rank_width), 0, 1)
    core_block = jnp.einsum(
        "tbr,sbq->tsrq", row_solved, column_three, preferred_element_type=jnp.float32
    )
    slab_keep = jnp.arange(rank_width, dtype=jnp.int32) < slab_ranks[..., None]
    masked_right = jnp.where(slab_keep[:, :, None, :], slab_right, jnp.zeros((), jnp.bfloat16))
    fresh_left, fresh_right = recompress(
        slab_left, masked_right, row_factor, core_block, column_factor, sketch.astype(jnp.float32)
    )
    row_ids = jnp.arange(tile_rows, dtype=jnp.int32) * rows_total + my_row
    col_ids = jnp.arange(column_tiles, dtype=jnp.int32) * cols_total + my_col
    live_tile = (row_ids[:, None] > col_ids[None, :])[:, :, None, None]
    return (
        jnp.where(live_tile, fresh_left, 0.0).astype(jnp.bfloat16),
        jnp.where(live_tile, fresh_right, 0.0).astype(jnp.bfloat16),
    )


def partner(step):
    return 2 * step + CROSSED * min(step, 1)


def nt(first, second):
    return lax.dot_general(first, second, (((1,), (1,)), ((), ())), preferred_element_type=F32)


def nn(first, second):
    return lax.dot_general(first, second, (((1,), (0,)), ((), ())), preferred_element_type=F32)


def split(value):
    high = value.astype(BF16)
    return high, (value - high.astype(F32)).astype(BF16)


def wide(value):
    return jnp.concatenate(split(value), axis=0)


def fold(value):
    half = value.shape[0] // 2
    return value[:half] + value[half:]


def dot_split(op, first, second_parts):
    stacked = wide(first)
    return fold(op(stacked, second_parts[0]) + op(stacked, second_parts[1]))


def grant(mebibytes):
    return pltpu.CompilerParams(vmem_limit_bytes=mebibytes << 20)


def line_mask(tile_lines, ranks):
    width = tile_lines // ranks.shape[0]
    keep = (jnp.arange(width, dtype=jnp.int32)[None, :] < ranks[:, None]).astype(F32).reshape(-1)
    return (
        jnp.broadcast_to(keep[:, None], (tile_lines, LANES)),
        jnp.broadcast_to(keep[None, :], (8, tile_lines)),
    )


def in_vmem(count):
    return [pl.BlockSpec(memory_space=VMEM)] * count


def small_cost(bytes_accessed, flops=0):
    return pl.CostEstimate(flops=flops, bytes_accessed=bytes_accessed, transcendentals=0)


def solve_step(block, my_col, right_ref, inverse, out_ref, step, copy=None):
    @pl.when(block >= my_col)
    def _():
        if copy is not None:
            copy.wait()
        out_ref[step] = nt(right_ref[...], inverse[step]).astype(out_ref.dtype)

    @pl.when(block < my_col)
    def _():
        out_ref[step] = jnp.zeros(out_ref.shape[1:], out_ref.dtype)


def solve_odd_kernel(
    right_hbm, inverse_hbm, out_ref, right_ref, even_ref, inverse_ref, odd_sems, even_sems
):
    parts = out_ref.shape[0]
    piece = right_ref.shape[1]
    my_col = lax.axis_index("col")
    right_copy = pltpu.make_async_copy(right_hbm, right_ref, odd_sems.at[parts])
    right_copy.start()
    copies = []
    for odd, target, sems in ((1, inverse_ref, odd_sems), (0, even_ref, even_sems)):
        for step in range(parts):
            block = my_col ^ (partner(step) ^ odd)
            rows = pl.ds(pl.multiple_of(block * piece, piece), piece)
            copy = pltpu.make_async_copy(inverse_hbm.at[rows], target.at[step], sems.at[step])
            pl.when(block >= my_col)(copy.start)
            copies.append((block, copy))
    right_copy.wait()
    for step in range(parts):
        block, copy = copies[step]
        solve_step(block, my_col, right_ref, inverse_ref, out_ref, step, copy)
    for block, copy in copies[parts:]:
        pl.when(block >= my_col)(copy.wait)


def solve_odd(right, inverse, parts):
    lines, piece = right.shape
    return pl.pallas_call(
        solve_odd_kernel,
        in_specs=[pl.BlockSpec(memory_space=pltpu.HBM)] * 2,
        out_specs=in_vmem(3),
        out_shape=[
            jax.ShapeDtypeStruct((parts, lines, piece), PAIR_TYPE),
            jax.ShapeDtypeStruct((lines, piece), BF16),
            jax.ShapeDtypeStruct((parts, piece, piece), BF16),
        ],
        scratch_shapes=[
            VMEM((parts, piece, piece), BF16),
            pltpu.SemaphoreType.DMA((parts + 1,)),
            pltpu.SemaphoreType.DMA((parts,)),
        ],
        name="solve_odd",
        compiler_params=grant(4),
        cost_estimate=small_cost(
            4 * parts * piece * piece + 4 * parts * lines * piece,
            2 * parts * lines * piece * piece,
        ),
    )(right, inverse)


def solve_even_kernel(right_ref, even_ref, out_ref):
    my_col = lax.axis_index("col")
    for step in range(out_ref.shape[0]):
        solve_step(my_col ^ partner(step), my_col, right_ref, even_ref, out_ref, step)


def solve_even(right, even):
    lines, piece = right.shape
    parts = even.shape[0]
    return pl.pallas_call(
        solve_even_kernel,
        in_specs=in_vmem(2),
        out_specs=pl.BlockSpec(memory_space=VMEM),
        out_shape=jax.ShapeDtypeStruct((parts, lines, piece), F32),
        name="solve_even",
        compiler_params=grant(4),
        cost_estimate=small_cost(
            2 * parts * piece * piece + 4 * parts * lines * piece,
            2 * parts * lines * piece * piece,
        ),
    )(right, even)


def pair_add_kernel(mine_ref, other_ref, keep_ref, *send_refs):
    keep_ref[...] = mine_ref[0] + other_ref[0].astype(F32)
    for step, ref in enumerate(send_refs):
        ref[...] = (mine_ref[step + 1] + other_ref[step + 1].astype(F32)).astype(ref.dtype)


def pair_add(mine, other, send_type):
    parts, lines, piece = mine.shape
    return pl.pallas_call(
        pair_add_kernel,
        in_specs=in_vmem(2),
        out_specs=in_vmem(parts),
        out_shape=[jax.ShapeDtypeStruct((lines, piece), F32)]
        + [jax.ShapeDtypeStruct((lines, piece), send_type)] * (parts - 1),
        name="pair_add",
        compiler_params=grant(4),
        cost_estimate=small_cost(3 * mine.size * 4),
    )(mine, other)


def gather_add_kernel(head, first_ref, mask_ref, *refs):
    *others, solved_ref, head_ref = refs
    total = first_ref[...]
    for ref in others:
        total = total + ref[...].astype(F32)
    keep = jnp.concatenate([mask_ref[...]] * (total.shape[1] // LANES), axis=1)
    rounded = jnp.where(keep > 0.0, total, 0.0).astype(BF16)
    solved_ref[...] = rounded
    head_ref[...] = rounded[:head]


def gather_add(first, mask, others, head):
    return pl.pallas_call(
        functools.partial(gather_add_kernel, head),
        in_specs=in_vmem(2 + len(others)),
        out_specs=in_vmem(2),
        out_shape=[
            jax.ShapeDtypeStruct(first.shape, BF16),
            jax.ShapeDtypeStruct((head, first.shape[1]), BF16),
        ],
        name="gather_add",
        compiler_params=grant(4),
        cost_estimate=small_cost(first.size * 10),
    )(first, mask, *others)


def column_tiles(rows_total, cols_total, width, own_ref, others):
    my_row = lax.axis_index("row")
    for shift in range(rows_total):
        source = own_ref if shift == 0 else others[shift - 1]
        for index in range(cols_total // rows_total):
            lines = source[index * width : (index + 1) * width, :]
            yield index * rows_total + (my_row ^ shift), lines


def message_kernel(rows_total, cols_total, width, own_ref, *refs):
    others = refs[: rows_total - 1]
    *message_refs, stage = refs[rows_total - 1 :]
    my_col = lax.axis_index("col")
    lines = own_ref.shape[0]
    for tile, value in column_tiles(rows_total, cols_total, width, own_ref, others):
        stage[tile] = value
    for step, ref in enumerate(message_refs):
        target = my_col ^ partner(step)
        ref[:width] = stage[target]
        ref[width : width + lines] = own_ref[...]
        ref[width + lines :] = stage[target ^ 1]


def messages(own, others, rows_total, cols_total, width):
    lines, piece = own.shape
    half = cols_total // 2
    return pl.pallas_call(
        functools.partial(message_kernel, rows_total, cols_total, width),
        in_specs=in_vmem(rows_total),
        out_specs=in_vmem(half),
        out_shape=[jax.ShapeDtypeStruct((lines + 2 * width, piece), BF16)] * half,
        scratch_shapes=[VMEM((cols_total, width, piece), BF16)],
        name="messages",
        compiler_params=grant(4),
        cost_estimate=small_cost(half * (lines + 2 * width) * piece * 4),
    )(own, *others)


def bundle_kernel(width, *refs):
    *pieces, here_ref, there_ref = refs
    for step, ref in enumerate(pieces):
        here_ref[step] = ref[: here_ref.shape[1]]
        there_ref[step] = ref[width:]


def bundle(pieces, width):
    count = len(pieces)
    lines, piece = pieces[0].shape
    shape = jax.ShapeDtypeStruct((count, lines - width, piece), BF16)
    return pl.pallas_call(
        functools.partial(bundle_kernel, width),
        in_specs=in_vmem(count),
        out_specs=in_vmem(2),
        out_shape=[shape, shape],
        name="bundle",
        compiler_params=grant(4),
        cost_estimate=small_cost(count * pieces[0].size * 6),
    )(*pieces)


def core_kernel(rows_total, cols_total, width, own_ref, *refs):
    others = refs[: rows_total - 1]
    even_ref, odd_ref, stage = refs[rows_total - 1 :]
    my_col = lax.axis_index("col")
    half = cols_total // 2
    for tile, value in column_tiles(rows_total, cols_total, width, own_ref, others):
        relative = my_col ^ tile
        step = lax.shift_right_logical(relative, 1)
        given = (relative & 1) ^ (jnp.minimum(step, 1) * CROSSED)
        stage[given * half + step] = value
    piece = own_ref.shape[1]
    own = own_ref[...]
    odd_ref[...] = nt(stage[half:].reshape(half * width, piece), own).reshape(odd_ref.shape)
    even_ref[...] = nt(stage[:half].reshape(half * width, piece), own).reshape(even_ref.shape)


def core_parts(own, others, rows_total, cols_total, width):
    lines, piece = own.shape
    half = cols_total // 2
    shape = jax.ShapeDtypeStruct((half, width, lines), F32)
    return pl.pallas_call(
        functools.partial(core_kernel, rows_total, cols_total, width),
        in_specs=in_vmem(rows_total),
        out_specs=in_vmem(2),
        out_shape=[shape, shape],
        scratch_shapes=[VMEM((cols_total, width, piece), BF16)],
        name="core_parts",
        compiler_params=grant(4),
        cost_estimate=small_cost(400000, 2 * lines * piece * cols_total * width),
    )(own, *others)


def piece_spot(relative, piece):
    block = lax.axis_index("col") ^ relative
    return pl.ds(pl.multiple_of(block * piece, LANES), piece)


def same_tile(lines, width):
    lane = lax.broadcasted_iota(jnp.int32, (lines, lines), 1)
    line = lax.broadcasted_iota(jnp.int32, (lines, lines), 0)
    return (lane // width) == (line // width)


def panel_piece(even_ref, odd_ref, relative, width):
    step = relative // 2
    if relative != partner(step):
        lines = odd_ref.shape[1] - width
        return odd_ref[step, :lines], odd_ref[step, lines:]
    return even_ref[step, width:], even_ref[step, :width]


def partial_grams(given, left_ref, right_ref, sketch_ref, panel_ref, width):
    count, lines, piece = panel_ref.shape
    lines = lines - width
    relatives = [partner(step) ^ given for step in range(count)]
    if given:
        panel = jnp.concatenate([panel_ref[k, :lines] for k in range(count)], axis=1)
        column = jnp.concatenate([panel_ref[k, lines:] for k in range(count)], axis=1)
    else:
        panel = jnp.concatenate([panel_ref[k, width:] for k in range(count)], axis=1)
        column = jnp.concatenate([panel_ref[k, :width] for k in range(count)], axis=1)
    left, right, sketch = (
        jnp.concatenate([ref[:, piece_spot(k, piece)] for k in relatives], axis=1)
        for ref in (left_ref, right_ref, sketch_ref)
    )
    return (
        nt(left, panel),
        nt(panel, panel),
        nt(column, right),
        nt(column, column),
        nt(sketch, column),
    )


def early_gram_kernel(width, *refs):
    left_ref, right_ref, sketch_ref, even_ref, keep_line_ref, keep_lane_ref = refs[:6]
    left_high_ref, left_low_ref, right_gram_ref, sketch_right_ref, *sum_refs = refs[6:]
    sums = partial_grams(0, left_ref, right_ref, sketch_ref, even_ref, width)
    for ref, value in zip(sum_refs, sums):
        ref[...] = value
    same = same_tile(left_ref.shape[0], width)
    left, right = left_ref[...], right_ref[...]
    left_high_ref[...], left_low_ref[...] = split(jnp.where(same, nt(left, left), 0.0))
    keep_line = keep_line_ref[...] > 0.0
    keep_lane = keep_lane_ref[:1] > 0.0
    right_gram_ref[...] = jnp.where(same & keep_line & keep_lane, nt(right, right), 0.0)
    sketch_right_ref[...] = jnp.where(keep_lane, nt(sketch_ref[...], right), 0.0)


def early_grams(left, right, sketch, even, keep_line, keep_lane, width):
    lines, order = left.shape
    rounded = jax.ShapeDtypeStruct((lines, lines), BF16)
    square = jax.ShapeDtypeStruct((lines, lines), F32)
    flat = jax.ShapeDtypeStruct((width, lines), F32)
    small = jax.ShapeDtypeStruct((width, width), F32)
    outs = [rounded, rounded, square, flat, square, square, flat, small, small]
    return pl.pallas_call(
        functools.partial(early_gram_kernel, width),
        in_specs=in_vmem(6),
        out_specs=in_vmem(len(outs)),
        out_shape=outs,
        name="early_grams",
        compiler_params=grant(16),
        cost_estimate=small_cost(1000000, 2 * order * lines * lines * 5),
    )(left, right, sketch, even, keep_line, keep_lane)


def late_gram_kernel(width, *refs):
    left_ref, right_ref, sketch_ref, odd_ref, keep_lane_ref, *sum_refs = refs[:10]
    side_high_ref, side_low_ref, turned_high_ref, turned_low_ref, *out_refs = refs[10:]
    lines = left_ref.shape[0]
    same = same_tile(lines, width)
    sums = partial_grams(1, left_ref, right_ref, sketch_ref, odd_ref, width)
    cross, own, column_right, column_column, sketch_column = (
        ref[...] + value for ref, value in zip(sum_refs, sums)
    )
    cross = jnp.where(same, cross, 0.0)
    side_high_ref[:lines], side_low_ref[:lines] = split(cross)
    turned_high_ref[...], turned_low_ref[...] = split(cross.T)
    side_high_ref[lines:], side_low_ref[lines:] = split(jnp.where(same, own, 0.0))
    column_right = jnp.where(keep_lane_ref[:1] > 0.0, column_right, 0.0)
    for ref, value in zip(out_refs, (column_right, column_column, sketch_column)):
        ref[...] = value


def late_grams(left, right, sketch, odd, keep_lane, sums, width):
    lines, order = left.shape
    square = jax.ShapeDtypeStruct((lines, lines), BF16)
    tall = jax.ShapeDtypeStruct((2 * lines, lines), BF16)
    flat = jax.ShapeDtypeStruct((width, lines), F32)
    small = jax.ShapeDtypeStruct((width, width), F32)
    return pl.pallas_call(
        functools.partial(late_gram_kernel, width),
        in_specs=in_vmem(10),
        out_specs=in_vmem(7),
        out_shape=[tall, tall, square, square, flat, small, small],
        name="late_grams",
        compiler_params=grant(16),
        cost_estimate=small_cost(1000000, 2 * order * lines * lines * 2),
    )(left, right, sketch, odd, keep_lane, *sums)


def factor_and_apply(gram, shift, bands):
    width = gram.shape[0]
    count = width // 8
    chunk = count // 2
    lanes = lax.broadcasted_iota(jnp.int32, (8, LANES), 1)
    inner_lane = lax.rem(lanes, width)
    group = lanes - inner_lane
    sub = lax.broadcasted_iota(jnp.int32, (8, LANES), 0)
    inverse_shift = 1.0 / shift
    matrix = [
        gram[8 * b : 8 * b + 8] * inverse_shift + jnp.where(inner_lane == sub + 8 * b, 1.0, 0.0)
        for b in range(count)
    ]
    bands = [matrix] + [[band[8 * b : 8 * b + 8] for b in range(count)] for band in bands]

    def pick(vector, row):
        return vector[row : row + 1]

    for start in range(0, count, chunk):
        first_column = 8 * start
        columns = [
            {
                b: jnp.take_along_axis(matrix[b], group + first_column + k, axis=1)
                for b in range(start + k // 8, count)
            }
            for k in range(8 * chunk)
        ]
        last_half = start + chunk == count
        for k in range(0, 8 * chunk, 2):
            b, row = start + k // 8, k % 8
            one, two = columns[k], columns[k + 1]
            corner = pick(one[b], row)
            side = pick(one[b], row + 1)
            other = pick(two[b], row + 1)
            scale_one = lax.rsqrt(corner)
            scale_two = (corner * scale_one) * lax.rsqrt(corner * other - side * side)
            side = side * scale_one
            one = {c: one[c] * scale_one for c in one}
            two = {c: (two[c] - side * one[c]) * scale_two for c in two}
            for i in range(k + 2, 8 * chunk):
                c, place = start + i // 8, i % 8
                lead_one, lead_two = pick(one[c], place), pick(two[c], place)
                for d in columns[i]:
                    columns[i][d] = columns[i][d] - lead_one * one[d] - lead_two * two[d]
            below_one = dict(one)
            below_two = dict(two)
            below_one[b] = jnp.where(sub > row, one[b], 0.0)
            below_two[b] = jnp.where(sub > row + 1, two[b], 0.0)
            for number, band in enumerate(bands):
                if number == 0 and last_half:
                    continue
                done_one = pick(band[b], row) * scale_one
                done_two = (pick(band[b], row + 1) - side * done_one) * scale_two
                for c in range(b, count):
                    band[c] = band[c] - below_one[c] * done_one - below_two[c] * done_two
                if number > 0:
                    band[b] = jnp.where(
                        sub == row, done_one, jnp.where(sub == row + 1, done_two, band[b])
                    )
    scale = lax.rsqrt(shift)
    return [jnp.concatenate([part * scale for part in band], axis=0) for band in bands[1:]]


def finish_kernel(half, width, rows_total, *refs):
    core_refs = refs[:half]
    (
        left_high_ref,
        left_low_ref,
        right_gram_ref,
        sketch_right_ref,
        side_high_ref,
        side_low_ref,
        turned_high_ref,
        turned_low_ref,
        column_right_ref,
        column_column_ref,
        sketch_column_ref,
        left_ref,
        right_ref,
        even_ref,
        odd_ref,
        keep_lane_ref,
        out_left_hbm,
        out_right_hbm,
        out_left_ref,
        out_right_ref,
        sems,
    ) = refs[half:]
    my_row, my_col = lax.axis_index("row"), lax.axis_index("col")
    lines, order = left_ref.shape
    tiles = lines // width
    piece = odd_ref.shape[2]
    count = 2 * half
    same = same_tile(lines, width)

    def diagonal(value):
        return jnp.where(same, value, 0.0)

    def stacked(value):
        return diagonal(jnp.concatenate([value] * tiles, axis=0))

    def blocks(value):
        return jnp.concatenate([stacked(value[:, :lines]), stacked(value[:, lines:])], axis=1)

    keep_lane = keep_lane_ref[:1] > 0.0
    lane_row = lax.broadcasted_iota(jnp.int32, (1, lines), 1)
    live_line = jnp.zeros((1, lines), jnp.bool_)
    for tile in range(tiles):
        low = tile * width
        live = (tile * rows_total + my_row) > my_col
        live_line |= (lane_row >= low) & (lane_row < low + jnp.where(live, width, 0))

    row_parts = [
        jnp.concatenate(
            [jnp.concatenate([one[...], turned[...]], axis=0), side[...]],
            axis=1,
        )
        for one, turned, side in (
            (left_high_ref, turned_high_ref, side_high_ref),
            (left_low_ref, turned_low_ref, side_low_ref),
        )
    ]
    core = core_refs[0][...]
    for ref in core_refs[1:]:
        core = core + ref[...]
    core_split = split(core)
    core_blocks = stacked(core)
    core_block_split = split(core_blocks)

    first = jnp.concatenate([sketch_right_ref[...], -dot_split(nn, sketch_column_ref[...], core_split)], axis=1)
    ones = jnp.where(same, 1.0, 0.0).astype(BF16)

    def traced(one, two):
        both = jnp.sum(one * two, axis=0, keepdims=True)
        both = both[:, :lines] + both[:, lines:]
        high, low = split(jnp.broadcast_to(both, (8, lines)))
        return (nn(high, ones) + nn(low, ones)) * (shift_rate / width) + tiny_shift

    image = dot_split(nn, first, row_parts)
    shift = traced(first, image)
    gram = dot_split(nt, first, split(blocks(image)))
    core_lines = core.T
    cross = -diagonal(dot_split(nn, core_lines, split(column_right_ref[...])))
    inner = dot_split(nn, column_column_ref[...], core_split)
    corner = diagonal(dot_split(nn, core_lines, split(inner)))
    middle = jnp.concatenate(
        [
            jnp.concatenate([right_gram_ref[...], cross.T], axis=1),
            jnp.concatenate([cross, corner], axis=1),
        ],
        axis=0,
    )
    middle_parts = split(middle)
    beyond_parts = split(dot_split(nn, middle, row_parts))
    top, bottom = factor_and_apply(gram, shift, [image[:, :lines], image[:, lines:]])
    basis = jnp.concatenate([top, bottom], axis=1)

    second = dot_split(nn, basis, middle_parts)
    image = dot_split(nn, basis, beyond_parts)
    shift = traced(second, image)
    gram = dot_split(nt, second, split(blocks(image)))
    back = -dot_split(nt, image[:, lines:], core_block_split)
    left_top, left_bottom, right_top, right_bottom = factor_and_apply(
        gram, shift, [second[:, :lines], second[:, lines:], image[:, :lines], back]
    )
    factor_size = factor_scale * math.sqrt(order)
    live_scale = jnp.where(live_line, factor_size, 0.0)
    live_back = jnp.where(live_line, 1.0 / factor_size, 0.0)
    left_small = jnp.concatenate(
        [stacked(left_top * live_scale), stacked(left_bottom * live_scale)], axis=1
    ).astype(BF16)
    right_small = jnp.concatenate(
        [
            stacked(jnp.where(keep_lane, right_top * live_back, 0.0)),
            stacked(right_bottom * live_back),
        ],
        axis=1,
    ).astype(BF16)
    for relative in range(count):
        spot = piece_spot(relative, piece)
        panel, column = panel_piece(even_ref, odd_ref, relative, width)
        rows = jnp.concatenate([left_ref[:, spot], panel], axis=0)
        out_left_ref[relative] = nn(left_small, rows).astype(BF16)
        tall = jnp.concatenate([right_ref[:, spot]] + [column] * tiles, axis=0)
        out_right_ref[relative] = nn(right_small, tall).astype(BF16)
        for side, (ref, hbm) in enumerate(
            ((out_left_ref, out_left_hbm), (out_right_ref, out_right_hbm))
        ):
            pltpu.make_async_copy(ref.at[relative], hbm.at[:, spot], sems.at[side]).start()
    for side, hbm in enumerate((out_left_hbm, out_right_hbm)):
        pltpu.make_async_copy(hbm, hbm, sems.at[side]).wait()


def finish(cores, others, rows_total, width):
    half = len(cores)
    left = others[11]
    lines, piece = left.shape[0], left.shape[1] // (2 * half)
    shape = jax.ShapeDtypeStruct(left.shape, BF16)
    operands = (*cores, *others)
    return pl.pallas_call(
        functools.partial(finish_kernel, half, width, rows_total),
        in_specs=in_vmem(len(operands)),
        out_specs=[pl.BlockSpec(memory_space=pltpu.HBM)] * 2,
        out_shape=[shape, shape],
        scratch_shapes=[
            VMEM((2 * half, lines, piece), BF16),
            VMEM((2 * half, lines, piece), BF16),
            pltpu.SemaphoreType.DMA((2,)),
        ],
        name="finish",
        compiler_params=grant(16),
        cost_estimate=small_cost(5000000, 10**9),
    )(*operands)


def flat_lines(block):
    return jnp.swapaxes(block, -1, -2).reshape(-1, block.shape[-2])


def fast_shards(
    slab_left, slab_right, slab_ranks, panel_left, panel_right, panel_ranks, inverse_factor, sketch
):
    rows_total = lax.axis_size("row")
    cols_total = lax.axis_size("col")
    width = panel_left.shape[-1]
    half = cols_total // 2
    left, right = flat_lines(slab_left), flat_lines(slab_right)
    panel, solve_right = flat_lines(panel_left), flat_lines(panel_right)
    sketch_lines = flat_lines(sketch)
    head = width * (cols_total // rows_total)

    def swap(block, step):
        return lax.ppermute(block, "col", [(i, i ^ step) for i in range(cols_total)])

    def turn(block, shift):
        pairs = [(i, i ^ shift) for i in range(rows_total)]
        return lax.ppermute(block, "row", pairs)

    def across(blocks):
        return [swap(block, partner(step + 1)) for step, block in enumerate(blocks)]

    def along(block):
        return [turn(block, shift) for shift in range(1, rows_total)]

    panel_keep, _ = line_mask(panel.shape[0], panel_ranks)
    slab_line, slab_lane = line_mask(panel.shape[0], slab_ranks.reshape(-1))
    solve_right = pltpu.with_memory_space_constraint(solve_right, pltpu.HBM)
    inverse_factor = pltpu.with_memory_space_constraint(inverse_factor, pltpu.HBM)
    odd, right_panel, even_blocks = solve_odd(solve_right, inverse_factor, half)
    other = swap(odd, 1)
    even = solve_even(right_panel, even_blocks)
    kept, *sends = pair_add(even, other, BF16)
    received = across(sends)
    panel_others = along(panel[:head])
    solved, solved_head = gather_add(kept, panel_keep, received, head)
    solved_others = along(solved_head)
    own_message, *sends = messages(panel, panel_others, rows_total, cols_total, width)
    even_panel, odd_panel = bundle([own_message] + across(sends), width)
    odd_panel = swap(odd_panel, 1)
    early = early_grams(left, right, sketch_lines, even_panel, slab_line, slab_lane, width)
    slab_parts, sums = early[:4], early[4:]
    panel_parts = late_grams(left, right, sketch_lines, odd_panel, slab_lane, sums, width)
    core_even, core_odd = core_parts(solved, solved_others, rows_total, cols_total, width)
    kept, *sends = pair_add(core_even, swap(core_odd, 1), F32)
    fresh_left, fresh_right = finish(
        [kept] + across(sends),
        (*slab_parts, *panel_parts, left, right, even_panel, odd_panel, slab_lane),
        rows_total,
        width,
    )

    def placed(block):
        tiles = slab_left.shape[:2] + (width, slab_left.shape[2])
        return jnp.swapaxes(block.reshape(tiles), -1, -2)

    return placed(fresh_left), placed(fresh_right)


def fast_fits(rows_total, cols_total, tile_rows, piece_rows, width, column_tiles):
    return (
        column_tiles == 1
        and tile_rows * width == LANES
        and width % 8 == 0
        and piece_rows % LANES == 0
        and cols_total & (cols_total - 1) == 0
        and cols_total >= 4
        and rows_total & (rows_total - 1) == 0
        and cols_total % rows_total == 0
        and rows_total > 1
        and cols_total <= tile_rows * rows_total
    )


def shards(*args):
    tile_rows, piece_rows, width = args[3].shape
    rows_total, cols_total = lax.axis_size("row"), lax.axis_size("col")
    fits = fast_fits(rows_total, cols_total, tile_rows, piece_rows, width, args[0].shape[1])
    return fast_shards(*args) if fits else plain_shards(*args)


def solution(mesh):
    placed = (
        P("row", "col", None, None),
        P("row", "col", None, None),
        P("row", "col"),
        P("row", "col", None),
        P("row", "col", None),
        P("row"),
        P(None, "col"),
        P(),
    )
    return jax.shard_map(
        shards,
        mesh=mesh,
        in_specs=placed,
        out_specs=(P("row", "col", None, None), P("row", "col", None, None)),
        check_vma=False,
    )
```

```python
import functools
import math

import jax
import jax.numpy as jnp
from jax import lax
from jax.experimental import pallas as pl
from jax.experimental.pallas import tpu as pltpu
from jax.sharding import PartitionSpec as P


highest = lax.Precision.HIGHEST
stacked_precision = lax.Precision.HIGH
shift_rate = 0.01
tiny_shift = 1e-06
factor_scale = 0.5
LANES = 128
F32 = jnp.float32
BF16 = jnp.bfloat16
VMEM = pltpu.VMEM
PAIR_TYPE = BF16
CROSSED = 1
FLIPPED = 1


def spread(block, axis, owner):
    block = jnp.where(lax.axis_index(axis) == owner, block, jnp.zeros_like(block))
    return lax.psum(block, axis)


def product(first_matrix, second_matrix):
    return jnp.matmul(first_matrix, second_matrix, precision=highest)


def stacked_product(first_matrix, second_matrix):
    return jnp.matmul(first_matrix, second_matrix, precision=stacked_precision)


def flipped(matrix):
    return jnp.swapaxes(matrix, -1, -2)


def orthonormal(vectors):
    gram_matrix = product(flipped(vectors), vectors)
    shift_value = (
        shift_rate * jnp.trace(gram_matrix, axis1=-2, axis2=-1) / gram_matrix.shape[-1] + tiny_shift
    )
    identity = jnp.eye(gram_matrix.shape[-1], dtype=gram_matrix.dtype)
    lower_factor = jnp.linalg.cholesky(gram_matrix + shift_value[..., None, None] * identity)
    solved_rows = lax.linalg.triangular_solve(
        lower_factor, flipped(vectors), left_side=True, lower=True
    )
    return flipped(solved_rows)


def recompress(slab_factor, masked_right, row_factor, core_block, column_factor, sketch_float):
    target_shape = core_block.shape[:2] + slab_factor.shape[2:]
    column_wide = jnp.broadcast_to(column_factor[None], target_shape)
    row_core = product(row_factor, core_block)
    column_core = product(column_wide, flipped(core_block))
    forward_left = jnp.concatenate([slab_factor.astype(jnp.float32), -row_core], axis=-1)
    forward_right = jnp.concatenate([masked_right.astype(jnp.float32), column_wide], axis=-1)
    backward_left = jnp.concatenate([masked_right.astype(jnp.float32), -column_core], axis=-1)
    backward_right = jnp.concatenate([slab_factor.astype(jnp.float32), row_factor], axis=-1)

    def forward(vectors):
        return stacked_product(forward_left, stacked_product(flipped(forward_right), vectors))

    def backward(vectors):
        return stacked_product(backward_left, stacked_product(flipped(backward_right), vectors))

    basis_now = orthonormal(forward(sketch_float))
    basis_now = orthonormal(forward(backward(basis_now)))
    projected = backward(basis_now)
    factor_size = factor_scale * math.sqrt(slab_factor.shape[-2])
    return (basis_now * factor_size, projected / factor_size)


def plain_shards(
    slab_left, slab_right, slab_ranks, panel_left, panel_right, panel_ranks, inverse_factor, sketch
):
    rows_total = lax.axis_size("row")
    cols_total = lax.axis_size("col")
    my_row = lax.axis_index("row")
    my_col = lax.axis_index("col")
    tile_rows, piece_rows, rank_width = panel_left.shape
    column_tiles = slab_left.shape[1]
    tile_order = inverse_factor.shape[0]
    panel_keep = jnp.arange(rank_width, dtype=jnp.int32)[None, :] < panel_ranks[:, None]
    masked_panel = jnp.where(panel_keep[:, None, :], panel_right, jnp.zeros((), jnp.bfloat16))
    flat_right = jnp.swapaxes(masked_panel, 0, 1).reshape(piece_rows, tile_rows * rank_width)
    flat_left = jnp.swapaxes(panel_left, 0, 1).reshape(piece_rows, tile_rows * rank_width)
    solved_part = lax.psum_scatter(
        jnp.dot(inverse_factor, flat_right, preferred_element_type=jnp.float32),
        "col",
        scatter_dimension=0,
        tiled=True,
    ).astype(jnp.bfloat16)
    full_left, full_solved = (
        lax.all_gather(flat_left, "col", axis=0, tiled=True),
        lax.all_gather(solved_part, "col", axis=0, tiled=True),
    )
    full_left = full_left.reshape(tile_order, tile_rows, rank_width)
    full_solved = full_solved.reshape(tile_order, tile_rows, rank_width)
    first_pick = my_col // rows_total
    position = first_pick + 0
    picked_left = lax.dynamic_slice_in_dim(full_left, position, 1, 1)
    picked_solved = lax.dynamic_slice_in_dim(full_solved, position, 1, 1)
    send_left = picked_left.reshape(tile_order, column_tiles * rank_width)
    send_solved = picked_solved.reshape(tile_order, column_tiles * rank_width)
    root_row = my_col % rows_total
    column_left, column_solved = (
        spread(send_left, "row", root_row),
        spread(send_solved, "row", root_row),
    )
    row_factor = jnp.swapaxes(full_left, 0, 1)[:, None]
    row_solved = jnp.swapaxes(full_solved, 0, 1)
    column_factor = jnp.swapaxes(column_left.reshape(tile_order, column_tiles, rank_width), 0, 1)
    column_three = jnp.swapaxes(column_solved.reshape(tile_order, column_tiles, rank_width), 0, 1)
    core_block = jnp.einsum(
        "tbr,sbq->tsrq", row_solved, column_three, preferred_element_type=jnp.float32
    )
    slab_keep = jnp.arange(rank_width, dtype=jnp.int32) < slab_ranks[..., None]
    masked_right = jnp.where(slab_keep[:, :, None, :], slab_right, jnp.zeros((), jnp.bfloat16))
    fresh_left, fresh_right = recompress(
        slab_left, masked_right, row_factor, core_block, column_factor, sketch.astype(jnp.float32)
    )
    row_ids = jnp.arange(tile_rows, dtype=jnp.int32) * rows_total + my_row
    col_ids = jnp.arange(column_tiles, dtype=jnp.int32) * cols_total + my_col
    live_tile = (row_ids[:, None] > col_ids[None, :])[:, :, None, None]
    return (
        jnp.where(live_tile, fresh_left, 0.0).astype(jnp.bfloat16),
        jnp.where(live_tile, fresh_right, 0.0).astype(jnp.bfloat16),
    )


def partner(step):
    return 2 * step + CROSSED * min(step, 1)


def flip(row):
    return row & FLIPPED


def owned_block():
    return lax.axis_index("col") ^ flip(lax.axis_index("row"))


def nt(first, second):
    return lax.dot_general(first, second, (((1,), (1,)), ((), ())), preferred_element_type=F32)


def nn(first, second):
    return lax.dot_general(first, second, (((1,), (0,)), ((), ())), preferred_element_type=F32)


def split(value):
    high = value.astype(BF16)
    return high, (value - high.astype(F32)).astype(BF16)


def wide(value):
    return jnp.concatenate(split(value), axis=0)


def fold(value):
    half = value.shape[0] // 2
    return value[:half] + value[half:]


def dot_split(op, first, second_parts):
    stacked = wide(first)
    return fold(op(stacked, second_parts[0]) + op(stacked, second_parts[1]))


def grant(mebibytes):
    return pltpu.CompilerParams(vmem_limit_bytes=mebibytes << 20)


def line_mask(tile_lines, ranks):
    width = tile_lines // ranks.shape[0]
    keep = (jnp.arange(width, dtype=jnp.int32)[None, :] < ranks[:, None]).astype(F32).reshape(-1)
    return (
        jnp.broadcast_to(keep[:, None], (tile_lines, LANES)),
        jnp.broadcast_to(keep[None, :], (8, tile_lines)),
    )


def in_vmem(count):
    return [pl.BlockSpec(memory_space=VMEM)] * count


def small_cost(bytes_accessed, flops=0):
    return pl.CostEstimate(flops=flops, bytes_accessed=bytes_accessed, transcendentals=0)


def solve_step(block, my_col, right_ref, inverse, out_ref, step, copy=None, spare=None):
    @pl.when(block >= my_col)
    def _():
        if copy is not None:
            copy.wait()
        value = nt(right_ref[...], inverse[step])
        out_ref[step] = value.astype(out_ref.dtype)
        if spare is not None and step == 0:
            out_ref[spare] = (value - out_ref[step].astype(F32)).astype(out_ref.dtype)

    @pl.when(block < my_col)
    def _():
        out_ref[step] = jnp.zeros(out_ref.shape[1:], out_ref.dtype)
        if spare is not None and step == 0:
            out_ref[spare] = jnp.zeros(out_ref.shape[1:], out_ref.dtype)


def solve_odd_kernel(
    right_hbm, inverse_hbm, out_ref, right_ref, even_ref, inverse_ref, odd_sems, even_sems
):
    parts = inverse_ref.shape[0]
    piece = right_ref.shape[1]
    my_col, owned = lax.axis_index("col"), owned_block()
    right_copy = pltpu.make_async_copy(right_hbm, right_ref, odd_sems.at[parts])
    right_copy.start()
    copies = []
    for odd, target, sems in ((1, inverse_ref, odd_sems), (0, even_ref, even_sems)):
        for step in range(parts):
            block = owned ^ (partner(step) ^ odd)
            rows = pl.ds(pl.multiple_of(block * piece, piece), piece)
            copy = pltpu.make_async_copy(inverse_hbm.at[rows], target.at[step], sems.at[step])
            pl.when(block >= my_col)(copy.start)
            copies.append((block, copy))
    right_copy.wait()
    for step in range(parts):
        block, copy = copies[step]
        solve_step(block, my_col, right_ref, inverse_ref, out_ref, step, copy, parts)
    for block, copy in copies[parts:]:
        pl.when(block >= my_col)(copy.wait)


def solve_odd(right, inverse, parts):
    lines, piece = right.shape
    return pl.pallas_call(
        solve_odd_kernel,
        in_specs=[pl.BlockSpec(memory_space=pltpu.HBM)] * 2,
        out_specs=in_vmem(3),
        out_shape=[
            jax.ShapeDtypeStruct((parts + 1, lines, piece), PAIR_TYPE),
            jax.ShapeDtypeStruct((lines, piece), BF16),
            jax.ShapeDtypeStruct((parts, piece, piece), BF16),
        ],
        scratch_shapes=[
            VMEM((parts, piece, piece), BF16),
            pltpu.SemaphoreType.DMA((parts + 1,)),
            pltpu.SemaphoreType.DMA((parts,)),
        ],
        name="solve_odd",
        compiler_params=grant(4),
        cost_estimate=small_cost(
            4 * parts * piece * piece + 4 * parts * lines * piece,
            2 * parts * lines * piece * piece,
        ),
    )(right, inverse)


def solve_even_kernel(right_ref, even_ref, out_ref):
    my_col = lax.axis_index("col")
    for step in range(out_ref.shape[0]):
        solve_step(owned_block() ^ partner(step), my_col, right_ref, even_ref, out_ref, step)


def solve_even(right, even):
    lines, piece = right.shape
    parts = even.shape[0]
    return pl.pallas_call(
        solve_even_kernel,
        in_specs=in_vmem(2),
        out_specs=pl.BlockSpec(memory_space=VMEM),
        out_shape=jax.ShapeDtypeStruct((parts, lines, piece), F32),
        name="solve_even",
        compiler_params=grant(4),
        cost_estimate=small_cost(
            2 * parts * piece * piece + 4 * parts * lines * piece,
            2 * parts * lines * piece * piece,
        ),
    )(right, even)


def pair_add_kernel(mine_ref, other_ref, keep_ref, *send_refs):
    total = mine_ref[0] + other_ref[0].astype(F32)
    if other_ref.shape[0] > mine_ref.shape[0]:
        total = total + other_ref[mine_ref.shape[0]].astype(F32)
    keep_ref[...] = total
    for step, ref in enumerate(send_refs):
        ref[...] = (mine_ref[step + 1] + other_ref[step + 1].astype(F32)).astype(ref.dtype)


def pair_add(mine, other, send_type):
    parts, lines, piece = mine.shape
    return pl.pallas_call(
        pair_add_kernel,
        in_specs=in_vmem(2),
        out_specs=in_vmem(parts),
        out_shape=[jax.ShapeDtypeStruct((lines, piece), F32)]
        + [jax.ShapeDtypeStruct((lines, piece), send_type)] * (parts - 1),
        name="pair_add",
        compiler_params=grant(4),
        cost_estimate=small_cost(3 * mine.size * 4),
    )(mine, other)


def gather_add_kernel(head, first_ref, mask_ref, *refs):
    *others, solved_ref, head_ref = refs
    total = first_ref[...]
    for ref in others:
        total = total + ref[...].astype(F32)
    keep = jnp.concatenate([mask_ref[...]] * (total.shape[1] // LANES), axis=1)
    halves = wide(jnp.where(keep > 0.0, total, 0.0))
    solved_ref[...] = halves
    head_ref[...] = halves[:head]


def gather_add(first, mask, others, head):
    return pl.pallas_call(
        functools.partial(gather_add_kernel, head),
        in_specs=in_vmem(2 + len(others)),
        out_specs=in_vmem(2),
        out_shape=[
            jax.ShapeDtypeStruct((2 * first.shape[0], first.shape[1]), BF16),
            jax.ShapeDtypeStruct((head, first.shape[1]), BF16),
        ],
        name="gather_add",
        compiler_params=grant(4),
        cost_estimate=small_cost(first.size * 10),
    )(first, mask, *others)


def column_tiles(rows_total, cols_total, width, own_ref, others):
    my_row = lax.axis_index("row")
    for shift in range(rows_total):
        source = own_ref if shift == 0 else others[shift - 1]
        for index in range(cols_total // rows_total):
            lines = source[index * width : (index + 1) * width, :]
            yield index * rows_total + (my_row ^ shift), lines


def message_kernel(rows_total, cols_total, width, own_ref, *refs):
    others = refs[: rows_total - 1]
    *message_refs, stage = refs[rows_total - 1 :]
    my_col = lax.axis_index("col")
    lines = own_ref.shape[0]
    for tile, value in column_tiles(rows_total, cols_total, width, own_ref, others):
        stage[tile] = value
    for step, ref in enumerate(message_refs):
        target = my_col ^ partner(step)
        ref[:width] = stage[target]
        ref[width : width + lines] = own_ref[...]
        ref[width + lines :] = stage[target ^ 1]


def messages(own, others, rows_total, cols_total, width):
    lines, piece = own.shape
    half = cols_total // 2
    return pl.pallas_call(
        functools.partial(message_kernel, rows_total, cols_total, width),
        in_specs=in_vmem(rows_total),
        out_specs=in_vmem(half),
        out_shape=[jax.ShapeDtypeStruct((lines + 2 * width, piece), BF16)] * half,
        scratch_shapes=[VMEM((cols_total, width, piece), BF16)],
        name="messages",
        compiler_params=grant(4),
        cost_estimate=small_cost(half * (lines + 2 * width) * piece * 4),
    )(own, *others)


def bundle_kernel(width, *refs):
    *pieces, here_ref, there_ref = refs
    for step, ref in enumerate(pieces):
        here_ref[step] = ref[: here_ref.shape[1]]
        there_ref[step] = ref[width:]


def bundle(pieces, width):
    count = len(pieces)
    lines, piece = pieces[0].shape
    shape = jax.ShapeDtypeStruct((count, lines - width, piece), BF16)
    return pl.pallas_call(
        functools.partial(bundle_kernel, width),
        in_specs=in_vmem(count),
        out_specs=in_vmem(2),
        out_shape=[shape, shape],
        name="bundle",
        compiler_params=grant(4),
        cost_estimate=small_cost(count * pieces[0].size * 6),
    )(*pieces)


def core_kernel(rows_total, cols_total, width, own_ref, *refs):
    others = refs[: rows_total - 1]
    even_ref, odd_ref, stage = refs[rows_total - 1 :]
    my_col = lax.axis_index("col")
    half = cols_total // 2
    for tile, value in column_tiles(rows_total, cols_total, width, own_ref, others):
        relative = my_col ^ tile
        step = lax.shift_right_logical(relative, 1)
        given = (relative & 1) ^ (jnp.minimum(step, 1) * CROSSED)
        stage[given * half + step] = value
    piece = own_ref.shape[1]
    lines = odd_ref.shape[2]
    high, low = own_ref[:lines], own_ref[lines:]
    for ref, part in ((odd_ref, stage[half:]), (even_ref, stage[:half])):
        part = part.reshape(half * width, piece)
        ref[...] = (nt(part, high) + nt(part, low)).reshape(ref.shape)


def core_parts(own, others, rows_total, cols_total, width):
    lines, piece = own.shape[0] // 2, own.shape[1]
    half = cols_total // 2
    shape = jax.ShapeDtypeStruct((half, width, lines), F32)
    return pl.pallas_call(
        functools.partial(core_kernel, rows_total, cols_total, width),
        in_specs=in_vmem(rows_total),
        out_specs=in_vmem(2),
        out_shape=[shape, shape],
        scratch_shapes=[VMEM((cols_total, width, piece), BF16)],
        name="core_parts",
        compiler_params=grant(4),
        cost_estimate=small_cost(400000, 2 * lines * piece * cols_total * width),
    )(own, *others)


def piece_spot(relative, piece):
    block = lax.axis_index("col") ^ relative
    return pl.ds(pl.multiple_of(block * piece, LANES), piece)


def same_tile(lines, width):
    lane = lax.broadcasted_iota(jnp.int32, (lines, lines), 1)
    line = lax.broadcasted_iota(jnp.int32, (lines, lines), 0)
    return (lane // width) == (line // width)


def panel_piece(even_ref, odd_ref, relative, width):
    step = relative // 2
    if relative != partner(step):
        lines = odd_ref.shape[1] - width
        return odd_ref[step, :lines], odd_ref[step, lines:]
    return even_ref[step, width:], even_ref[step, :width]


def partial_grams(given, left_ref, right_ref, sketch_ref, panel_ref, width):
    count, lines, piece = panel_ref.shape
    lines = lines - width
    relatives = [partner(step) ^ given for step in range(count)]
    if given:
        panel = jnp.concatenate([panel_ref[k, :lines] for k in range(count)], axis=1)
        column = jnp.concatenate([panel_ref[k, lines:] for k in range(count)], axis=1)
    else:
        panel = jnp.concatenate([panel_ref[k, width:] for k in range(count)], axis=1)
        column = jnp.concatenate([panel_ref[k, :width] for k in range(count)], axis=1)
    left, right, sketch = (
        jnp.concatenate([ref[:, piece_spot(k, piece)] for k in relatives], axis=1)
        for ref in (left_ref, right_ref, sketch_ref)
    )
    return (
        nt(left, panel),
        nt(panel, panel),
        nt(column, right),
        nt(column, column),
        nt(sketch, column),
    )


def early_gram_kernel(width, *refs):
    left_ref, right_ref, sketch_ref, even_ref, keep_line_ref, keep_lane_ref = refs[:6]
    left_high_ref, left_low_ref, right_gram_ref, sketch_right_ref, *sum_refs = refs[6:]
    sums = partial_grams(0, left_ref, right_ref, sketch_ref, even_ref, width)
    for ref, value in zip(sum_refs, sums):
        ref[...] = value
    same = same_tile(left_ref.shape[0], width)
    left, right = left_ref[...], right_ref[...]
    left_high_ref[...], left_low_ref[...] = split(jnp.where(same, nt(left, left), 0.0))
    keep_line = keep_line_ref[...] > 0.0
    keep_lane = keep_lane_ref[:1] > 0.0
    right_gram_ref[...] = jnp.where(same & keep_line & keep_lane, nt(right, right), 0.0)
    sketch_right_ref[...] = jnp.where(keep_lane, nt(sketch_ref[...], right), 0.0)


def early_grams(left, right, sketch, even, keep_line, keep_lane, width):
    lines, order = left.shape
    rounded = jax.ShapeDtypeStruct((lines, lines), BF16)
    square = jax.ShapeDtypeStruct((lines, lines), F32)
    flat = jax.ShapeDtypeStruct((width, lines), F32)
    small = jax.ShapeDtypeStruct((width, width), F32)
    outs = [rounded, rounded, square, flat, square, square, flat, small, small]
    return pl.pallas_call(
        functools.partial(early_gram_kernel, width),
        in_specs=in_vmem(6),
        out_specs=in_vmem(len(outs)),
        out_shape=outs,
        name="early_grams",
        compiler_params=grant(16),
        cost_estimate=small_cost(1000000, 2 * order * lines * lines * 5),
    )(left, right, sketch, even, keep_line, keep_lane)


def late_gram_kernel(width, *refs):
    left_ref, right_ref, sketch_ref, odd_ref, keep_lane_ref, *sum_refs = refs[:10]
    side_high_ref, side_low_ref, turned_high_ref, turned_low_ref, *out_refs = refs[10:]
    lines = left_ref.shape[0]
    same = same_tile(lines, width)
    sums = partial_grams(1, left_ref, right_ref, sketch_ref, odd_ref, width)
    cross, own, column_right, column_column, sketch_column = (
        ref[...] + value for ref, value in zip(sum_refs, sums)
    )
    cross = jnp.where(same, cross, 0.0)
    side_high_ref[:lines], side_low_ref[:lines] = split(cross)
    turned_high_ref[...], turned_low_ref[...] = split(cross.T)
    side_high_ref[lines:], side_low_ref[lines:] = split(jnp.where(same, own, 0.0))
    column_right = jnp.where(keep_lane_ref[:1] > 0.0, column_right, 0.0)
    for ref, value in zip(out_refs, (column_right, column_column, sketch_column)):
        ref[...] = value


def late_grams(left, right, sketch, odd, keep_lane, sums, width):
    lines, order = left.shape
    square = jax.ShapeDtypeStruct((lines, lines), BF16)
    tall = jax.ShapeDtypeStruct((2 * lines, lines), BF16)
    flat = jax.ShapeDtypeStruct((width, lines), F32)
    small = jax.ShapeDtypeStruct((width, width), F32)
    return pl.pallas_call(
        functools.partial(late_gram_kernel, width),
        in_specs=in_vmem(10),
        out_specs=in_vmem(7),
        out_shape=[tall, tall, square, square, flat, small, small],
        name="late_grams",
        compiler_params=grant(16),
        cost_estimate=small_cost(1000000, 2 * order * lines * lines * 2),
    )(left, right, sketch, odd, keep_lane, *sums)


def factor_and_apply(gram, shift, bands):
    width = gram.shape[0]
    count = width // 8
    chunk = count // 2
    lanes = lax.broadcasted_iota(jnp.int32, (8, LANES), 1)
    inner_lane = lax.rem(lanes, width)
    group = lanes - inner_lane
    sub = lax.broadcasted_iota(jnp.int32, (8, LANES), 0)
    inverse_shift = 1.0 / shift
    matrix = [
        gram[8 * b : 8 * b + 8] * inverse_shift + jnp.where(inner_lane == sub + 8 * b, 1.0, 0.0)
        for b in range(count)
    ]
    bands = [matrix] + [[band[8 * b : 8 * b + 8] for b in range(count)] for band in bands]

    def pick(vector, row):
        return vector[row : row + 1]

    for start in range(0, count, chunk):
        first_column = 8 * start
        columns = [
            {
                b: jnp.take_along_axis(matrix[b], group + first_column + k, axis=1)
                for b in range(start + k // 8, count)
            }
            for k in range(8 * chunk)
        ]
        last_half = start + chunk == count
        for k in range(0, 8 * chunk, 2):
            b, row = start + k // 8, k % 8
            one, two = columns[k], columns[k + 1]
            corner = pick(one[b], row)
            side = pick(one[b], row + 1)
            other = pick(two[b], row + 1)
            scale_one = lax.rsqrt(corner)
            scale_two = (corner * scale_one) * lax.rsqrt(corner * other - side * side)
            side = side * scale_one
            one = {c: one[c] * scale_one for c in one}
            two = {c: (two[c] - side * one[c]) * scale_two for c in two}
            for i in range(k + 2, 8 * chunk):
                c, place = start + i // 8, i % 8
                lead_one, lead_two = pick(one[c], place), pick(two[c], place)
                for d in columns[i]:
                    columns[i][d] = columns[i][d] - lead_one * one[d] - lead_two * two[d]
            below_one = dict(one)
            below_two = dict(two)
            below_one[b] = jnp.where(sub > row, one[b], 0.0)
            below_two[b] = jnp.where(sub > row + 1, two[b], 0.0)
            for number, band in enumerate(bands):
                if number == 0 and last_half:
                    continue
                done_one = pick(band[b], row) * scale_one
                done_two = (pick(band[b], row + 1) - side * done_one) * scale_two
                for c in range(b, count):
                    band[c] = band[c] - below_one[c] * done_one - below_two[c] * done_two
                if number > 0:
                    band[b] = jnp.where(
                        sub == row, done_one, jnp.where(sub == row + 1, done_two, band[b])
                    )
    scale = lax.rsqrt(shift)
    return [jnp.concatenate([part * scale for part in band], axis=0) for band in bands[1:]]


def finish_kernel(half, width, rows_total, *refs):
    core_refs = refs[:half]
    (
        left_high_ref,
        left_low_ref,
        right_gram_ref,
        sketch_right_ref,
        side_high_ref,
        side_low_ref,
        turned_high_ref,
        turned_low_ref,
        column_right_ref,
        column_column_ref,
        sketch_column_ref,
        left_ref,
        right_ref,
        even_ref,
        odd_ref,
        keep_lane_ref,
        out_left_hbm,
        out_right_hbm,
        out_left_ref,
        out_right_ref,
        sems,
    ) = refs[half:]
    my_row, my_col = lax.axis_index("row"), lax.axis_index("col")
    lines, order = left_ref.shape
    tiles = lines // width
    piece = odd_ref.shape[2]
    count = 2 * half
    same = same_tile(lines, width)

    def diagonal(value):
        return jnp.where(same, value, 0.0)

    def stacked(value):
        return diagonal(jnp.concatenate([value] * tiles, axis=0))

    def blocks(value):
        return jnp.concatenate([stacked(value[:, :lines]), stacked(value[:, lines:])], axis=1)

    keep_lane = keep_lane_ref[:1] > 0.0
    lane_row = lax.broadcasted_iota(jnp.int32, (1, lines), 1)
    live_line = jnp.zeros((1, lines), jnp.bool_)
    for tile in range(tiles):
        low = tile * width
        live = (tile * rows_total + my_row) > my_col
        live_line |= (lane_row >= low) & (lane_row < low + jnp.where(live, width, 0))

    row_parts = [
        jnp.concatenate(
            [jnp.concatenate([one[...], turned[...]], axis=0), side[...]],
            axis=1,
        )
        for one, turned, side in (
            (left_high_ref, turned_high_ref, side_high_ref),
            (left_low_ref, turned_low_ref, side_low_ref),
        )
    ]
    core = core_refs[0][...]
    for ref in core_refs[1:]:
        core = core + ref[...]
    core_split = split(core)
    core_blocks = stacked(core)
    core_block_split = split(core_blocks)

    first = jnp.concatenate([sketch_right_ref[...], -dot_split(nn, sketch_column_ref[...], core_split)], axis=1)
    ones = jnp.where(same, 1.0, 0.0).astype(BF16)

    def traced(one, two):
        both = jnp.sum(one * two, axis=0, keepdims=True)
        both = both[:, :lines] + both[:, lines:]
        high, low = split(jnp.broadcast_to(both, (8, lines)))
        return (nn(high, ones) + nn(low, ones)) * (shift_rate / width) + tiny_shift

    image = dot_split(nn, first, row_parts)
    shift = traced(first, image)
    gram = dot_split(nt, first, split(blocks(image)))
    core_lines = core.T
    cross = -diagonal(dot_split(nn, core_lines, split(column_right_ref[...])))
    inner = dot_split(nn, column_column_ref[...], core_split)
    corner = diagonal(dot_split(nn, core_lines, split(inner)))
    middle = jnp.concatenate(
        [
            jnp.concatenate([right_gram_ref[...], cross.T], axis=1),
            jnp.concatenate([cross, corner], axis=1),
        ],
        axis=0,
    )
    middle_parts = split(middle)
    beyond_parts = split(dot_split(nn, middle, row_parts))
    top, bottom = factor_and_apply(gram, shift, [image[:, :lines], image[:, lines:]])
    basis = jnp.concatenate([top, bottom], axis=1)

    second = dot_split(nn, basis, middle_parts)
    image = dot_split(nn, basis, beyond_parts)
    shift = traced(second, image)
    gram = dot_split(nt, second, split(blocks(image)))
    back = -dot_split(nt, image[:, lines:], core_block_split)
    left_top, left_bottom, right_top, right_bottom = factor_and_apply(
        gram, shift, [second[:, :lines], second[:, lines:], image[:, :lines], back]
    )
    factor_size = factor_scale * math.sqrt(order)
    live_scale = jnp.where(live_line, factor_size, 0.0)
    live_back = jnp.where(live_line, 1.0 / factor_size, 0.0)
    left_small = jnp.concatenate(
        [stacked(left_top * live_scale), stacked(left_bottom * live_scale)], axis=1
    ).astype(BF16)
    right_small = jnp.concatenate(
        [
            stacked(jnp.where(keep_lane, right_top * live_back, 0.0)),
            stacked(right_bottom * live_back),
        ],
        axis=1,
    ).astype(BF16)
    for relative in range(count):
        spot = piece_spot(relative, piece)
        panel, column = panel_piece(even_ref, odd_ref, relative, width)
        rows = jnp.concatenate([left_ref[:, spot], panel], axis=0)
        out_left_ref[relative] = nn(left_small, rows).astype(BF16)
        tall = jnp.concatenate([right_ref[:, spot]] + [column] * tiles, axis=0)
        out_right_ref[relative] = nn(right_small, tall).astype(BF16)
        for side, (ref, hbm) in enumerate(
            ((out_left_ref, out_left_hbm), (out_right_ref, out_right_hbm))
        ):
            pltpu.make_async_copy(ref.at[relative], hbm.at[:, spot], sems.at[side]).start()
    for side, hbm in enumerate((out_left_hbm, out_right_hbm)):
        pltpu.make_async_copy(hbm, hbm, sems.at[side]).wait()


def finish(cores, others, rows_total, width):
    half = len(cores)
    left = others[11]
    lines, piece = left.shape[0], left.shape[1] // (2 * half)
    shape = jax.ShapeDtypeStruct(left.shape, BF16)
    operands = (*cores, *others)
    return pl.pallas_call(
        functools.partial(finish_kernel, half, width, rows_total),
        in_specs=in_vmem(len(operands)),
        out_specs=[pl.BlockSpec(memory_space=pltpu.HBM)] * 2,
        out_shape=[shape, shape],
        scratch_shapes=[
            VMEM((2 * half, lines, piece), BF16),
            VMEM((2 * half, lines, piece), BF16),
            pltpu.SemaphoreType.DMA((2,)),
        ],
        name="finish",
        compiler_params=grant(16),
        cost_estimate=small_cost(5000000, 10**9),
    )(*operands)


def flat_lines(block):
    return jnp.swapaxes(block, -1, -2).reshape(-1, block.shape[-2])


def fast_shards(
    slab_left, slab_right, slab_ranks, panel_left, panel_right, panel_ranks, inverse_factor, sketch
):
    rows_total = lax.axis_size("row")
    cols_total = lax.axis_size("col")
    width = panel_left.shape[-1]
    half = cols_total // 2
    left, right = flat_lines(slab_left), flat_lines(slab_right)
    panel, solve_right = flat_lines(panel_left), flat_lines(panel_right)
    sketch_lines = flat_lines(sketch)
    head = width * (cols_total // rows_total)

    def swap(block, step):
        return lax.ppermute(block, "col", [(i, i ^ step) for i in range(cols_total)])

    def turn(block, shift, owners=False):
        pairs = []
        for row in range(rows_total):
            other = row ^ shift
            change = flip(row) ^ flip(other) if owners else 0
            for col in range(cols_total):
                pairs.append((row * cols_total + col, other * cols_total + (col ^ change)))
        return lax.ppermute(block, ("row", "col"), pairs)

    def across(blocks):
        return [swap(block, partner(step + 1)) for step, block in enumerate(blocks)]

    def along(block, owners=False):
        return [turn(block, shift, owners) for shift in range(1, rows_total)]

    panel_keep, _ = line_mask(panel.shape[0], panel_ranks)
    slab_line, slab_lane = line_mask(panel.shape[0], slab_ranks.reshape(-1))
    solve_right = pltpu.with_memory_space_constraint(solve_right, pltpu.HBM)
    inverse_factor = pltpu.with_memory_space_constraint(inverse_factor, pltpu.HBM)
    odd, right_panel, even_blocks = solve_odd(solve_right, inverse_factor, half)
    other = swap(odd, 1)
    even = solve_even(right_panel, even_blocks)
    kept, *sends = pair_add(even, other, BF16)
    received = across(sends)
    panel_others = along(panel[:head])
    solved, solved_head = gather_add(kept, panel_keep, received, head)
    solved_others = along(solved_head, True)
    own_message, *sends = messages(panel, panel_others, rows_total, cols_total, width)
    even_panel, odd_panel = bundle([own_message] + across(sends), width)
    odd_panel = swap(odd_panel, 1)
    early = early_grams(left, right, sketch_lines, even_panel, slab_line, slab_lane, width)
    slab_parts, sums = early[:4], early[4:]
    panel_parts = late_grams(left, right, sketch_lines, odd_panel, slab_lane, sums, width)
    core_even, core_odd = core_parts(solved, solved_others, rows_total, cols_total, width)
    kept, *sends = pair_add(core_even, swap(core_odd, 1), F32)
    fresh_left, fresh_right = finish(
        [kept] + across(sends),
        (*slab_parts, *panel_parts, left, right, even_panel, odd_panel, slab_lane),
        rows_total,
        width,
    )

    def placed(block):
        tiles = slab_left.shape[:2] + (width, slab_left.shape[2])
        return jnp.swapaxes(block.reshape(tiles), -1, -2)

    return placed(fresh_left), placed(fresh_right)


def fast_fits(rows_total, cols_total, tile_rows, piece_rows, width, column_tiles):
    return (
        column_tiles == 1
        and tile_rows * width == LANES
        and width % 8 == 0
        and piece_rows % LANES == 0
        and cols_total & (cols_total - 1) == 0
        and cols_total >= 4
        and rows_total & (rows_total - 1) == 0
        and cols_total % rows_total == 0
        and rows_total > 1
        and cols_total <= tile_rows * rows_total
    )


def shards(*args):
    tile_rows, piece_rows, width = args[3].shape
    rows_total, cols_total = lax.axis_size("row"), lax.axis_size("col")
    fits = fast_fits(rows_total, cols_total, tile_rows, piece_rows, width, args[0].shape[1])
    return fast_shards(*args) if fits else plain_shards(*args)


def solution(mesh):
    placed = (
        P("row", "col", None, None),
        P("row", "col", None, None),
        P("row", "col"),
        P("row", "col", None),
        P("row", "col", None),
        P("row"),
        P(None, "col"),
        P(),
    )
    return jax.shard_map(
        shards,
        mesh=mesh,
        in_specs=placed,
        out_specs=(P("row", "col", None, None), P("row", "col", None, None)),
        check_vma=False,
    )
```

```python
import functools
import math

import jax
import jax.numpy as jnp
from jax import lax
from jax.experimental import pallas as pl
from jax.experimental.pallas import tpu as pltpu
from jax.sharding import PartitionSpec as P


highest = lax.Precision.HIGHEST
stacked_precision = lax.Precision.HIGH
shift_rate = 0.01
tiny_shift = 1e-06
factor_scale = 0.5
LANES = 128
F32 = jnp.float32
BF16 = jnp.bfloat16
VMEM = pltpu.VMEM
PAIR_TYPE = BF16
CROSSED = 1


def spread(block, axis, owner):
    block = jnp.where(lax.axis_index(axis) == owner, block, jnp.zeros_like(block))
    return lax.psum(block, axis)


def product(first_matrix, second_matrix):
    return jnp.matmul(first_matrix, second_matrix, precision=highest)


def stacked_product(first_matrix, second_matrix):
    return jnp.matmul(first_matrix, second_matrix, precision=stacked_precision)


def flipped(matrix):
    return jnp.swapaxes(matrix, -1, -2)


def orthonormal(vectors):
    gram_matrix = product(flipped(vectors), vectors)
    shift_value = (
        shift_rate * jnp.trace(gram_matrix, axis1=-2, axis2=-1) / gram_matrix.shape[-1] + tiny_shift
    )
    identity = jnp.eye(gram_matrix.shape[-1], dtype=gram_matrix.dtype)
    lower_factor = jnp.linalg.cholesky(gram_matrix + shift_value[..., None, None] * identity)
    solved_rows = lax.linalg.triangular_solve(
        lower_factor, flipped(vectors), left_side=True, lower=True
    )
    return flipped(solved_rows)


def recompress(slab_factor, masked_right, row_factor, core_block, column_factor, sketch_float):
    target_shape = core_block.shape[:2] + slab_factor.shape[2:]
    column_wide = jnp.broadcast_to(column_factor[None], target_shape)
    row_core = product(row_factor, core_block)
    column_core = product(column_wide, flipped(core_block))
    forward_left = jnp.concatenate([slab_factor.astype(jnp.float32), -row_core], axis=-1)
    forward_right = jnp.concatenate([masked_right.astype(jnp.float32), column_wide], axis=-1)
    backward_left = jnp.concatenate([masked_right.astype(jnp.float32), -column_core], axis=-1)
    backward_right = jnp.concatenate([slab_factor.astype(jnp.float32), row_factor], axis=-1)

    def forward(vectors):
        return stacked_product(forward_left, stacked_product(flipped(forward_right), vectors))

    def backward(vectors):
        return stacked_product(backward_left, stacked_product(flipped(backward_right), vectors))

    basis_now = orthonormal(forward(sketch_float))
    basis_now = orthonormal(forward(backward(basis_now)))
    projected = backward(basis_now)
    factor_size = factor_scale * math.sqrt(slab_factor.shape[-2])
    return (basis_now * factor_size, projected / factor_size)


def plain_shards(
    slab_left, slab_right, slab_ranks, panel_left, panel_right, panel_ranks, inverse_factor, sketch
):
    rows_total = lax.axis_size("row")
    cols_total = lax.axis_size("col")
    my_row = lax.axis_index("row")
    my_col = lax.axis_index("col")
    tile_rows, piece_rows, rank_width = panel_left.shape
    column_tiles = slab_left.shape[1]
    tile_order = inverse_factor.shape[0]
    panel_keep = jnp.arange(rank_width, dtype=jnp.int32)[None, :] < panel_ranks[:, None]
    masked_panel = jnp.where(panel_keep[:, None, :], panel_right, jnp.zeros((), jnp.bfloat16))
    flat_right = jnp.swapaxes(masked_panel, 0, 1).reshape(piece_rows, tile_rows * rank_width)
    flat_left = jnp.swapaxes(panel_left, 0, 1).reshape(piece_rows, tile_rows * rank_width)
    solved_part = lax.psum_scatter(
        jnp.dot(inverse_factor, flat_right, preferred_element_type=jnp.float32),
        "col",
        scatter_dimension=0,
        tiled=True,
    ).astype(jnp.bfloat16)
    full_left, full_solved = (
        lax.all_gather(flat_left, "col", axis=0, tiled=True),
        lax.all_gather(solved_part, "col", axis=0, tiled=True),
    )
    full_left = full_left.reshape(tile_order, tile_rows, rank_width)
    full_solved = full_solved.reshape(tile_order, tile_rows, rank_width)
    first_pick = my_col // rows_total
    position = first_pick + 0
    picked_left = lax.dynamic_slice_in_dim(full_left, position, 1, 1)
    picked_solved = lax.dynamic_slice_in_dim(full_solved, position, 1, 1)
    send_left = picked_left.reshape(tile_order, column_tiles * rank_width)
    send_solved = picked_solved.reshape(tile_order, column_tiles * rank_width)
    root_row = my_col % rows_total
    column_left, column_solved = (
        spread(send_left, "row", root_row),
        spread(send_solved, "row", root_row),
    )
    row_factor = jnp.swapaxes(full_left, 0, 1)[:, None]
    row_solved = jnp.swapaxes(full_solved, 0, 1)
    column_factor = jnp.swapaxes(column_left.reshape(tile_order, column_tiles, rank_width), 0, 1)
    column_three = jnp.swapaxes(column_solved.reshape(tile_order, column_tiles, rank_width), 0, 1)
    core_block = jnp.einsum(
        "tbr,sbq->tsrq", row_solved, column_three, preferred_element_type=jnp.float32
    )
    slab_keep = jnp.arange(rank_width, dtype=jnp.int32) < slab_ranks[..., None]
    masked_right = jnp.where(slab_keep[:, :, None, :], slab_right, jnp.zeros((), jnp.bfloat16))
    fresh_left, fresh_right = recompress(
        slab_left, masked_right, row_factor, core_block, column_factor, sketch.astype(jnp.float32)
    )
    row_ids = jnp.arange(tile_rows, dtype=jnp.int32) * rows_total + my_row
    col_ids = jnp.arange(column_tiles, dtype=jnp.int32) * cols_total + my_col
    live_tile = (row_ids[:, None] > col_ids[None, :])[:, :, None, None]
    return (
        jnp.where(live_tile, fresh_left, 0.0).astype(jnp.bfloat16),
        jnp.where(live_tile, fresh_right, 0.0).astype(jnp.bfloat16),
    )


def partner(step):
    return 2 * step + CROSSED * min(step, 1)


def flip(row):
    return (row ^ (row >> 1)) & 1


def owned_block():
    return lax.axis_index("col") ^ flip(lax.axis_index("row"))


def nt(first, second):
    return lax.dot_general(first, second, (((1,), (1,)), ((), ())), preferred_element_type=F32)


def nn(first, second):
    return lax.dot_general(first, second, (((1,), (0,)), ((), ())), preferred_element_type=F32)


def split(value):
    high = value.astype(BF16)
    return high, (value - high.astype(F32)).astype(BF16)


def wide(value):
    return jnp.concatenate(split(value), axis=0)


def fold(value):
    half = value.shape[0] // 2
    return value[:half] + value[half:]


def dot_split(op, first, second_parts):
    stacked = wide(first)
    return fold(op(stacked, second_parts[0]) + op(stacked, second_parts[1]))


def grant(mebibytes):
    return pltpu.CompilerParams(vmem_limit_bytes=mebibytes << 20)


def line_mask(tile_lines, ranks):
    width = tile_lines // ranks.shape[0]
    keep = (jnp.arange(width, dtype=jnp.int32)[None, :] < ranks[:, None]).astype(F32).reshape(-1)
    return (
        jnp.broadcast_to(keep[:, None], (tile_lines, LANES)),
        jnp.broadcast_to(keep[None, :], (8, tile_lines)),
    )


def in_vmem(count):
    return [pl.BlockSpec(memory_space=VMEM)] * count


def small_cost(bytes_accessed, flops=0):
    return pl.CostEstimate(flops=flops, bytes_accessed=bytes_accessed, transcendentals=0)


def solve_step(block, my_col, right_ref, inverse, out_ref, step, copy=None, spare=None):
    @pl.when(block >= my_col)
    def _():
        if copy is not None:
            copy.wait()
        value = nt(right_ref[...], inverse[step])
        out_ref[step] = value.astype(out_ref.dtype)
        if spare is not None and step == 0:
            out_ref[spare] = (value - out_ref[step].astype(F32)).astype(out_ref.dtype)

    @pl.when(block < my_col)
    def _():
        out_ref[step] = jnp.zeros(out_ref.shape[1:], out_ref.dtype)
        if spare is not None and step == 0:
            out_ref[spare] = jnp.zeros(out_ref.shape[1:], out_ref.dtype)


def solve_odd_kernel(
    right_hbm, inverse_hbm, out_ref, right_ref, even_ref, inverse_ref, odd_sems, even_sems
):
    parts = inverse_ref.shape[0]
    piece = right_ref.shape[1]
    my_col, owned = lax.axis_index("col"), owned_block()
    right_copy = pltpu.make_async_copy(right_hbm, right_ref, odd_sems.at[parts])
    right_copy.start()
    copies = []
    for odd, target, sems in ((1, inverse_ref, odd_sems), (0, even_ref, even_sems)):
        for step in range(parts):
            block = owned ^ (partner(step) ^ odd)
            rows = pl.ds(pl.multiple_of(block * piece, piece), piece)
            copy = pltpu.make_async_copy(inverse_hbm.at[rows], target.at[step], sems.at[step])
            pl.when(block >= my_col)(copy.start)
            copies.append((block, copy))
    right_copy.wait()
    for step in range(parts):
        block, copy = copies[step]
        solve_step(block, my_col, right_ref, inverse_ref, out_ref, step, copy, parts)
    for block, copy in copies[parts:]:
        pl.when(block >= my_col)(copy.wait)


def solve_odd(right, inverse, parts):
    lines, piece = right.shape
    return pl.pallas_call(
        solve_odd_kernel,
        in_specs=[pl.BlockSpec(memory_space=pltpu.HBM)] * 2,
        out_specs=in_vmem(3),
        out_shape=[
            jax.ShapeDtypeStruct((parts + 1, lines, piece), PAIR_TYPE),
            jax.ShapeDtypeStruct((lines, piece), BF16),
            jax.ShapeDtypeStruct((parts, piece, piece), BF16),
        ],
        scratch_shapes=[
            VMEM((parts, piece, piece), BF16),
            pltpu.SemaphoreType.DMA((parts + 1,)),
            pltpu.SemaphoreType.DMA((parts,)),
        ],
        name="solve_odd",
        compiler_params=grant(4),
        cost_estimate=small_cost(
            4 * parts * piece * piece + 4 * parts * lines * piece,
            2 * parts * lines * piece * piece,
        ),
    )(right, inverse)


def solve_even_kernel(right_ref, even_ref, out_ref):
    my_col = lax.axis_index("col")
    for step in range(out_ref.shape[0]):
        solve_step(owned_block() ^ partner(step), my_col, right_ref, even_ref, out_ref, step)


def solve_even(right, even):
    lines, piece = right.shape
    parts = even.shape[0]
    return pl.pallas_call(
        solve_even_kernel,
        in_specs=in_vmem(2),
        out_specs=pl.BlockSpec(memory_space=VMEM),
        out_shape=jax.ShapeDtypeStruct((parts, lines, piece), F32),
        name="solve_even",
        compiler_params=grant(4),
        cost_estimate=small_cost(
            2 * parts * piece * piece + 4 * parts * lines * piece,
            2 * parts * lines * piece * piece,
        ),
    )(right, even)


def pair_add_kernel(mine_ref, other_ref, keep_ref, *send_refs):
    total = mine_ref[0] + other_ref[0].astype(F32)
    if other_ref.shape[0] > mine_ref.shape[0]:
        total = total + other_ref[mine_ref.shape[0]].astype(F32)
    keep_ref[...] = total
    for step, ref in enumerate(send_refs):
        ref[...] = (mine_ref[step + 1] + other_ref[step + 1].astype(F32)).astype(ref.dtype)


def pair_add(mine, other, send_type):
    parts, lines, piece = mine.shape
    return pl.pallas_call(
        pair_add_kernel,
        in_specs=in_vmem(2),
        out_specs=in_vmem(parts),
        out_shape=[jax.ShapeDtypeStruct((lines, piece), F32)]
        + [jax.ShapeDtypeStruct((lines, piece), send_type)] * (parts - 1),
        name="pair_add",
        compiler_params=grant(4),
        cost_estimate=small_cost(3 * mine.size * 4),
    )(mine, other)


def gather_add_kernel(head, first_ref, mask_ref, *refs):
    *others, solved_ref, head_ref = refs
    total = first_ref[...]
    for ref in others:
        total = total + ref[...].astype(F32)
    keep = jnp.concatenate([mask_ref[...]] * (total.shape[1] // LANES), axis=1)
    rounded = jnp.where(keep > 0.0, total, 0.0).astype(BF16)
    solved_ref[...] = rounded
    head_ref[...] = rounded[:head]


def gather_add(first, mask, others, head):
    return pl.pallas_call(
        functools.partial(gather_add_kernel, head),
        in_specs=in_vmem(2 + len(others)),
        out_specs=in_vmem(2),
        out_shape=[
            jax.ShapeDtypeStruct(first.shape, BF16),
            jax.ShapeDtypeStruct((head, first.shape[1]), BF16),
        ],
        name="gather_add",
        compiler_params=grant(4),
        cost_estimate=small_cost(first.size * 10),
    )(first, mask, *others)


def column_tiles(rows_total, cols_total, width, own_ref, others):
    my_row = lax.axis_index("row")
    for shift in range(rows_total):
        source = own_ref if shift == 0 else others[shift - 1]
        for index in range(cols_total // rows_total):
            lines = source[index * width : (index + 1) * width, :]
            yield index * rows_total + (my_row ^ shift), lines


def message_kernel(rows_total, cols_total, width, own_ref, *refs):
    others = refs[: rows_total - 1]
    *message_refs, stage = refs[rows_total - 1 :]
    my_col = lax.axis_index("col")
    lines = own_ref.shape[0]
    for tile, value in column_tiles(rows_total, cols_total, width, own_ref, others):
        stage[tile] = value
    for step, ref in enumerate(message_refs):
        target = my_col ^ partner(step)
        ref[:width] = stage[target]
        ref[width : width + lines] = own_ref[...]
        ref[width + lines :] = stage[target ^ 1]


def messages(own, others, rows_total, cols_total, width):
    lines, piece = own.shape
    half = cols_total // 2
    return pl.pallas_call(
        functools.partial(message_kernel, rows_total, cols_total, width),
        in_specs=in_vmem(rows_total),
        out_specs=in_vmem(half),
        out_shape=[jax.ShapeDtypeStruct((lines + 2 * width, piece), BF16)] * half,
        scratch_shapes=[VMEM((cols_total, width, piece), BF16)],
        name="messages",
        compiler_params=grant(4),
        cost_estimate=small_cost(half * (lines + 2 * width) * piece * 4),
    )(own, *others)


def bundle_kernel(width, *refs):
    *pieces, here_ref, there_ref = refs
    for step, ref in enumerate(pieces):
        here_ref[step] = ref[: here_ref.shape[1]]
        there_ref[step] = ref[width:]


def bundle(pieces, width):
    count = len(pieces)
    lines, piece = pieces[0].shape
    shape = jax.ShapeDtypeStruct((count, lines - width, piece), BF16)
    return pl.pallas_call(
        functools.partial(bundle_kernel, width),
        in_specs=in_vmem(count),
        out_specs=in_vmem(2),
        out_shape=[shape, shape],
        name="bundle",
        compiler_params=grant(4),
        cost_estimate=small_cost(count * pieces[0].size * 6),
    )(*pieces)


def core_kernel(rows_total, cols_total, width, own_ref, *refs):
    others = refs[: rows_total - 1]
    even_ref, odd_ref, stage = refs[rows_total - 1 :]
    my_col = lax.axis_index("col")
    half = cols_total // 2
    for tile, value in column_tiles(rows_total, cols_total, width, own_ref, others):
        relative = my_col ^ tile
        step = lax.shift_right_logical(relative, 1)
        given = (relative & 1) ^ (jnp.minimum(step, 1) * CROSSED)
        stage[given * half + step] = value
    piece = own_ref.shape[1]
    own = own_ref[...]
    odd_ref[...] = nt(stage[half:].reshape(half * width, piece), own).reshape(odd_ref.shape)
    even_ref[...] = nt(stage[:half].reshape(half * width, piece), own).reshape(even_ref.shape)


def core_parts(own, others, rows_total, cols_total, width):
    lines, piece = own.shape
    half = cols_total // 2
    shape = jax.ShapeDtypeStruct((half, width, lines), F32)
    return pl.pallas_call(
        functools.partial(core_kernel, rows_total, cols_total, width),
        in_specs=in_vmem(rows_total),
        out_specs=in_vmem(2),
        out_shape=[shape, shape],
        scratch_shapes=[VMEM((cols_total, width, piece), BF16)],
        name="core_parts",
        compiler_params=grant(4),
        cost_estimate=small_cost(400000, 2 * lines * piece * cols_total * width),
    )(own, *others)


def piece_spot(relative, piece):
    block = lax.axis_index("col") ^ relative
    return pl.ds(pl.multiple_of(block * piece, LANES), piece)


def same_tile(lines, width):
    lane = lax.broadcasted_iota(jnp.int32, (lines, lines), 1)
    line = lax.broadcasted_iota(jnp.int32, (lines, lines), 0)
    return (lane // width) == (line // width)


def panel_piece(even_ref, odd_ref, relative, width):
    step = relative // 2
    if relative != partner(step):
        lines = odd_ref.shape[1] - width
        return odd_ref[step, :lines], odd_ref[step, lines:]
    return even_ref[step, width:], even_ref[step, :width]


def partial_grams(given, left_ref, right_ref, sketch_ref, panel_ref, width):
    count, lines, piece = panel_ref.shape
    lines = lines - width
    relatives = [partner(step) ^ given for step in range(count)]
    if given:
        panel = jnp.concatenate([panel_ref[k, :lines] for k in range(count)], axis=1)
        column = jnp.concatenate([panel_ref[k, lines:] for k in range(count)], axis=1)
    else:
        panel = jnp.concatenate([panel_ref[k, width:] for k in range(count)], axis=1)
        column = jnp.concatenate([panel_ref[k, :width] for k in range(count)], axis=1)
    left, right, sketch = (
        jnp.concatenate([ref[:, piece_spot(k, piece)] for k in relatives], axis=1)
        for ref in (left_ref, right_ref, sketch_ref)
    )
    return (
        nt(left, panel),
        nt(panel, panel),
        nt(column, right),
        nt(column, column),
        nt(sketch, column),
    )


def early_gram_kernel(width, *refs):
    left_ref, right_ref, sketch_ref, even_ref, keep_line_ref, keep_lane_ref = refs[:6]
    left_high_ref, left_low_ref, right_gram_ref, sketch_right_ref, *sum_refs = refs[6:]
    sums = partial_grams(0, left_ref, right_ref, sketch_ref, even_ref, width)
    for ref, value in zip(sum_refs, sums):
        ref[...] = value
    same = same_tile(left_ref.shape[0], width)
    left, right = left_ref[...], right_ref[...]
    left_high_ref[...], left_low_ref[...] = split(jnp.where(same, nt(left, left), 0.0))
    keep_line = keep_line_ref[...] > 0.0
    keep_lane = keep_lane_ref[:1] > 0.0
    right_gram_ref[...] = jnp.where(same & keep_line & keep_lane, nt(right, right), 0.0)
    sketch_right_ref[...] = jnp.where(keep_lane, nt(sketch_ref[...], right), 0.0)


def early_grams(left, right, sketch, even, keep_line, keep_lane, width):
    lines, order = left.shape
    rounded = jax.ShapeDtypeStruct((lines, lines), BF16)
    square = jax.ShapeDtypeStruct((lines, lines), F32)
    flat = jax.ShapeDtypeStruct((width, lines), F32)
    small = jax.ShapeDtypeStruct((width, width), F32)
    outs = [rounded, rounded, square, flat, square, square, flat, small, small]
    return pl.pallas_call(
        functools.partial(early_gram_kernel, width),
        in_specs=in_vmem(6),
        out_specs=in_vmem(len(outs)),
        out_shape=outs,
        name="early_grams",
        compiler_params=grant(16),
        cost_estimate=small_cost(1000000, 2 * order * lines * lines * 5),
    )(left, right, sketch, even, keep_line, keep_lane)


def late_gram_kernel(width, *refs):
    left_ref, right_ref, sketch_ref, odd_ref, keep_lane_ref, *sum_refs = refs[:10]
    side_high_ref, side_low_ref, turned_high_ref, turned_low_ref, *out_refs = refs[10:]
    lines = left_ref.shape[0]
    same = same_tile(lines, width)
    sums = partial_grams(1, left_ref, right_ref, sketch_ref, odd_ref, width)
    cross, own, column_right, column_column, sketch_column = (
        ref[...] + value for ref, value in zip(sum_refs, sums)
    )
    cross = jnp.where(same, cross, 0.0)
    side_high_ref[:lines], side_low_ref[:lines] = split(cross)
    turned_high_ref[...], turned_low_ref[...] = split(cross.T)
    side_high_ref[lines:], side_low_ref[lines:] = split(jnp.where(same, own, 0.0))
    column_right = jnp.where(keep_lane_ref[:1] > 0.0, column_right, 0.0)
    for ref, value in zip(out_refs, (column_right, column_column, sketch_column)):
        ref[...] = value


def late_grams(left, right, sketch, odd, keep_lane, sums, width):
    lines, order = left.shape
    square = jax.ShapeDtypeStruct((lines, lines), BF16)
    tall = jax.ShapeDtypeStruct((2 * lines, lines), BF16)
    flat = jax.ShapeDtypeStruct((width, lines), F32)
    small = jax.ShapeDtypeStruct((width, width), F32)
    return pl.pallas_call(
        functools.partial(late_gram_kernel, width),
        in_specs=in_vmem(10),
        out_specs=in_vmem(7),
        out_shape=[tall, tall, square, square, flat, small, small],
        name="late_grams",
        compiler_params=grant(16),
        cost_estimate=small_cost(1000000, 2 * order * lines * lines * 2),
    )(left, right, sketch, odd, keep_lane, *sums)


def factor_and_apply(gram, shift, bands):
    width = gram.shape[0]
    count = width // 8
    chunk = count // 2
    lanes = lax.broadcasted_iota(jnp.int32, (8, LANES), 1)
    inner_lane = lax.rem(lanes, width)
    group = lanes - inner_lane
    sub = lax.broadcasted_iota(jnp.int32, (8, LANES), 0)
    inverse_shift = 1.0 / shift
    matrix = [
        gram[8 * b : 8 * b + 8] * inverse_shift + jnp.where(inner_lane == sub + 8 * b, 1.0, 0.0)
        for b in range(count)
    ]
    bands = [matrix] + [[band[8 * b : 8 * b + 8] for b in range(count)] for band in bands]

    def pick(vector, row):
        return vector[row : row + 1]

    for start in range(0, count, chunk):
        first_column = 8 * start
        columns = [
            {
                b: jnp.take_along_axis(matrix[b], group + first_column + k, axis=1)
                for b in range(start + k // 8, count)
            }
            for k in range(8 * chunk)
        ]
        last_half = start + chunk == count
        for k in range(0, 8 * chunk, 2):
            b, row = start + k // 8, k % 8
            one, two = columns[k], columns[k + 1]
            corner = pick(one[b], row)
            side = pick(one[b], row + 1)
            other = pick(two[b], row + 1)
            scale_one = lax.rsqrt(corner)
            scale_two = (corner * scale_one) * lax.rsqrt(corner * other - side * side)
            side = side * scale_one
            one = {c: one[c] * scale_one for c in one}
            two = {c: (two[c] - side * one[c]) * scale_two for c in two}
            for i in range(k + 2, 8 * chunk):
                c, place = start + i // 8, i % 8
                lead_one, lead_two = pick(one[c], place), pick(two[c], place)
                for d in columns[i]:
                    columns[i][d] = columns[i][d] - lead_one * one[d] - lead_two * two[d]
            below_one = dict(one)
            below_two = dict(two)
            below_one[b] = jnp.where(sub > row, one[b], 0.0)
            below_two[b] = jnp.where(sub > row + 1, two[b], 0.0)
            for number, band in enumerate(bands):
                if number == 0 and last_half:
                    continue
                done_one = pick(band[b], row) * scale_one
                done_two = (pick(band[b], row + 1) - side * done_one) * scale_two
                for c in range(b, count):
                    band[c] = band[c] - below_one[c] * done_one - below_two[c] * done_two
                if number > 0:
                    band[b] = jnp.where(
                        sub == row, done_one, jnp.where(sub == row + 1, done_two, band[b])
                    )
    scale = lax.rsqrt(shift)
    return [jnp.concatenate([part * scale for part in band], axis=0) for band in bands[1:]]


def finish_kernel(half, width, rows_total, *refs):
    core_refs = refs[:half]
    (
        left_high_ref,
        left_low_ref,
        right_gram_ref,
        sketch_right_ref,
        side_high_ref,
        side_low_ref,
        turned_high_ref,
        turned_low_ref,
        column_right_ref,
        column_column_ref,
        sketch_column_ref,
        left_ref,
        right_ref,
        even_ref,
        odd_ref,
        keep_lane_ref,
        out_left_hbm,
        out_right_hbm,
        out_left_ref,
        out_right_ref,
        sems,
    ) = refs[half:]
    my_row, my_col = lax.axis_index("row"), lax.axis_index("col")
    lines, order = left_ref.shape
    tiles = lines // width
    piece = odd_ref.shape[2]
    count = 2 * half
    same = same_tile(lines, width)

    def diagonal(value):
        return jnp.where(same, value, 0.0)

    def stacked(value):
        return diagonal(jnp.concatenate([value] * tiles, axis=0))

    def blocks(value):
        return jnp.concatenate([stacked(value[:, :lines]), stacked(value[:, lines:])], axis=1)

    keep_lane = keep_lane_ref[:1] > 0.0
    lane_row = lax.broadcasted_iota(jnp.int32, (1, lines), 1)
    live_line = jnp.zeros((1, lines), jnp.bool_)
    for tile in range(tiles):
        low = tile * width
        live = (tile * rows_total + my_row) > my_col
        live_line |= (lane_row >= low) & (lane_row < low + jnp.where(live, width, 0))

    row_parts = [
        jnp.concatenate(
            [jnp.concatenate([one[...], turned[...]], axis=0), side[...]],
            axis=1,
        )
        for one, turned, side in (
            (left_high_ref, turned_high_ref, side_high_ref),
            (left_low_ref, turned_low_ref, side_low_ref),
        )
    ]
    core = core_refs[0][...]
    for ref in core_refs[1:]:
        core = core + ref[...]
    core_split = split(core)
    core_blocks = stacked(core)
    core_block_split = split(core_blocks)

    first = jnp.concatenate([sketch_right_ref[...], -dot_split(nn, sketch_column_ref[...], core_split)], axis=1)
    ones = jnp.where(same, 1.0, 0.0).astype(BF16)

    def traced(one, two):
        both = jnp.sum(one * two, axis=0, keepdims=True)
        both = both[:, :lines] + both[:, lines:]
        high, low = split(jnp.broadcast_to(both, (8, lines)))
        return (nn(high, ones) + nn(low, ones)) * (shift_rate / width) + tiny_shift

    image = dot_split(nn, first, row_parts)
    shift = traced(first, image)
    gram = dot_split(nt, first, split(blocks(image)))
    core_lines = core.T
    cross = -diagonal(dot_split(nn, core_lines, split(column_right_ref[...])))
    inner = dot_split(nn, column_column_ref[...], core_split)
    corner = diagonal(dot_split(nn, core_lines, split(inner)))
    middle = jnp.concatenate(
        [
            jnp.concatenate([right_gram_ref[...], cross.T], axis=1),
            jnp.concatenate([cross, corner], axis=1),
        ],
        axis=0,
    )
    middle_parts = split(middle)
    beyond_parts = split(dot_split(nn, middle, row_parts))
    top, bottom = factor_and_apply(gram, shift, [image[:, :lines], image[:, lines:]])
    basis = jnp.concatenate([top, bottom], axis=1)

    second = dot_split(nn, basis, middle_parts)
    image = dot_split(nn, basis, beyond_parts)
    shift = traced(second, image)
    gram = dot_split(nt, second, split(blocks(image)))
    back = -dot_split(nt, image[:, lines:], core_block_split)
    left_top, left_bottom, right_top, right_bottom = factor_and_apply(
        gram, shift, [second[:, :lines], second[:, lines:], image[:, :lines], back]
    )
    factor_size = factor_scale * math.sqrt(order)
    live_scale = jnp.where(live_line, factor_size, 0.0)
    live_back = jnp.where(live_line, 1.0 / factor_size, 0.0)
    left_small = jnp.concatenate(
        [stacked(left_top * live_scale), stacked(left_bottom * live_scale)], axis=1
    ).astype(BF16)
    right_small = jnp.concatenate(
        [
            stacked(jnp.where(keep_lane, right_top * live_back, 0.0)),
            stacked(right_bottom * live_back),
        ],
        axis=1,
    ).astype(BF16)
    for relative in range(count):
        spot = piece_spot(relative, piece)
        panel, column = panel_piece(even_ref, odd_ref, relative, width)
        rows = jnp.concatenate([left_ref[:, spot], panel], axis=0)
        out_left_ref[relative] = nn(left_small, rows).astype(BF16)
        tall = jnp.concatenate([right_ref[:, spot]] + [column] * tiles, axis=0)
        out_right_ref[relative] = nn(right_small, tall).astype(BF16)
        for side, (ref, hbm) in enumerate(
            ((out_left_ref, out_left_hbm), (out_right_ref, out_right_hbm))
        ):
            pltpu.make_async_copy(ref.at[relative], hbm.at[:, spot], sems.at[side]).start()
    for side, hbm in enumerate((out_left_hbm, out_right_hbm)):
        pltpu.make_async_copy(hbm, hbm, sems.at[side]).wait()


def finish(cores, others, rows_total, width):
    half = len(cores)
    left = others[11]
    lines, piece = left.shape[0], left.shape[1] // (2 * half)
    shape = jax.ShapeDtypeStruct(left.shape, BF16)
    operands = (*cores, *others)
    return pl.pallas_call(
        functools.partial(finish_kernel, half, width, rows_total),
        in_specs=in_vmem(len(operands)),
        out_specs=[pl.BlockSpec(memory_space=pltpu.HBM)] * 2,
        out_shape=[shape, shape],
        scratch_shapes=[
            VMEM((2 * half, lines, piece), BF16),
            VMEM((2 * half, lines, piece), BF16),
            pltpu.SemaphoreType.DMA((2,)),
        ],
        name="finish",
        compiler_params=grant(16),
        cost_estimate=small_cost(5000000, 10**9),
    )(*operands)


def flat_lines(block):
    return jnp.swapaxes(block, -1, -2).reshape(-1, block.shape[-2])


def fast_shards(
    slab_left, slab_right, slab_ranks, panel_left, panel_right, panel_ranks, inverse_factor, sketch
):
    rows_total = lax.axis_size("row")
    cols_total = lax.axis_size("col")
    width = panel_left.shape[-1]
    half = cols_total // 2
    left, right = flat_lines(slab_left), flat_lines(slab_right)
    panel, solve_right = flat_lines(panel_left), flat_lines(panel_right)
    sketch_lines = flat_lines(sketch)
    head = width * (cols_total // rows_total)

    def swap(block, step):
        return lax.ppermute(block, "col", [(i, i ^ step) for i in range(cols_total)])

    def turn(block, shift, owners=False):
        pairs = []
        for row in range(rows_total):
            other = row ^ shift
            change = flip(row) ^ flip(other) if owners else 0
            for col in range(cols_total):
                pairs.append((row * cols_total + col, other * cols_total + (col ^ change)))
        return lax.ppermute(block, ("row", "col"), pairs)

    def across(blocks):
        return [swap(block, partner(step + 1)) for step, block in enumerate(blocks)]

    def along(block, owners=False):
        return [turn(block, shift, owners) for shift in range(1, rows_total)]

    panel_keep, _ = line_mask(panel.shape[0], panel_ranks)
    slab_line, slab_lane = line_mask(panel.shape[0], slab_ranks.reshape(-1))
    solve_right = pltpu.with_memory_space_constraint(solve_right, pltpu.HBM)
    inverse_factor = pltpu.with_memory_space_constraint(inverse_factor, pltpu.HBM)
    odd, right_panel, even_blocks = solve_odd(solve_right, inverse_factor, half)
    other = swap(odd, 1)
    even = solve_even(right_panel, even_blocks)
    kept, *sends = pair_add(even, other, BF16)
    received = across(sends)
    panel_others = along(panel[:head])
    solved, solved_head = gather_add(kept, panel_keep, received, head)
    solved_others = along(solved_head, True)
    own_message, *sends = messages(panel, panel_others, rows_total, cols_total, width)
    even_panel, odd_panel = bundle([own_message] + across(sends), width)
    odd_panel = swap(odd_panel, 1)
    early = early_grams(left, right, sketch_lines, even_panel, slab_line, slab_lane, width)
    slab_parts, sums = early[:4], early[4:]
    panel_parts = late_grams(left, right, sketch_lines, odd_panel, slab_lane, sums, width)
    core_even, core_odd = core_parts(solved, solved_others, rows_total, cols_total, width)
    kept, *sends = pair_add(core_even, swap(core_odd, 1), F32)
    fresh_left, fresh_right = finish(
        [kept] + across(sends),
        (*slab_parts, *panel_parts, left, right, even_panel, odd_panel, slab_lane),
        rows_total,
        width,
    )

    def placed(block):
        tiles = slab_left.shape[:2] + (width, slab_left.shape[2])
        return jnp.swapaxes(block.reshape(tiles), -1, -2)

    return placed(fresh_left), placed(fresh_right)


def fast_fits(rows_total, cols_total, tile_rows, piece_rows, width, column_tiles):
    return (
        column_tiles == 1
        and tile_rows * width == LANES
        and width % 8 == 0
        and piece_rows % LANES == 0
        and cols_total & (cols_total - 1) == 0
        and cols_total >= 4
        and rows_total & (rows_total - 1) == 0
        and cols_total % rows_total == 0
        and rows_total > 1
        and cols_total <= tile_rows * rows_total
    )


def shards(*args):
    tile_rows, piece_rows, width = args[3].shape
    rows_total, cols_total = lax.axis_size("row"), lax.axis_size("col")
    fits = fast_fits(rows_total, cols_total, tile_rows, piece_rows, width, args[0].shape[1])
    return fast_shards(*args) if fits else plain_shards(*args)


def solution(mesh):
    placed = (
        P("row", "col", None, None),
        P("row", "col", None, None),
        P("row", "col"),
        P("row", "col", None),
        P("row", "col", None),
        P("row"),
        P(None, "col"),
        P(),
    )
    return jax.shard_map(
        shards,
        mesh=mesh,
        in_specs=placed,
        out_specs=(P("row", "col", None, None), P("row", "col", None, None)),
        check_vma=False,
    )
```
